32 devices in a mesh: grp: 2 (over y), tile: 4 (over z), sub: 4 (over x, core).
Axes of the slice: x: 2, y: 2, z: 4, core: 2. Of those that a mesh axis runs over, the one named last changes fastest.
Arguments:
- features: bfloat16 [24, 32, 1024], P(('grp', 'tile'), 'sub'), parts along dimension 0, may hold values from -6 to 6
- out_grad: bfloat16 [24, 32, 1024], P(('grp', 'tile'), 'sub'), parts along dimension 0, may hold values from -6 to 6
- filters: bfloat16 [5, 32, 32], replicated, may hold values from -0.5 to 0.5
- tile_map: int32 [12], replicated, may hold values from 0 to 11, as said below
Outputs:
- in_grad: bfloat16 [24, 32, 1024], P(('grp', 'tile'), 'sub'), parts along dimension 0
- weight_grad: float32 [10, 32, 32], P('grp', 'sub'), parts along dimension 0
The draws below stay inside these ranges and needn't reach their ends.
There are 2 independent parts, one for each index of `grp`. The reference program is written for one: setup_inputs(seed, part) draws one part's arguments, and reference() takes and returns one part's arrays. A program takes and returns all parts, laid end to end along the dimension named above; an argument that names none is the same for every part. Nothing has to cross between parts.
Inputs may be any that keep to these rules, and one draw needn't show every extreme that they name: tile_map[s] is the nested index of the tile held in slot s; slots 3 * j to 3 * j + 2 lie on index j of tile and hold the nested indices 3 * j to 3 * j + 2 in some order.
All inputs are finite; a program needn't handle non-finite values.
Results may differ from the reference program's by a relative error of at most 0.00045.
Values may be sent and summed in bfloat16 or wider, within the bound.
A program may use at most 64 MiB of HBM per device.

```python
import math
import jax
import jax.numpy as jnp
from jax import lax

C = 32
K = 5
TPD = 3
TS = 32
Q = 1
TILES = 12
PIXELS = 12288


def draw_tile_map(key, part):
    blocks = jnp.arange(TILES, dtype=jnp.int32).reshape(TILES // TPD, TPD)
    shuffled = jax.random.permutation(key, blocks, axis=1, independent=True)
    return shuffled.reshape(TILES).astype(jnp.int32)


def shard_levels(stream_key, shape, pieces, smallest, largest):
    def one(dim, blocks):
        draws = jax.random.uniform(jax.random.fold_in(jax.random.fold_in(stream_key, 6), dim), (blocks,), jnp.float32, smallest / len(pieces), largest / len(pieces))
        return jnp.repeat(jnp.exp(draws), shape[dim] // blocks).reshape((-1,) + (1,) * (len(shape) - dim - 1))

    factor_of = one(*pieces[0])
    for cut in pieces[1:]:
        factor_of = factor_of * one(*cut)
    return factor_of


def noise(own_key, shape, spread, limit, cuts=(), kind=jnp.bfloat16):
    result = jax.random.normal(own_key, shape, jnp.float32) * spread
    if len(cuts) > 0:
        result = shard_levels(own_key, shape, cuts, -0.22, 0.18) * result
    return jnp.clip(result, min=-limit, max=limit).astype(kind)


def setup_inputs(seed: int = 0, part: int = 0) -> dict:
    streams_of = jax.random.split(jax.random.key(seed), 5)
    own_keys = jax.random.split(jax.random.fold_in(streams_of[4], part), 5)
    features = noise(own_keys[0], (TILES, C, TS * TS), 1.0, 6.0, ((0, 4), (1, 4)))
    out_grad = noise(own_keys[1], (TILES, C, TS * TS), 1.0, 6.0, ((0, 4), (1, 4)))
    filters = noise(streams_of[2], (K, C, C), (K * C) ** -0.5, 0.5)
    tile_map = draw_tile_map(jax.random.fold_in(streams_of[4], 71), part)
    return dict(features=features, out_grad=out_grad, filters=filters, tile_map=tile_map)


def tile_coords(nested_code, bit_count):
    coord_x = nested_code * 0
    coord_y = nested_code * 0
    for bit_level in range(bit_count):
        coord_x = coord_x + nested_code // 4 ** bit_level % 2 * 2 ** bit_level
        coord_y = coord_y + nested_code // (2 * 4 ** bit_level) % 2 * 2 ** bit_level
    return (coord_x, coord_y)

def nested_index(coord_x, coord_y, bit_count):
    nested_code = coord_x * 0
    for bit_level in range(bit_count):
        nested_code = nested_code + coord_x // 2 ** bit_level % 2 * 4 ** bit_level
        nested_code = nested_code + coord_y // 2 ** bit_level % 2 * (2 * 4 ** bit_level)
    return nested_code

def pick(condition, when_true, when_false):
    return when_false + (when_true - when_false) * condition

def neighbour_codes(tile_ids, per_face, side_count):
    bit_count = side_count.bit_length() - 1
    face_id = tile_ids // per_face
    coord_x, coord_y = tile_coords(tile_ids % per_face, bit_count)
    column = face_id % 4
    is_north = face_id < 4
    is_south = face_id >= 8
    last_tile = side_count - 1

    def by_cycle(north_value, equator_value, south_value):
        return pick(is_north, north_value, pick(is_south, south_value, equator_value))
    side_rules = [(coord_x > 0, (face_id, coord_x - 1, coord_y, 1), (by_cycle(4 + column, 8 + (column + 3) % 4, 8 + (column + 3) % 4), by_cycle(last_tile, last_tile, coord_y), by_cycle(coord_y, coord_y, 0), by_cycle(1, 1, 2))), (coord_x < last_tile, (face_id, coord_x + 1, coord_y, 0), (by_cycle((column + 1) % 4, column, 4 + (column + 1) % 4), by_cycle(coord_y, 0, 0), by_cycle(last_tile, coord_y, coord_y), by_cycle(3, 0, 0))), (coord_y > 0, (face_id, coord_x, coord_y - 1, 3), (by_cycle(4 + (column + 1) % 4, 8 + column, 8 + (column + 1) % 4), by_cycle(coord_x, coord_x, 0), by_cycle(last_tile, last_tile, coord_x), by_cycle(3, 3, 0))), (coord_y < last_tile, (face_id, coord_x, coord_y + 1, 2), (by_cycle((column + 3) % 4, (column + 3) % 4, 4 + column), by_cycle(last_tile, coord_x, coord_x), by_cycle(coord_x, 0, 0), by_cycle(1, 2, 2)))]
    target_list = []
    edge_list = []
    for inside, within, across in side_rules:
        chosen = [pick(inside, near_value, far_value) for near_value, far_value in zip(within, across)]
        target_list.append(chosen[0] * per_face + nested_index(chosen[1], chosen[2], bit_count))
        edge_list.append(chosen[3] + tile_ids * 0)
    return (target_list, edge_list)

def neighbour_table(tile_map, per_face, side_count):
    target_list, edge_list = neighbour_codes(tile_map, per_face, side_count)
    targets = jnp.stack(target_list, axis=1).astype(jnp.int32)
    edges = jnp.stack(edge_list, axis=1).astype(jnp.int32)
    slot_of = jnp.argsort(tile_map).astype(jnp.int32)
    return (slot_of[targets].astype(jnp.int32), edges)

def edge_lines(values, tile_side):
    return jnp.stack([values[..., :tile_side], values[..., -tile_side:], values[..., ::tile_side], values[..., tile_side - 1::tile_side]], axis=1)

def stencil(values, ghosts, tile_side):
    position = jnp.arange(values.shape[-1]) % tile_side
    zero_line = jnp.zeros_like(values[..., :1])
    upper_side = jnp.concatenate([ghosts[:, 0], values[..., :-tile_side]], axis=-1)
    lower_side = jnp.concatenate([values[..., tile_side:], ghosts[:, 1]], axis=-1)
    left_side = jnp.where(position == 0, jnp.repeat(ghosts[:, 2], tile_side, axis=-1), jnp.concatenate([zero_line, values[..., :-1]], axis=-1))
    right_side = jnp.where(position == tile_side - 1, jnp.repeat(ghosts[:, 3], tile_side, axis=-1), jnp.concatenate([values[..., 1:], zero_line], axis=-1))
    return -0.25 * (upper_side + lower_side + left_side + right_side)

def reference(features, out_grad, filters, tile_map):
    slot_table, edge_table = neighbour_table(tile_map, TILES // 12, Q)
    highest = lax.Precision.HIGHEST

    def laplace(values):
        return stencil(values, edge_lines(values, TS)[slot_table, edge_table], TS)
    inputs = features.astype(jnp.float32)
    cotangent = out_grad.astype(jnp.float32)
    weights = filters.astype(jnp.float32)
    previous, current = (inputs, laplace(inputs))
    filter_terms = [jnp.einsum('sip,sop->io', inputs, cotangent, precision=highest), jnp.einsum('sip,sop->io', current, cotangent, precision=highest)]
    for degree in range(2, K):
        previous, current = (current, 2.0 * laplace(current) - previous)
        filter_terms.append(jnp.einsum('sip,sop->io', current, cotangent, precision=highest))
    weight_grad = jnp.stack(filter_terms) / math.sqrt(PIXELS)

    def mixed(degree):
        return jnp.einsum('sop,io->sip', cotangent, weights[degree], precision=highest)
    next_sum = mixed(K - 1)
    after_next = jnp.zeros_like(next_sum)
    for degree in range(K - 2, 0, -1):
        next_sum, after_next = (mixed(degree) + 2.0 * laplace(next_sum) - after_next, next_sum)
    in_grad = (mixed(0) + laplace(next_sum) - after_next).astype(jnp.bfloat16)
    return (in_grad, weight_grad)
```

```python
import functools
import math

import jax
import jax.numpy as jnp
import numpy as np
from jax import lax
from jax.experimental import pallas as pl
from jax.experimental.pallas import tpu as pltpu
from jax.sharding import PartitionSpec as P

K = 5


def from_behind(value, axis, steps):
    count = lax.axis_size(axis)
    pairs = [(source, (source + steps) % count) for source in range(count)]
    return lax.ppermute(value, axis, pairs)


def tile_coords(nested_code, bit_count):
    coord_x = nested_code * 0
    coord_y = nested_code * 0
    for bit_level in range(bit_count):
        coord_x = coord_x + nested_code // 4**bit_level % 2 * 2**bit_level
        coord_y = coord_y + nested_code // (2 * 4**bit_level) % 2 * 2**bit_level
    return (coord_x, coord_y)


def nested_index(coord_x, coord_y, bit_count):
    nested_code = coord_x * 0
    for bit_level in range(bit_count):
        nested_code = nested_code + coord_x // 2**bit_level % 2 * 4**bit_level
        nested_code = nested_code + coord_y // 2**bit_level % 2 * (2 * 4**bit_level)
    return nested_code


def pick(condition, when_true, when_false):
    return when_false + (when_true - when_false) * condition


def neighbour_codes(tile_ids, per_face, side_count):
    bit_count = side_count.bit_length() - 1
    face_id = tile_ids // per_face
    coord_x, coord_y = tile_coords(tile_ids % per_face, bit_count)
    column = face_id % 4
    is_north = face_id < 4
    is_south = face_id >= 8
    last_tile = side_count - 1

    def by_cycle(north_value, equator_value, south_value):
        return pick(is_north, north_value, pick(is_south, south_value, equator_value))

    side_rules = [
        (
            coord_x > 0,
            (face_id, coord_x - 1, coord_y, 1),
            (
                by_cycle(4 + column, 8 + (column + 3) % 4, 8 + (column + 3) % 4),
                by_cycle(last_tile, last_tile, coord_y),
                by_cycle(coord_y, coord_y, 0),
                by_cycle(1, 1, 2),
            ),
        ),
        (
            coord_x < last_tile,
            (face_id, coord_x + 1, coord_y, 0),
            (
                by_cycle((column + 1) % 4, column, 4 + (column + 1) % 4),
                by_cycle(coord_y, 0, 0),
                by_cycle(last_tile, coord_y, coord_y),
                by_cycle(3, 0, 0),
            ),
        ),
        (
            coord_y > 0,
            (face_id, coord_x, coord_y - 1, 3),
            (
                by_cycle(4 + (column + 1) % 4, 8 + column, 8 + (column + 1) % 4),
                by_cycle(coord_x, coord_x, 0),
                by_cycle(last_tile, last_tile, coord_x),
                by_cycle(3, 3, 0),
            ),
        ),
        (
            coord_y < last_tile,
            (face_id, coord_x, coord_y + 1, 2),
            (
                by_cycle((column + 3) % 4, (column + 3) % 4, 4 + column),
                by_cycle(last_tile, coord_x, coord_x),
                by_cycle(coord_x, 0, 0),
                by_cycle(1, 2, 2),
            ),
        ),
    ]
    target_list = []
    edge_list = []
    for inside, within, across in side_rules:
        chosen = [
            pick(inside, near_value, far_value) for near_value, far_value in zip(within, across)
        ]
        target_list.append(chosen[0] * per_face + nested_index(chosen[1], chosen[2], bit_count))
        edge_list.append(chosen[3] + tile_ids * 0)
    return (target_list, edge_list)


def neighbour_table(tile_map, per_face, side_count):
    target_list, edge_list = neighbour_codes(tile_map, per_face, side_count)
    targets = jnp.stack(target_list, axis=1).astype(jnp.int32)
    edges = jnp.stack(edge_list, axis=1).astype(jnp.int32)
    slot_of = jnp.argsort(tile_map).astype(jnp.int32)
    return (slot_of[targets].astype(jnp.int32), edges)


def peer_offsets(slot_count, device_count, per_face, side_count):
    tile_ids = np.arange(slot_count * device_count, dtype=np.int64)
    target_list, edge_list = neighbour_codes(tile_ids, per_face, side_count)
    targets = np.stack(target_list, axis=1)
    offsets = (tile_ids[:, None] // slot_count - targets // slot_count) % device_count
    distinct = sorted(set((int(value) for value in offsets.ravel())) - {0})
    position = np.zeros(device_count, dtype=np.int32)
    for order, value in enumerate(distinct):
        position[value] = order + 1
    return (distinct, position)


def edge_lines(values, tile_side):
    return jnp.stack(
        [
            values[..., :tile_side],
            values[..., -tile_side:],
            values[..., ::tile_side],
            values[..., tile_side - 1 :: tile_side],
        ],
        axis=1,
    )


def stencil(values, ghosts, tile_side):
    position = jnp.arange(values.shape[-1]) % tile_side
    zero_line = jnp.zeros_like(values[..., :1])
    upper_side = jnp.concatenate([ghosts[:, 0], values[..., :-tile_side]], axis=-1)
    lower_side = jnp.concatenate([values[..., tile_side:], ghosts[:, 1]], axis=-1)
    left_side = jnp.where(
        position == 0,
        jnp.repeat(ghosts[:, 2], tile_side, axis=-1),
        jnp.concatenate([zero_line, values[..., :-1]], axis=-1),
    )
    right_side = jnp.where(
        position == tile_side - 1,
        jnp.repeat(ghosts[:, 3], tile_side, axis=-1),
        jnp.concatenate([values[..., 1:], zero_line], axis=-1),
    )
    return -0.25 * (upper_side + lower_side + left_side + right_side)


def tile_total(filter_part):
    return lax.psum(filter_part, "tile")


def general_path(features, out_grad, filters, tile_map):
    slot_count = features.shape[0]
    group_channels = features.shape[1]
    tile_side = math.isqrt(features.shape[2])
    device_count = lax.axis_size("tile")
    total_tiles = slot_count * device_count
    side_count = math.isqrt(total_tiles // 12)
    scale_factor = 1.0 / math.sqrt(total_tiles * features.shape[2])
    highest = lax.Precision.HIGHEST
    slot_table, edge_table = neighbour_table(tile_map, total_tiles // 12, side_count)
    my_device = lax.axis_index("tile")
    first_slot = my_device * slot_count
    my_slots = lax.dynamic_slice_in_dim(slot_table, first_slot, slot_count, 0)
    my_edges = lax.dynamic_slice_in_dim(edge_table, first_slot, slot_count, 0)
    channel_start = lax.axis_index("sub") * group_channels
    weights = filters.astype(jnp.float32)
    distinct, position = peer_offsets(slot_count, device_count, total_tiles // 12, side_count)
    sender_gap = (my_device - my_slots // slot_count) % device_count
    local_rows = jnp.asarray(position)[sender_gap] * slot_count + my_slots % slot_count

    def laplace(values):
        border = edge_lines(values, tile_side).reshape(slot_count, 4, group_channels * tile_side)
        received = [border]
        for offset_value in distinct:
            received.append(from_behind(border, "tile", offset_value))
        stacked = jnp.concatenate(received, axis=0)
        stacked = stacked.reshape(stacked.shape[0], 4, group_channels, tile_side)
        rows = []
        for slot in range(slot_count):
            for side in range(4):
                start = (local_rows[slot, side], my_edges[slot, side], 0, 0)
                rows.append(
                    lax.dynamic_slice(stacked, start, (1, 1, group_channels, tile_side))
                )
        ghosts = jnp.concatenate(rows, axis=0)
        ghosts = ghosts.reshape(slot_count, 4, group_channels, tile_side)
        return stencil(values, ghosts, tile_side)

    whole_grad = lax.all_gather(out_grad, "sub", axis=1, tiled=True)
    cotangent = whole_grad.astype(jnp.float32)
    inputs = features.astype(jnp.float32)
    previous, current = (inputs, laplace(inputs))
    filter_terms = [
        jnp.einsum("sip,sop->io", inputs, cotangent, precision=highest),
        jnp.einsum("sip,sop->io", current, cotangent, precision=highest),
    ]
    for degree in range(2, K):
        previous, current = (current, 2.0 * laplace(current) - previous)
        filter_terms.append(jnp.einsum("sip,sop->io", current, cotangent, precision=highest))
    weight_grad = tile_total(jnp.stack(filter_terms)) * scale_factor
    row_block = lax.dynamic_slice_in_dim(weights, channel_start, group_channels, 1)

    def mixed(degree):
        return jnp.einsum("sop,io->sip", cotangent, row_block[degree], precision=highest)

    next_sum = mixed(K - 1)
    after_next = jnp.zeros_like(next_sum)
    for degree in range(K - 2, 0, -1):
        next_sum, after_next = (mixed(degree) + 2.0 * laplace(next_sum) - after_next, next_sum)
    in_grad = (mixed(0) + laplace(next_sum) - after_next).astype(jnp.bfloat16)
    return (in_grad, weight_grad)


DEPTH = K - 1
GHOST_SIDES = (0, 2, 3, 1)
OUTSIDE = 6


def face_graph(tile_side):
    tile_ids = np.arange(12, dtype=np.int64)
    target_list, edge_list = neighbour_codes(tile_ids, 1, 1)
    targets = np.stack(target_list, axis=1)
    edges = np.stack(edge_list, axis=1)
    pixels = tile_side * tile_side
    grid = np.arange(pixels).reshape(tile_side, tile_side)
    lines = [grid[0], grid[-1], grid[:, 0], grid[:, -1]]
    ghosts = np.zeros((12, 4, tile_side), dtype=np.int64)
    around = np.zeros((12, 4, tile_side, tile_side), dtype=np.int64)
    for tile in range(12):
        for side in range(4):
            ghosts[tile, side] = targets[tile, side] * pixels + lines[edges[tile, side]]
        whole = tile * pixels + grid
        around[tile, 0] = np.concatenate([ghosts[tile, 0][None], whole[:-1]], 0)
        around[tile, 1] = np.concatenate([whole[1:], ghosts[tile, 1][None]], 0)
        around[tile, 2] = np.concatenate([ghosts[tile, 2][:, None], whole[:, :-1]], 1)
        around[tile, 3] = np.concatenate([whole[:, 1:], ghosts[tile, 3][:, None]], 1)
    around = around.transpose(0, 2, 3, 1).reshape(12 * pixels, 4)
    return targets, edges, ghosts, around


@functools.lru_cache(None)
def ghost_tables(tile_side, slots, tiles_n):
    targets, edges, ghosts, around = face_graph(tile_side)
    pixels = tile_side * tile_side
    grid = np.arange(pixels).reshape(tile_side, tile_side)
    strips = np.stack(
        [
            grid[:DEPTH].ravel(),
            grid[-DEPTH:].ravel(),
            grid[:, :DEPTH].T.ravel(),
            grid[:, -DEPTH:].T.ravel(),
        ]
    )
    sources_of = []
    by_class = []
    for tile in range(12):
        wanted = np.concatenate([ghosts[tile, side] for side in GHOST_SIDES])
        power = np.zeros((wanted.size, 12 * pixels), dtype=np.int32)
        power[np.arange(wanted.size), wanted] = 1
        powers = [power]
        for _ in range(DEPTH - 1):
            powers.append(sum(powers[-1][:, around[:, side]] for side in range(4)))
        rows = np.concatenate(
            [powers[0], powers[1], powers[2] - 8 * powers[0], powers[3] - 12 * powers[1]]
        )
        support = np.flatnonzero(np.any(rows != 0, axis=0))
        sources = [(int(targets[tile, side]), int(edges[tile, side])) for side in range(4)]
        own = [(tile, side) for side in range(4)]
        covered = set(int(t) * pixels + int(p) for t, e in sources + own for p in strips[e])
        left = [int(p) for p in support if int(p) not in covered]
        corner_tiles = {}
        for pixel in left:
            corner_tiles.setdefault(pixel // pixels, []).append(pixel % pixels)
        first = lambda t: int(
            np.flatnonzero(np.any(rows[:, [t * pixels + p for p in corner_tiles[t]]] != 0, axis=1))[0]
        )
        for other in sorted(corner_tiles, key=first):
            choice = [e for e in range(4) if set(corner_tiles[other]) <= set(strips[e].tolist())]
            sources.append((other, choice[0]))
        assert len(sources) <= OUTSIDE
        while len(sources) < OUTSIDE:
            sources.append(sources[-1])
        sources_of.append(sources)
        lanes = np.concatenate([t * pixels + strips[e] for t, e in sources + own])
        seen, keep = set(), np.zeros(lanes.size, dtype=bool)
        for lane, pixel in enumerate(lanes.tolist()):
            keep[lane] = pixel not in seen
            seen.add(pixel)
        assert set(support.tolist()) <= seen
        matrix = (rows[:, lanes] * keep[None]).T
        assert np.abs(matrix).max() <= 127
        if tile % 4 == 0:
            by_class.append(matrix)
        else:
            assert np.array_equal(matrix, by_class[-1])
    wanted = {}
    for tile in range(12):
        for t, e in sources_of[tile]:
            pair = (t // slots, tile // slots)
            if pair[0] != pair[1]:
                held = wanted.setdefault(pair, [])
                if (t, e) not in held:
                    held.append((t, e))
    packed = max(len(held) for held in wanted.values())
    send = np.zeros((tiles_n, tiles_n, packed), dtype=np.int32)
    for (q, p), held in wanted.items():
        for order, (t, e) in enumerate(held):
            send[q, p, order] = (t - q * slots) * 4 + e
    take_from = np.zeros((12, OUTSIDE), dtype=np.int32)
    for tile in range(12):
        for order, (t, e) in enumerate(sources_of[tile]):
            q, p = t // slots, tile // slots
            if q == p:
                take_from[tile, order] = (t - q * slots) * 4 + e
            else:
                at = wanted[(q, p)].index((t, e))
                take_from[tile, order] = slots * 4 + q * packed + at
    table = np.concatenate([take_from.ravel(), send.ravel()])
    spread = np.zeros((4, tile_side, tile_side, tile_side))
    step = np.arange(tile_side)
    spread[0, step, 0, step] = 1
    spread[1, step, step, 0] = 1
    spread[2, step, step, -1] = 1
    spread[3, step, -1, step] = 1
    local = np.zeros((pixels, pixels))
    for u in range(tile_side):
        for v in range(tile_side):
            for du, dv in ((1, 0), (-1, 0), (0, 1), (0, -1)):
                if 0 <= u + du < tile_side and 0 <= v + dv < tile_side:
                    local[grid[u, v], grid[u + du, v + dv]] = -0.25
    inward = [-0.25 * spread.reshape(4 * tile_side, pixels)]
    inward.append(2.0 * inward[0] @ local)
    for _ in range(DEPTH - 2):
        inward.append(2.0 * inward[-1] @ local - inward[-2])
    inward = np.concatenate(inward)
    assert np.array_equal(inward, inward.astype(jnp.bfloat16).astype(np.float64))
    take = np.zeros((pixels, 2 * DEPTH * tile_side), dtype=np.float32)
    take[np.concatenate([strips[2], strips[3]]), np.arange(2 * DEPTH * tile_side)] = 1
    return np.stack(by_class), table, packed, inward, take


def split(value):
    high = value.astype(jnp.bfloat16).astype(jnp.float32)
    return high, value - high


def product(left, right):
    return lax.dot_general(
        left, right, (((1,), (1,)), ((), ())), preferred_element_type=jnp.float32
    )


def face_kernel(
    sizes,
    x_hbm,
    g_hbm,
    f_hbm,
    map_hbm,
    table_hbm,
    ghost_hbm,
    inward_hbm,
    take_hbm,
    in_ref,
    w_ref,
    x_ref,
    g_ref,
    g_all,
    x_mine,
    g_mine,
    x_pack,
    g_pack,
    x_ext,
    g_ext,
    block,
    block_in,
    result,
    ghost,
    inward,
    take,
    f_ref,
    map_ref,
    table_ref,
    load_sem,
    x_send,
    x_recv,
    s_send,
    s_recv,
    g_send,
    g_recv,
    f_send,
    f_recv,
    w_send,
    w_recv,
):
    slots, tiles_n, subs, side, packed, scale = sizes
    chans = x_ref.shape[1]
    total = subs * chans
    pixels = side * side
    width = DEPTH * side
    rows = slots * chans
    bf16, f32 = jnp.bfloat16, jnp.float32
    j = lax.axis_index("tile")
    s = lax.axis_index("sub")
    tile_peers = []
    for d in range(tiles_n - 1):
        up = d + (j <= d).astype(jnp.int32)
        back = tiles_n - 2 - d
        down = back + (j <= back).astype(jnp.int32)
        tile_peers.append(jnp.where(2 * j < tiles_n, down, up))
    sub_peers = [lax.rem(s + d, subs) for d in range(1, subs)]
    friends = [{"tile": peer} for peer in tile_peers] + [{"sub": peer} for peer in sub_peers]
    kinds = [(slots * j + m) // 4 for m in range(slots)]

    first_loads = [
        pltpu.make_async_copy(map_hbm, map_ref, load_sem.at[0]),
        pltpu.make_async_copy(table_hbm, table_ref, load_sem.at[1]),
        pltpu.make_async_copy(x_hbm, x_ref, load_sem.at[2]),
        pltpu.make_async_copy(g_hbm, g_ref, load_sem.at[3]),
        pltpu.make_async_copy(take_hbm, take, load_sem.at[4]),
    ]
    for copy in first_loads:
        copy.start()
    barrier = pltpu.get_barrier_semaphore()
    for friend in friends:
        pl.semaphore_signal(
            barrier, inc=1, device_id=friend, device_id_type=pl.DeviceIdType.MESH
        )
    loads = [
        pltpu.make_async_copy(ghost_hbm.at[kinds[0]], ghost.at[0], load_sem.at[5]),
        pltpu.make_async_copy(ghost_hbm.at[kinds[-1]], ghost.at[1], load_sem.at[6]),
        pltpu.make_async_copy(inward_hbm, inward, load_sem.at[7]),
        pltpu.make_async_copy(f_hbm, f_ref, load_sem.at[8]),
        pltpu.make_async_copy(g_hbm, g_all.at[s], load_sem.at[9]),
    ]
    for copy in loads:
        copy.start()

    base = slots * j
    for copy in first_loads:
        copy.wait()

    def slot_of(m):
        found = 0
        for slot in range(1, slots):
            found = jnp.where(map_ref[base + slot] == base + m, slot, found)
        return found

    slot_list = [slot_of(m) for m in range(slots)]
    x_own = jnp.concatenate([x_ref[slot_list[m]].astype(f32) for m in range(slots)], axis=0)
    g_own = jnp.concatenate([g_ref[slot_list[m]].astype(f32) for m in range(slots)], axis=0)
    both = jnp.concatenate([x_own, g_own], axis=0).astype(bf16)
    cut = jnp.dot(both, take[...], preferred_element_type=f32)

    def strips_of(value, cut_value):
        return [
            value[:, :width],
            value[:, pixels - width :],
            cut_value[:, :width],
            cut_value[:, width:],
        ]

    x_strips = strips_of(x_own, cut[:rows])
    g_strips = strips_of(g_own, cut[rows:])
    for m in range(slots):
        at = slice(m * chans, (m + 1) * chans)
        for e in range(4):
            x_mine[m * 4 + e] = x_strips[e][at].astype(bf16)
            g_mine[m * 4 + e] = g_strips[e][at].astype(bf16)
    sends = 12 * OUTSIDE
    for d, peer in enumerate(tile_peers):
        for i in range(packed):
            index = table_ref[sends + (j * tiles_n + peer) * packed + i]
            x_pack[d, i] = x_mine[index]
            g_pack[d, i] = g_mine[index]
    for m in range(slots):
        at = slice(m * chans, (m + 1) * chans)
        for e in range(4):
            x_ext[m * 4 + e] = x_strips[e][at].astype(bf16)

    def landing(sender):
        return pl.ds(slots * 4 + sender * packed, packed)

    def remote(source, target, send, recv, device):
        return pltpu.make_async_remote_copy(
            source,
            target,
            send,
            recv,
            device_id=device,
            device_id_type=pl.DeviceIdType.MESH,
        )

    def x_copy(d, sender, peer):
        return remote(
            x_pack.at[d], x_ext.at[landing(sender)], x_send.at[d], x_recv.at[sender], {"tile": peer}
        )

    def strip_copy(d, sender, peer):
        return remote(
            g_pack.at[d],
            g_ext.at[s, landing(sender)],
            s_send.at[d],
            s_recv.at[sender],
            {"tile": peer},
        )

    def g_copy(d, sender, peer):
        return remote(g_hbm, g_all.at[sender], g_send.at[d], g_recv.at[sender], {"sub": peer})

    def forward_copy(q, d, sender, peer):
        held = g_ext.at[sender, landing(q)]
        return remote(held, held, f_send.at[q, d], f_recv.at[q, sender], {"sub": peer})

    def block_copy(d, sender, peer):
        return remote(block, block_in.at[sender], w_send.at[d], w_recv.at[sender], {"tile": peer})

    pl.semaphore_wait(barrier, len(friends))
    for d, peer in enumerate(tile_peers):
        x_copy(d, j, peer).start()
    for d, peer in enumerate(sub_peers):
        g_copy(d, s, peer).start()
    for d, peer in enumerate(tile_peers):
        strip_copy(d, j, peer).start()

    lane = lax.broadcasted_iota(jnp.int32, (rows, pixels), 1)
    y_at = lane % side

    def around(value):
        out = jnp.where(lane < side, 0.0, pltpu.roll(value, side, 1))
        out = out + jnp.where(lane >= pixels - side, 0.0, pltpu.roll(value, pixels - side, 1))
        out = out + jnp.where(y_at == 0, 0.0, pltpu.roll(value, 1, 1))
        return out + jnp.where(y_at == side - 1, 0.0, pltpu.roll(value, pixels - 1, 1))

    def of_slot(value, m, count):
        return value[m * count : (m + 1) * count]

    previous, current = x_own, -0.25 * around(x_own)
    held = [previous]
    for k in range(1, K):
        held += list(split(current))
        if k < K - 1:
            previous, current = current, -0.5 * around(current) - previous
    terms = [
        jnp.concatenate([of_slot(value, m, chans) for value in held], axis=0).astype(bf16)
        for m in range(slots)
    ]

    for copy in loads:
        copy.wait()
    outer = OUTSIDE * width
    mid_first = [kinds[m] == kinds[0] for m in range(slots)]
    scales = (1.0, -0.5, 0.25, -0.125)

    def ghost_lines(value, at, count):
        first = jnp.dot(value, ghost[0, at], preferred_element_type=f32)
        last = jnp.dot(value, ghost[1, at], preferred_element_type=f32)
        return [
            jnp.where(mid_first[m], of_slot(first, m, count), of_slot(last, m, count))
            for m in range(slots)
        ]

    x_inner = ghost_lines(
        jnp.concatenate(x_strips, axis=1).astype(bf16), slice(outer, outer + 4 * width), chans
    )

    filters = jnp.concatenate([f_ref[k].astype(f32) for k in range(K)], axis=1).astype(bf16)
    pick_row = lax.broadcasted_iota(jnp.int32, (chans, total), 0) + chans * s
    pick_col = lax.broadcasted_iota(jnp.int32, (chans, total), 1)
    mine = jnp.dot(
        jnp.where(pick_row == pick_col, 1.0, 0.0).astype(bf16),
        filters,
        preferred_element_type=f32,
    )
    mixing = jnp.concatenate(
        [mine[:, k * total : (k + 1) * total] for k in range(K)], axis=0
    ).astype(bf16)
    outside = []
    for m in range(DEPTH):
        pieces = [mine[:, (m + 1) * total :]]
        if m > 0:
            pieces.append(jnp.zeros((chans, m * total), f32))
        outside.append(jnp.concatenate(pieces, axis=1))
    outside = jnp.concatenate(outside, axis=0)
    outside = jnp.concatenate([outside, outside], axis=1).astype(bf16)

    for d, peer in enumerate(sub_peers):
        g_copy(d, peer, peer).wait_recv()
    g_full = [
        jnp.concatenate([g_all[e, slot_list[m]].astype(f32) for e in range(subs)], axis=0)
        for m in range(slots)
    ]
    g_bf = [value.astype(bf16) for value in g_full]
    grad = jnp.zeros((terms[0].shape[0], total), f32)
    for m in range(slots):
        grad = grad + product(terms[m], g_bf[m])
    edge = product(jnp.concatenate(g_full, axis=0).astype(bf16), inward[...])
    edge = jnp.concatenate(
        [
            jnp.concatenate(
                [
                    of_slot(edge, m, total)[:, n * width : (n + 1) * width]
                    for n in range(DEPTH)
                ],
                axis=0,
            )
            for m in range(slots)
        ],
        axis=1,
    )
    edge = jnp.concatenate(split(edge), axis=0).astype(bf16)

    for d, peer in enumerate(tile_peers):
        x_copy(d, peer, peer).wait_recv()
    wanted = [
        [table_ref[(base + m) * OUTSIDE + r] for r in range(OUTSIDE)] for m in range(slots)
    ]

    def outer_strips(read):
        return jnp.concatenate(
            [
                jnp.concatenate([read(wanted[m][r]).astype(f32) for r in range(OUTSIDE)], axis=1)
                for m in range(slots)
            ],
            axis=0,
        )

    def by_power(lines):
        return jnp.concatenate(
            [
                lines[:, n * width : (n + 1) * width] * scales[n] for n in range(DEPTH)
            ],
            axis=0,
        )

    x_lines = ghost_lines(
        outer_strips(lambda index: x_ext[index]).astype(bf16), slice(0, outer), chans
    )
    x_lines = jnp.concatenate(
        [by_power(x_lines[m] + x_inner[m]) for m in range(slots)], axis=1
    )
    across = product(jnp.concatenate(split(x_lines), axis=0).astype(bf16), edge)
    half = DEPTH * chans
    across = across[:half] + across[half:]
    across = across[:, : DEPTH * total] + across[:, DEPTH * total :]
    later = [
        of_slot(grad, 2 * k - 1, chans) + of_slot(grad, 2 * k, chans) for k in range(1, K)
    ]
    later = jnp.concatenate(later, axis=1)
    place = lax.broadcasted_iota(jnp.int32, later.shape, 1)
    for n in range(DEPTH):
        shifted = of_slot(across, n, chans)
        if n > 0:
            shifted = jnp.where(
                place < n * total, 0.0, pltpu.roll(shifted, n * total, 1)
            )
        later = later + shifted
    block[0] = later * scale
    block[1] = jnp.concatenate(
        [grad[:chans] * scale, jnp.zeros((chans, width - total), f32)], axis=1
    )
    for d, peer in enumerate(tile_peers):
        block_copy(d, j, peer).start()
    for q, peer in enumerate(tile_peers):
        strip_copy(q, peer, peer).wait_recv()
        for d, other in enumerate(sub_peers):
            forward_copy(peer, d, s, other).start()

    mixed = [jnp.dot(mixing, g_bf[m], preferred_element_type=f32) for m in range(slots)]
    grads = [
        jnp.concatenate([of_slot(mixed[m], k, chans) for m in range(slots)], axis=0)
        for k in range(K)
    ]
    after, upper = grads[K - 1], grads[K - 2] - 0.5 * around(grads[K - 1])
    for k in range(K - 3, 0, -1):
        after, upper = upper, grads[k] - 0.5 * around(upper) - after
    inner = grads[0] - 0.25 * around(upper) - after

    whole = jnp.concatenate(g_full, axis=0)
    whole_strips = strips_of(
        whole, jnp.dot(whole.astype(bf16), take[...], preferred_element_type=f32)
    )
    for m in range(slots):
        for e in range(subs):
            at = slice(m * total + e * chans, m * total + (e + 1) * chans)
            for side_at in range(4):
                g_ext[e, m * 4 + side_at] = whole_strips[side_at][at].astype(bf16)
    g_inner = ghost_lines(
        jnp.concatenate(whole_strips, axis=1).astype(bf16),
        slice(outer, outer + 4 * width),
        total,
    )

    for q, peer in enumerate(tile_peers):
        for d, other in enumerate(sub_peers):
            forward_copy(peer, d, other, other).wait_recv()
    gathered = outer_strips(
        lambda index: jnp.concatenate([g_ext[e, index].astype(f32) for e in range(subs)], axis=0)
    )
    g_lines = ghost_lines(gathered.astype(bf16), slice(0, outer), total)
    g_lines = jnp.concatenate(
        [by_power(g_lines[m] + g_inner[m]) for m in range(slots)], axis=1
    )
    mixed = jnp.dot(
        outside,
        jnp.concatenate(split(g_lines), axis=0).astype(bf16),
        preferred_element_type=f32,
    )
    mixed = jnp.concatenate(
        [
            jnp.concatenate(
                [
                    of_slot(mixed, n, chans)[:, m * width : (m + 1) * width]
                    for n in range(DEPTH)
                ],
                axis=1,
            )
            for m in range(slots)
        ],
        axis=0,
    )
    spread = jnp.dot(
        jnp.concatenate(split(mixed), axis=0).astype(bf16),
        inward[...],
        preferred_element_type=f32,
    )
    inner = inner + spread[:rows] + spread[rows:]
    for m in range(slots):
        result[m] = of_slot(inner, m, chans)
    for slot in range(slots):
        in_ref[slot] = result[lax.rem(map_ref[base + slot], slots)].astype(bf16)

    for d, peer in enumerate(tile_peers):
        block_copy(d, peer, peer).wait_recv()
    block_in[j] = block[...]
    summed = block_in[0]
    for q in range(1, tiles_n):
        summed = summed + block_in[q]
    w_ref[0] = summed[1, :, :total]
    for k in range(1, K):
        w_ref[k] = summed[0, :, (k - 1) * total : k * total]

    for d, peer in enumerate(tile_peers):
        x_copy(d, j, peer).wait_send()
        strip_copy(d, j, peer).wait_send()
        block_copy(d, j, peer).wait_send()
        for e, other in enumerate(sub_peers):
            forward_copy(peer, e, s, other).wait_send()
    for d, peer in enumerate(sub_peers):
        g_copy(d, s, peer).wait_send()


def face_path(features, out_grad, filters, tile_map):
    slots, chans, pixels = features.shape
    side = math.isqrt(pixels)
    tiles_n, subs = lax.axis_size("tile"), lax.axis_size("sub")
    matrices, table, packed, inward, take = ghost_tables(side, slots, tiles_n)
    scale = 1.0 / math.sqrt(slots * tiles_n * pixels)
    width = DEPTH * side
    vmem = pl.BlockSpec(memory_space=pltpu.VMEM)
    hbm = pl.BlockSpec(memory_space=pltpu.HBM)
    dma = pltpu.SemaphoreType.DMA
    bf16, f32 = jnp.bfloat16, jnp.float32
    held = slots * 4 + tiles_n * packed
    return pl.pallas_call(
        functools.partial(face_kernel, (slots, tiles_n, subs, side, packed, scale)),
        out_shape=(
            pltpu.VMEM(features.shape, bf16),
            pltpu.VMEM((K, chans, filters.shape[2]), f32),
        ),
        in_specs=[hbm] * 8,
        out_specs=(vmem, vmem),
        scratch_shapes=[
            pltpu.VMEM(features.shape, bf16),
            pltpu.VMEM(features.shape, bf16),
            pltpu.VMEM((subs,) + features.shape, bf16),
            pltpu.VMEM((slots * 4, chans, width), bf16),
            pltpu.VMEM((slots * 4, chans, width), bf16),
            pltpu.VMEM((tiles_n - 1, packed, chans, width), bf16),
            pltpu.VMEM((tiles_n - 1, packed, chans, width), bf16),
            pltpu.VMEM((held, chans, width), bf16),
            pltpu.VMEM((subs, held, chans, width), bf16),
            pltpu.VMEM((2, chans, width), f32),
            pltpu.VMEM((tiles_n, 2, chans, width), f32),
            pltpu.VMEM((slots, chans, pixels), f32),
            pltpu.VMEM((2,) + matrices.shape[1:], bf16),
            pltpu.VMEM(inward.shape, bf16),
            pltpu.VMEM(take.shape, bf16),
            pltpu.VMEM(filters.shape, bf16),
            pltpu.SMEM(tile_map.shape, jnp.int32),
            pltpu.SMEM(table.shape, jnp.int32),
            dma((10,)),
            dma((tiles_n,)),
            dma((tiles_n,)),
            dma((tiles_n,)),
            dma((tiles_n,)),
            dma((subs,)),
            dma((subs,)),
            dma((tiles_n, subs)),
            dma((tiles_n, subs)),
            dma((tiles_n,)),
            dma((tiles_n,)),
        ],
        compiler_params=pltpu.CompilerParams(
            collective_id=0, has_side_effects=True, vmem_limit_bytes=67043328 - 512 * 1024
        ),
    )(
        features,
        out_grad,
        filters,
        tile_map,
        jnp.asarray(table),
        jnp.asarray(matrices, bf16),
        jnp.asarray(inward, bf16),
        jnp.asarray(take, bf16),
    )


def on_device(features, out_grad, filters, tile_map):
    slots, chans, pixels = features.shape
    side = math.isqrt(pixels)
    whole_faces = slots * lax.axis_size("tile") == 12
    channels = chans * lax.axis_size("sub")
    if whole_faces and 1 < slots < 5 and DEPTH * side == 128 and chans % 8 == 0 and channels == 32:
        return face_path(features, out_grad, filters, tile_map)
    return general_path(features, out_grad, filters, tile_map)


def solution(mesh):
    placed = (P(("grp", "tile"), "sub", None), P(("grp", "tile"), "sub", None), P(), P())
    return jax.shard_map(
        on_device,
        mesh=mesh,
        in_specs=placed,
        out_specs=(P(("grp", "tile"), "sub", None), P("grp", "sub", None)),
        check_vma=False,
    )
```

```python
import functools
import math

import jax
import jax.numpy as jnp
import numpy as np
from jax import lax
from jax.experimental import pallas as pl
from jax.experimental.pallas import tpu as pltpu
from jax.sharding import PartitionSpec as P

K = 5


def from_behind(value, axis, steps):
    count = lax.axis_size(axis)
    pairs = [(source, (source + steps) % count) for source in range(count)]
    return lax.ppermute(value, axis, pairs)


def tile_coords(nested_code, bit_count):
    coord_x = nested_code * 0
    coord_y = nested_code * 0
    for bit_level in range(bit_count):
        coord_x = coord_x + nested_code // 4**bit_level % 2 * 2**bit_level
        coord_y = coord_y + nested_code // (2 * 4**bit_level) % 2 * 2**bit_level
    return (coord_x, coord_y)


def nested_index(coord_x, coord_y, bit_count):
    nested_code = coord_x * 0
    for bit_level in range(bit_count):
        nested_code = nested_code + coord_x // 2**bit_level % 2 * 4**bit_level
        nested_code = nested_code + coord_y // 2**bit_level % 2 * (2 * 4**bit_level)
    return nested_code


def pick(condition, when_true, when_false):
    return when_false + (when_true - when_false) * condition


def neighbour_codes(tile_ids, per_face, side_count):
    bit_count = side_count.bit_length() - 1
    face_id = tile_ids // per_face
    coord_x, coord_y = tile_coords(tile_ids % per_face, bit_count)
    column = face_id % 4
    is_north = face_id < 4
    is_south = face_id >= 8
    last_tile = side_count - 1

    def by_cycle(north_value, equator_value, south_value):
        return pick(is_north, north_value, pick(is_south, south_value, equator_value))

    side_rules = [
        (
            coord_x > 0,
            (face_id, coord_x - 1, coord_y, 1),
            (
                by_cycle(4 + column, 8 + (column + 3) % 4, 8 + (column + 3) % 4),
                by_cycle(last_tile, last_tile, coord_y),
                by_cycle(coord_y, coord_y, 0),
                by_cycle(1, 1, 2),
            ),
        ),
        (
            coord_x < last_tile,
            (face_id, coord_x + 1, coord_y, 0),
            (
                by_cycle((column + 1) % 4, column, 4 + (column + 1) % 4),
                by_cycle(coord_y, 0, 0),
                by_cycle(last_tile, coord_y, coord_y),
                by_cycle(3, 0, 0),
            ),
        ),
        (
            coord_y > 0,
            (face_id, coord_x, coord_y - 1, 3),
            (
                by_cycle(4 + (column + 1) % 4, 8 + column, 8 + (column + 1) % 4),
                by_cycle(coord_x, coord_x, 0),
                by_cycle(last_tile, last_tile, coord_x),
                by_cycle(3, 3, 0),
            ),
        ),
        (
            coord_y < last_tile,
            (face_id, coord_x, coord_y + 1, 2),
            (
                by_cycle((column + 3) % 4, (column + 3) % 4, 4 + column),
                by_cycle(last_tile, coord_x, coord_x),
                by_cycle(coord_x, 0, 0),
                by_cycle(1, 2, 2),
            ),
        ),
    ]
    target_list = []
    edge_list = []
    for inside, within, across in side_rules:
        chosen = [
            pick(inside, near_value, far_value) for near_value, far_value in zip(within, across)
        ]
        target_list.append(chosen[0] * per_face + nested_index(chosen[1], chosen[2], bit_count))
        edge_list.append(chosen[3] + tile_ids * 0)
    return (target_list, edge_list)


def neighbour_table(tile_map, per_face, side_count):
    target_list, edge_list = neighbour_codes(tile_map, per_face, side_count)
    targets = jnp.stack(target_list, axis=1).astype(jnp.int32)
    edges = jnp.stack(edge_list, axis=1).astype(jnp.int32)
    slot_of = jnp.argsort(tile_map).astype(jnp.int32)
    return (slot_of[targets].astype(jnp.int32), edges)


def peer_offsets(slot_count, device_count, per_face, side_count):
    tile_ids = np.arange(slot_count * device_count, dtype=np.int64)
    target_list, edge_list = neighbour_codes(tile_ids, per_face, side_count)
    targets = np.stack(target_list, axis=1)
    offsets = (tile_ids[:, None] // slot_count - targets // slot_count) % device_count
    distinct = sorted(set((int(value) for value in offsets.ravel())) - {0})
    position = np.zeros(device_count, dtype=np.int32)
    for order, value in enumerate(distinct):
        position[value] = order + 1
    return (distinct, position)


def edge_lines(values, tile_side):
    return jnp.stack(
        [
            values[..., :tile_side],
            values[..., -tile_side:],
            values[..., ::tile_side],
            values[..., tile_side - 1 :: tile_side],
        ],
        axis=1,
    )


def stencil(values, ghosts, tile_side):
    position = jnp.arange(values.shape[-1]) % tile_side
    zero_line = jnp.zeros_like(values[..., :1])
    upper_side = jnp.concatenate([ghosts[:, 0], values[..., :-tile_side]], axis=-1)
    lower_side = jnp.concatenate([values[..., tile_side:], ghosts[:, 1]], axis=-1)
    left_side = jnp.where(
        position == 0,
        jnp.repeat(ghosts[:, 2], tile_side, axis=-1),
        jnp.concatenate([zero_line, values[..., :-1]], axis=-1),
    )
    right_side = jnp.where(
        position == tile_side - 1,
        jnp.repeat(ghosts[:, 3], tile_side, axis=-1),
        jnp.concatenate([values[..., 1:], zero_line], axis=-1),
    )
    return -0.25 * (upper_side + lower_side + left_side + right_side)


def tile_total(filter_part):
    return lax.psum(filter_part, "tile")


def general_path(features, out_grad, filters, tile_map):
    slot_count = features.shape[0]
    group_channels = features.shape[1]
    tile_side = math.isqrt(features.shape[2])
    device_count = lax.axis_size("tile")
    total_tiles = slot_count * device_count
    side_count = math.isqrt(total_tiles // 12)
    scale_factor = 1.0 / math.sqrt(total_tiles * features.shape[2])
    highest = lax.Precision.HIGHEST
    slot_table, edge_table = neighbour_table(tile_map, total_tiles // 12, side_count)
    my_device = lax.axis_index("tile")
    first_slot = my_device * slot_count
    my_slots = lax.dynamic_slice_in_dim(slot_table, first_slot, slot_count, 0)
    my_edges = lax.dynamic_slice_in_dim(edge_table, first_slot, slot_count, 0)
    channel_start = lax.axis_index("sub") * group_channels
    weights = filters.astype(jnp.float32)
    distinct, position = peer_offsets(slot_count, device_count, total_tiles // 12, side_count)
    sender_gap = (my_device - my_slots // slot_count) % device_count
    local_rows = jnp.asarray(position)[sender_gap] * slot_count + my_slots % slot_count

    def laplace(values):
        border = edge_lines(values, tile_side).reshape(slot_count, 4, group_channels * tile_side)
        received = [border]
        for offset_value in distinct:
            received.append(from_behind(border, "tile", offset_value))
        stacked = jnp.concatenate(received, axis=0)
        stacked = stacked.reshape(stacked.shape[0], 4, group_channels, tile_side)
        rows = []
        for slot in range(slot_count):
            for side in range(4):
                start = (local_rows[slot, side], my_edges[slot, side], 0, 0)
                rows.append(
                    lax.dynamic_slice(stacked, start, (1, 1, group_channels, tile_side))
                )
        ghosts = jnp.concatenate(rows, axis=0)
        ghosts = ghosts.reshape(slot_count, 4, group_channels, tile_side)
        return stencil(values, ghosts, tile_side)

    whole_grad = lax.all_gather(out_grad, "sub", axis=1, tiled=True)
    cotangent = whole_grad.astype(jnp.float32)
    inputs = features.astype(jnp.float32)
    previous, current = (inputs, laplace(inputs))
    filter_terms = [
        jnp.einsum("sip,sop->io", inputs, cotangent, precision=highest),
        jnp.einsum("sip,sop->io", current, cotangent, precision=highest),
    ]
    for degree in range(2, K):
        previous, current = (current, 2.0 * laplace(current) - previous)
        filter_terms.append(jnp.einsum("sip,sop->io", current, cotangent, precision=highest))
    weight_grad = tile_total(jnp.stack(filter_terms)) * scale_factor
    row_block = lax.dynamic_slice_in_dim(weights, channel_start, group_channels, 1)

    def mixed(degree):
        return jnp.einsum("sop,io->sip", cotangent, row_block[degree], precision=highest)

    next_sum = mixed(K - 1)
    after_next = jnp.zeros_like(next_sum)
    for degree in range(K - 2, 0, -1):
        next_sum, after_next = (mixed(degree) + 2.0 * laplace(next_sum) - after_next, next_sum)
    in_grad = (mixed(0) + laplace(next_sum) - after_next).astype(jnp.bfloat16)
    return (in_grad, weight_grad)


DEPTH = K - 1
GHOST_SIDES = (0, 2, 3, 1)
OUTSIDE = 6


def face_graph(tile_side):
    tile_ids = np.arange(12, dtype=np.int64)
    target_list, edge_list = neighbour_codes(tile_ids, 1, 1)
    targets = np.stack(target_list, axis=1)
    edges = np.stack(edge_list, axis=1)
    pixels = tile_side * tile_side
    grid = np.arange(pixels).reshape(tile_side, tile_side)
    lines = [grid[0], grid[-1], grid[:, 0], grid[:, -1]]
    ghosts = np.zeros((12, 4, tile_side), dtype=np.int64)
    around = np.zeros((12, 4, tile_side, tile_side), dtype=np.int64)
    for tile in range(12):
        for side in range(4):
            ghosts[tile, side] = targets[tile, side] * pixels + lines[edges[tile, side]]
        whole = tile * pixels + grid
        around[tile, 0] = np.concatenate([ghosts[tile, 0][None], whole[:-1]], 0)
        around[tile, 1] = np.concatenate([whole[1:], ghosts[tile, 1][None]], 0)
        around[tile, 2] = np.concatenate([ghosts[tile, 2][:, None], whole[:, :-1]], 1)
        around[tile, 3] = np.concatenate([whole[:, 1:], ghosts[tile, 3][:, None]], 1)
    around = around.transpose(0, 2, 3, 1).reshape(12 * pixels, 4)
    return targets, edges, ghosts, around


@functools.lru_cache(None)
def ghost_tables(tile_side, slots, tiles_n):
    targets, edges, ghosts, around = face_graph(tile_side)
    pixels = tile_side * tile_side
    grid = np.arange(pixels).reshape(tile_side, tile_side)
    strips = np.stack(
        [
            grid[:DEPTH].ravel(),
            grid[-DEPTH:].ravel(),
            grid[:, :DEPTH].T.ravel(),
            grid[:, -DEPTH:].T.ravel(),
        ]
    )
    sources_of = []
    by_class = []
    for tile in range(12):
        wanted = np.concatenate([ghosts[tile, side] for side in GHOST_SIDES])
        power = np.zeros((wanted.size, 12 * pixels), dtype=np.int32)
        power[np.arange(wanted.size), wanted] = 1
        powers = [power]
        for _ in range(DEPTH - 1):
            powers.append(sum(powers[-1][:, around[:, side]] for side in range(4)))
        rows = np.concatenate(
            [powers[0], powers[1], powers[2] - 8 * powers[0], powers[3] - 12 * powers[1]]
        )
        support = np.flatnonzero(np.any(rows != 0, axis=0))
        sources = [(int(targets[tile, side]), int(edges[tile, side])) for side in range(4)]
        own = [(tile, side) for side in range(4)]
        covered = set(int(t) * pixels + int(p) for t, e in sources + own for p in strips[e])
        left = [int(p) for p in support if int(p) not in covered]
        corner_tiles = {}
        for pixel in left:
            corner_tiles.setdefault(pixel // pixels, []).append(pixel % pixels)
        first = lambda t: int(
            np.flatnonzero(np.any(rows[:, [t * pixels + p for p in corner_tiles[t]]] != 0, axis=1))[0]
        )
        for other in sorted(corner_tiles, key=first):
            choice = [e for e in range(4) if set(corner_tiles[other]) <= set(strips[e].tolist())]
            sources.append((other, choice[0]))
        assert len(sources) <= OUTSIDE
        while len(sources) < OUTSIDE:
            sources.append(sources[-1])
        sources_of.append(sources)
        lanes = np.concatenate([t * pixels + strips[e] for t, e in sources + own])
        seen, keep = set(), np.zeros(lanes.size, dtype=bool)
        for lane, pixel in enumerate(lanes.tolist()):
            keep[lane] = pixel not in seen
            seen.add(pixel)
        assert set(support.tolist()) <= seen
        matrix = (rows[:, lanes] * keep[None]).T
        assert np.abs(matrix).max() <= 127
        if tile % 4 == 0:
            by_class.append(matrix)
        else:
            assert np.array_equal(matrix, by_class[-1])
    wanted = {}
    for tile in range(12):
        for t, e in sources_of[tile]:
            pair = (t // slots, tile // slots)
            if pair[0] != pair[1]:
                held = wanted.setdefault(pair, [])
                if (t, e) not in held:
                    held.append((t, e))
    packed = max(len(held) for held in wanted.values())
    send = np.zeros((tiles_n, tiles_n, packed), dtype=np.int32)
    for (q, p), held in wanted.items():
        for order, (t, e) in enumerate(held):
            send[q, p, order] = (t - q * slots) * 4 + e
    take_from = np.zeros((12, OUTSIDE), dtype=np.int32)
    for tile in range(12):
        for order, (t, e) in enumerate(sources_of[tile]):
            q, p = t // slots, tile // slots
            if q == p:
                take_from[tile, order] = (t - q * slots) * 4 + e
            else:
                at = wanted[(q, p)].index((t, e))
                take_from[tile, order] = slots * 4 + q * packed + at
    table = np.concatenate([take_from.ravel(), send.ravel()])
    spread = np.zeros((4, tile_side, tile_side, tile_side))
    step = np.arange(tile_side)
    spread[0, step, 0, step] = 1
    spread[1, step, step, 0] = 1
    spread[2, step, step, -1] = 1
    spread[3, step, -1, step] = 1
    local = np.zeros((pixels, pixels))
    for u in range(tile_side):
        for v in range(tile_side):
            for du, dv in ((1, 0), (-1, 0), (0, 1), (0, -1)):
                if 0 <= u + du < tile_side and 0 <= v + dv < tile_side:
                    local[grid[u, v], grid[u + du, v + dv]] = -0.25
    inward = [-0.25 * spread.reshape(4 * tile_side, pixels)]
    inward.append(2.0 * inward[0] @ local)
    for _ in range(DEPTH - 2):
        inward.append(2.0 * inward[-1] @ local - inward[-2])
    inward = np.concatenate(inward)
    assert np.array_equal(inward, inward.astype(jnp.bfloat16).astype(np.float64))
    take = np.zeros((pixels, 2 * DEPTH * tile_side), dtype=np.float32)
    take[np.concatenate([strips[2], strips[3]]), np.arange(2 * DEPTH * tile_side)] = 1
    return np.stack(by_class), table, packed, inward, take


def split(value):
    high = value.astype(jnp.bfloat16).astype(jnp.float32)
    return high, value - high


def product(left, right):
    return lax.dot_general(
        left, right, (((1,), (1,)), ((), ())), preferred_element_type=jnp.float32
    )


def face_kernel(
    sizes,
    x_hbm,
    g_hbm,
    f_hbm,
    map_hbm,
    table_hbm,
    ghost_hbm,
    inward_hbm,
    take_hbm,
    in_ref,
    w_ref,
    x_ref,
    g_ref,
    g_all,
    x_mine,
    g_mine,
    x_pack,
    g_pack,
    x_ext,
    g_ext,
    block,
    block_in,
    result,
    ghost,
    inward,
    take,
    f_ref,
    map_ref,
    table_ref,
    load_sem,
    x_send,
    x_recv,
    s_send,
    s_recv,
    g_send,
    g_recv,
    f_send,
    f_recv,
    w_send,
    w_recv,
):
    slots, tiles_n, subs, side, packed, scale = sizes
    chans = x_ref.shape[1]
    total = subs * chans
    pixels = side * side
    width = DEPTH * side
    rows = slots * chans
    bf16, f32 = jnp.bfloat16, jnp.float32
    j = lax.axis_index("tile")
    s = lax.axis_index("sub")
    tile_peers = []
    for d in range(tiles_n - 1):
        up = d + (j <= d).astype(jnp.int32)
        back = tiles_n - 2 - d
        down = back + (j <= back).astype(jnp.int32)
        tile_peers.append(jnp.where(2 * j < tiles_n, down, up))
    sub_peers = [lax.rem(s + d, subs) for d in range(1, subs)]
    friends = [{"tile": peer} for peer in tile_peers] + [{"sub": peer} for peer in sub_peers]
    kinds = [(slots * j + m) // 4 for m in range(slots)]

    first_loads = [
        pltpu.make_async_copy(map_hbm, map_ref, load_sem.at[0]),
        pltpu.make_async_copy(table_hbm, table_ref, load_sem.at[1]),
        pltpu.make_async_copy(x_hbm, x_ref, load_sem.at[2]),
        pltpu.make_async_copy(g_hbm, g_ref, load_sem.at[3]),
        pltpu.make_async_copy(take_hbm, take, load_sem.at[4]),
    ]
    for copy in first_loads:
        copy.start()
    barrier = pltpu.get_barrier_semaphore()
    for friend in friends:
        pl.semaphore_signal(
            barrier, inc=1, device_id=friend, device_id_type=pl.DeviceIdType.MESH
        )
    loads = [
        pltpu.make_async_copy(ghost_hbm.at[kinds[0]], ghost.at[0], load_sem.at[5]),
        pltpu.make_async_copy(ghost_hbm.at[kinds[-1]], ghost.at[1], load_sem.at[6]),
        pltpu.make_async_copy(inward_hbm, inward, load_sem.at[7]),
        pltpu.make_async_copy(f_hbm, f_ref, load_sem.at[8]),
        pltpu.make_async_copy(g_hbm, g_all.at[s], load_sem.at[9]),
    ]
    for copy in loads:
        copy.start()

    def remote(source, target, send, recv, device):
        return pltpu.make_async_remote_copy(
            source,
            target,
            send,
            recv,
            device_id=device,
            device_id_type=pl.DeviceIdType.MESH,
        )

    def g_copy(d, sender, peer):
        return remote(g_hbm, g_all.at[sender], g_send.at[d], g_recv.at[sender], {"sub": peer})

    def open_up():
        pl.semaphore_wait(barrier, len(friends))
        for d, peer in enumerate(sub_peers):
            g_copy(d, s, peer).start()

    late = j == tiles_n - 1
    pl.when(late)(open_up)
    base = slots * j
    for copy in first_loads:
        copy.wait()

    def slot_of(m):
        found = 0
        for slot in range(1, slots):
            found = jnp.where(map_ref[base + slot] == base + m, slot, found)
        return found

    slot_list = [slot_of(m) for m in range(slots)]
    x_own = jnp.concatenate([x_ref[slot_list[m]].astype(f32) for m in range(slots)], axis=0)
    g_own = jnp.concatenate([g_ref[slot_list[m]].astype(f32) for m in range(slots)], axis=0)
    both = jnp.concatenate([x_own, g_own], axis=0).astype(bf16)
    cut = jnp.dot(both, take[...], preferred_element_type=f32)

    def strips_of(value, cut_value):
        return [
            value[:, :width],
            value[:, pixels - width :],
            cut_value[:, :width],
            cut_value[:, width:],
        ]

    x_strips = strips_of(x_own, cut[:rows])
    g_strips = strips_of(g_own, cut[rows:])
    for m in range(slots):
        at = slice(m * chans, (m + 1) * chans)
        for e in range(4):
            x_mine[m * 4 + e] = x_strips[e][at].astype(bf16)
            g_mine[m * 4 + e] = g_strips[e][at].astype(bf16)
    sends = 12 * OUTSIDE
    for d, peer in enumerate(tile_peers):
        for i in range(packed):
            index = table_ref[sends + (j * tiles_n + peer) * packed + i]
            x_pack[d, i] = x_mine[index]
            g_pack[d, i] = g_mine[index]
    for m in range(slots):
        at = slice(m * chans, (m + 1) * chans)
        for e in range(4):
            x_ext[m * 4 + e] = x_strips[e][at].astype(bf16)

    def landing(sender):
        return pl.ds(slots * 4 + sender * packed, packed)

    def x_copy(d, sender, peer):
        return remote(
            x_pack.at[d], x_ext.at[landing(sender)], x_send.at[d], x_recv.at[sender], {"tile": peer}
        )

    def strip_copy(d, sender, peer):
        return remote(
            g_pack.at[d],
            g_ext.at[s, landing(sender)],
            s_send.at[d],
            s_recv.at[sender],
            {"tile": peer},
        )

    def forward_copy(q, d, sender, peer):
        held = g_ext.at[sender, landing(q)]
        return remote(held, held, f_send.at[q, d], f_recv.at[q, sender], {"sub": peer})

    def block_copy(d, sender, peer):
        return remote(block, block_in.at[sender], w_send.at[d], w_recv.at[sender], {"tile": peer})

    pl.when(jnp.logical_not(late))(open_up)
    for d, peer in enumerate(tile_peers):
        x_copy(d, j, peer).start()
    for d, peer in enumerate(tile_peers):
        strip_copy(d, j, peer).start()

    lane = lax.broadcasted_iota(jnp.int32, (rows, pixels), 1)
    y_at = lane % side

    def around(value):
        out = jnp.where(lane < side, 0.0, pltpu.roll(value, side, 1))
        out = out + jnp.where(lane >= pixels - side, 0.0, pltpu.roll(value, pixels - side, 1))
        out = out + jnp.where(y_at == 0, 0.0, pltpu.roll(value, 1, 1))
        return out + jnp.where(y_at == side - 1, 0.0, pltpu.roll(value, pixels - 1, 1))

    def of_slot(value, m, count):
        return value[m * count : (m + 1) * count]

    previous, current = x_own, -0.25 * around(x_own)
    held = [previous]
    for k in range(1, K):
        held += list(split(current))
        if k < K - 1:
            previous, current = current, -0.5 * around(current) - previous
    terms = [
        jnp.concatenate([of_slot(value, m, chans) for value in held], axis=0).astype(bf16)
        for m in range(slots)
    ]

    for copy in loads:
        copy.wait()
    outer = OUTSIDE * width
    mid_first = [kinds[m] == kinds[0] for m in range(slots)]
    scales = (1.0, -0.5, 0.25, -0.125)

    def ghost_lines(value, at, count):
        first = jnp.dot(value, ghost[0, at], preferred_element_type=f32)
        last = jnp.dot(value, ghost[1, at], preferred_element_type=f32)
        return [
            jnp.where(mid_first[m], of_slot(first, m, count), of_slot(last, m, count))
            for m in range(slots)
        ]

    x_inner = ghost_lines(
        jnp.concatenate(x_strips, axis=1).astype(bf16), slice(outer, outer + 4 * width), chans
    )

    filters = jnp.concatenate([f_ref[k].astype(f32) for k in range(K)], axis=1).astype(bf16)
    pick_row = lax.broadcasted_iota(jnp.int32, (chans, total), 0) + chans * s
    pick_col = lax.broadcasted_iota(jnp.int32, (chans, total), 1)
    mine = jnp.dot(
        jnp.where(pick_row == pick_col, 1.0, 0.0).astype(bf16),
        filters,
        preferred_element_type=f32,
    )
    mixing = jnp.concatenate(
        [mine[:, k * total : (k + 1) * total] for k in range(K)], axis=0
    ).astype(bf16)
    outside = []
    for m in range(DEPTH):
        pieces = [mine[:, (m + 1) * total :]]
        if m > 0:
            pieces.append(jnp.zeros((chans, m * total), f32))
        outside.append(jnp.concatenate(pieces, axis=1))
    outside = jnp.concatenate(outside, axis=0)
    outside = jnp.concatenate([outside, outside], axis=1).astype(bf16)

    for d, peer in enumerate(sub_peers):
        g_copy(d, peer, peer).wait_recv()
    g_full = [
        jnp.concatenate([g_all[e, slot_list[m]].astype(f32) for e in range(subs)], axis=0)
        for m in range(slots)
    ]
    g_bf = [value.astype(bf16) for value in g_full]
    grad = jnp.zeros((terms[0].shape[0], total), f32)
    for m in range(slots):
        grad = grad + product(terms[m], g_bf[m])
    edge = product(jnp.concatenate(g_full, axis=0).astype(bf16), inward[...])
    edge = jnp.concatenate(
        [
            jnp.concatenate(
                [
                    of_slot(edge, m, total)[:, n * width : (n + 1) * width]
                    for n in range(DEPTH)
                ],
                axis=0,
            )
            for m in range(slots)
        ],
        axis=1,
    )
    edge = jnp.concatenate(split(edge), axis=0).astype(bf16)

    for d, peer in enumerate(tile_peers):
        x_copy(d, peer, peer).wait_recv()

    def pass_on():
        for q, peer in enumerate(tile_peers):
            strip_copy(q, peer, peer).wait_recv()
            for d, other in enumerate(sub_peers):
                forward_copy(peer, d, s, other).start()

    pl.when(2 * j < tiles_n)(pass_on)
    wanted = [
        [table_ref[(base + m) * OUTSIDE + r] for r in range(OUTSIDE)] for m in range(slots)
    ]

    def outer_strips(read):
        return jnp.concatenate(
            [
                jnp.concatenate([read(wanted[m][r]).astype(f32) for r in range(OUTSIDE)], axis=1)
                for m in range(slots)
            ],
            axis=0,
        )

    def by_power(lines):
        return jnp.concatenate(
            [
                lines[:, n * width : (n + 1) * width] * scales[n] for n in range(DEPTH)
            ],
            axis=0,
        )

    x_lines = ghost_lines(
        outer_strips(lambda index: x_ext[index]).astype(bf16), slice(0, outer), chans
    )
    x_lines = jnp.concatenate(
        [by_power(x_lines[m] + x_inner[m]) for m in range(slots)], axis=1
    )
    across = product(jnp.concatenate(split(x_lines), axis=0).astype(bf16), edge)
    half = DEPTH * chans
    across = across[:half] + across[half:]
    across = across[:, : DEPTH * total] + across[:, DEPTH * total :]
    later = [
        of_slot(grad, 2 * k - 1, chans) + of_slot(grad, 2 * k, chans) for k in range(1, K)
    ]
    later = jnp.concatenate(later, axis=1)
    place = lax.broadcasted_iota(jnp.int32, later.shape, 1)
    for n in range(DEPTH):
        shifted = of_slot(across, n, chans)
        if n > 0:
            shifted = jnp.where(
                place < n * total, 0.0, pltpu.roll(shifted, n * total, 1)
            )
        later = later + shifted
    block[0] = later * scale
    block[1] = jnp.concatenate(
        [grad[:chans] * scale, jnp.zeros((chans, width - total), f32)], axis=1
    )
    for d, peer in enumerate(tile_peers):
        block_copy(d, j, peer).start()
    pl.when(2 * j >= tiles_n)(pass_on)

    mixed = [jnp.dot(mixing, g_bf[m], preferred_element_type=f32) for m in range(slots)]
    grads = [
        jnp.concatenate([of_slot(mixed[m], k, chans) for m in range(slots)], axis=0)
        for k in range(K)
    ]
    after, upper = grads[K - 1], grads[K - 2] - 0.5 * around(grads[K - 1])
    for k in range(K - 3, 0, -1):
        after, upper = upper, grads[k] - 0.5 * around(upper) - after
    inner = grads[0] - 0.25 * around(upper) - after

    whole = jnp.concatenate(g_full, axis=0)
    whole_strips = strips_of(
        whole, jnp.dot(whole.astype(bf16), take[...], preferred_element_type=f32)
    )
    for m in range(slots):
        for e in range(subs):
            at = slice(m * total + e * chans, m * total + (e + 1) * chans)
            for side_at in range(4):
                g_ext[e, m * 4 + side_at] = whole_strips[side_at][at].astype(bf16)
    g_inner = ghost_lines(
        jnp.concatenate(whole_strips, axis=1).astype(bf16),
        slice(outer, outer + 4 * width),
        total,
    )

    for q, peer in enumerate(tile_peers):
        for d, other in enumerate(sub_peers):
            forward_copy(peer, d, other, other).wait_recv()
    gathered = outer_strips(
        lambda index: jnp.concatenate([g_ext[e, index].astype(f32) for e in range(subs)], axis=0)
    )
    g_lines = ghost_lines(gathered.astype(bf16), slice(0, outer), total)
    g_lines = jnp.concatenate(
        [by_power(g_lines[m] + g_inner[m]) for m in range(slots)], axis=1
    )
    mixed = jnp.dot(
        outside,
        jnp.concatenate(split(g_lines), axis=0).astype(bf16),
        preferred_element_type=f32,
    )
    mixed = jnp.concatenate(
        [
            jnp.concatenate(
                [
                    of_slot(mixed, n, chans)[:, m * width : (m + 1) * width]
                    for n in range(DEPTH)
                ],
                axis=1,
            )
            for m in range(slots)
        ],
        axis=0,
    )
    spread = jnp.dot(
        jnp.concatenate(split(mixed), axis=0).astype(bf16),
        inward[...],
        preferred_element_type=f32,
    )
    inner = inner + spread[:rows] + spread[rows:]
    for m in range(slots):
        result[m] = of_slot(inner, m, chans)
    for slot in range(slots):
        in_ref[slot] = result[lax.rem(map_ref[base + slot], slots)].astype(bf16)

    for d, peer in enumerate(tile_peers):
        block_copy(d, peer, peer).wait_recv()
    block_in[j] = block[...]
    summed = block_in[0]
    for q in range(1, tiles_n):
        summed = summed + block_in[q]
    w_ref[0] = summed[1, :, :total]
    for k in range(1, K):
        w_ref[k] = summed[0, :, (k - 1) * total : k * total]

    for d, peer in enumerate(tile_peers):
        x_copy(d, j, peer).wait_send()
        strip_copy(d, j, peer).wait_send()
        block_copy(d, j, peer).wait_send()
        for e, other in enumerate(sub_peers):
            forward_copy(peer, e, s, other).wait_send()
    for d, peer in enumerate(sub_peers):
        g_copy(d, s, peer).wait_send()


def store_kernel(in_vmem, w_vmem, in_hbm, w_hbm, sem):
    copies = [
        pltpu.make_async_copy(in_vmem, in_hbm, sem.at[0]),
        pltpu.make_async_copy(w_vmem, w_hbm, sem.at[1]),
    ]
    for copy in copies:
        copy.start()
    for copy in copies:
        copy.wait()


def face_path(features, out_grad, filters, tile_map):
    slots, chans, pixels = features.shape
    side = math.isqrt(pixels)
    tiles_n, subs = lax.axis_size("tile"), lax.axis_size("sub")
    matrices, table, packed, inward, take = ghost_tables(side, slots, tiles_n)
    scale = 1.0 / math.sqrt(slots * tiles_n * pixels)
    width = DEPTH * side
    vmem = pl.BlockSpec(memory_space=pltpu.VMEM)
    hbm = pl.BlockSpec(memory_space=pltpu.HBM)
    dma = pltpu.SemaphoreType.DMA
    bf16, f32 = jnp.bfloat16, jnp.float32
    held = slots * 4 + tiles_n * packed
    held_outs = pl.pallas_call(
        functools.partial(face_kernel, (slots, tiles_n, subs, side, packed, scale)),
        out_shape=(
            pltpu.VMEM(features.shape, bf16),
            pltpu.VMEM((K, chans, filters.shape[2]), f32),
        ),
        in_specs=[hbm] * 8,
        out_specs=(vmem, vmem),
        scratch_shapes=[
            pltpu.VMEM(features.shape, bf16),
            pltpu.VMEM(features.shape, bf16),
            pltpu.VMEM((subs,) + features.shape, bf16),
            pltpu.VMEM((slots * 4, chans, width), bf16),
            pltpu.VMEM((slots * 4, chans, width), bf16),
            pltpu.VMEM((tiles_n - 1, packed, chans, width), bf16),
            pltpu.VMEM((tiles_n - 1, packed, chans, width), bf16),
            pltpu.VMEM((held, chans, width), bf16),
            pltpu.VMEM((subs, held, chans, width), bf16),
            pltpu.VMEM((2, chans, width), f32),
            pltpu.VMEM((tiles_n, 2, chans, width), f32),
            pltpu.VMEM((slots, chans, pixels), f32),
            pltpu.VMEM((2,) + matrices.shape[1:], bf16),
            pltpu.VMEM(inward.shape, bf16),
            pltpu.VMEM(take.shape, bf16),
            pltpu.VMEM(filters.shape, bf16),
            pltpu.SMEM(tile_map.shape, jnp.int32),
            pltpu.SMEM(table.shape, jnp.int32),
            dma((10,)),
            dma((tiles_n,)),
            dma((tiles_n,)),
            dma((tiles_n,)),
            dma((tiles_n,)),
            dma((subs,)),
            dma((subs,)),
            dma((tiles_n, subs)),
            dma((tiles_n, subs)),
            dma((tiles_n,)),
            dma((tiles_n,)),
        ],
        compiler_params=pltpu.CompilerParams(
            collective_id=0, has_side_effects=True, vmem_limit_bytes=67043328 - 512 * 1024
        ),
    )(
        features,
        out_grad,
        filters,
        tile_map,
        jnp.asarray(table),
        jnp.asarray(matrices, bf16),
        jnp.asarray(inward, bf16),
        jnp.asarray(take, bf16),
    )
    held_outs = [pltpu.with_memory_space_constraint(value, pltpu.VMEM) for value in held_outs]
    return pl.pallas_call(
        store_kernel,
        out_shape=(
            jax.ShapeDtypeStruct(features.shape, bf16),
            jax.ShapeDtypeStruct((K, chans, filters.shape[2]), f32),
        ),
        in_specs=[vmem] * 2,
        out_specs=(hbm, hbm),
        scratch_shapes=[dma((2,))],
    )(*held_outs)


def on_device(features, out_grad, filters, tile_map):
    slots, chans, pixels = features.shape
    side = math.isqrt(pixels)
    whole_faces = slots * lax.axis_size("tile") == 12
    channels = chans * lax.axis_size("sub")
    if whole_faces and 1 < slots < 5 and DEPTH * side == 128 and chans % 8 == 0 and channels == 32:
        return face_path(features, out_grad, filters, tile_map)
    return general_path(features, out_grad, filters, tile_map)


def solution(mesh):
    placed = (P(("grp", "tile"), "sub", None), P(("grp", "tile"), "sub", None), P(), P())
    return jax.shard_map(
        on_device,
        mesh=mesh,
        in_specs=placed,
        out_specs=(P(("grp", "tile"), "sub", None), P("grp", "sub", None)),
        check_vma=False,
    )
```

```python
import functools
import math

import jax
import jax.numpy as jnp
import numpy as np
from jax import lax
from jax.experimental import pallas as pl
from jax.experimental.pallas import tpu as pltpu
from jax.sharding import PartitionSpec as P

K = 5


def from_behind(value, axis, steps):
    count = lax.axis_size(axis)
    pairs = [(source, (source + steps) % count) for source in range(count)]
    return lax.ppermute(value, axis, pairs)


def tile_coords(nested_code, bit_count):
    coord_x = nested_code * 0
    coord_y = nested_code * 0
    for bit_level in range(bit_count):
        coord_x = coord_x + nested_code // 4**bit_level % 2 * 2**bit_level
        coord_y = coord_y + nested_code // (2 * 4**bit_level) % 2 * 2**bit_level
    return (coord_x, coord_y)


def nested_index(coord_x, coord_y, bit_count):
    nested_code = coord_x * 0
    for bit_level in range(bit_count):
        nested_code = nested_code + coord_x // 2**bit_level % 2 * 4**bit_level
        nested_code = nested_code + coord_y // 2**bit_level % 2 * (2 * 4**bit_level)
    return nested_code


def pick(condition, when_true, when_false):
    return when_false + (when_true - when_false) * condition


def neighbour_codes(tile_ids, per_face, side_count):
    bit_count = side_count.bit_length() - 1
    face_id = tile_ids // per_face
    coord_x, coord_y = tile_coords(tile_ids % per_face, bit_count)
    column = face_id % 4
    is_north = face_id < 4
    is_south = face_id >= 8
    last_tile = side_count - 1

    def by_cycle(north_value, equator_value, south_value):
        return pick(is_north, north_value, pick(is_south, south_value, equator_value))

    side_rules = [
        (
            coord_x > 0,
            (face_id, coord_x - 1, coord_y, 1),
            (
                by_cycle(4 + column, 8 + (column + 3) % 4, 8 + (column + 3) % 4),
                by_cycle(last_tile, last_tile, coord_y),
                by_cycle(coord_y, coord_y, 0),
                by_cycle(1, 1, 2),
            ),
        ),
        (
            coord_x < last_tile,
            (face_id, coord_x + 1, coord_y, 0),
            (
                by_cycle((column + 1) % 4, column, 4 + (column + 1) % 4),
                by_cycle(coord_y, 0, 0),
                by_cycle(last_tile, coord_y, coord_y),
                by_cycle(3, 0, 0),
            ),
        ),
        (
            coord_y > 0,
            (face_id, coord_x, coord_y - 1, 3),
            (
                by_cycle(4 + (column + 1) % 4, 8 + column, 8 + (column + 1) % 4),
                by_cycle(coord_x, coord_x, 0),
                by_cycle(last_tile, last_tile, coord_x),
                by_cycle(3, 3, 0),
            ),
        ),
        (
            coord_y < last_tile,
            (face_id, coord_x, coord_y + 1, 2),
            (
                by_cycle((column + 3) % 4, (column + 3) % 4, 4 + column),
                by_cycle(last_tile, coord_x, coord_x),
                by_cycle(coord_x, 0, 0),
                by_cycle(1, 2, 2),
            ),
        ),
    ]
    target_list = []
    edge_list = []
    for inside, within, across in side_rules:
        chosen = [
            pick(inside, near_value, far_value) for near_value, far_value in zip(within, across)
        ]
        target_list.append(chosen[0] * per_face + nested_index(chosen[1], chosen[2], bit_count))
        edge_list.append(chosen[3] + tile_ids * 0)
    return (target_list, edge_list)


def neighbour_table(tile_map, per_face, side_count):
    target_list, edge_list = neighbour_codes(tile_map, per_face, side_count)
    targets = jnp.stack(target_list, axis=1).astype(jnp.int32)
    edges = jnp.stack(edge_list, axis=1).astype(jnp.int32)
    slot_of = jnp.argsort(tile_map).astype(jnp.int32)
    return (slot_of[targets].astype(jnp.int32), edges)


def peer_offsets(slot_count, device_count, per_face, side_count):
    tile_ids = np.arange(slot_count * device_count, dtype=np.int64)
    target_list, edge_list = neighbour_codes(tile_ids, per_face, side_count)
    targets = np.stack(target_list, axis=1)
    offsets = (tile_ids[:, None] // slot_count - targets // slot_count) % device_count
    distinct = sorted(set((int(value) for value in offsets.ravel())) - {0})
    position = np.zeros(device_count, dtype=np.int32)
    for order, value in enumerate(distinct):
        position[value] = order + 1
    return (distinct, position)


def edge_lines(values, tile_side):
    return jnp.stack(
        [
            values[..., :tile_side],
            values[..., -tile_side:],
            values[..., ::tile_side],
            values[..., tile_side - 1 :: tile_side],
        ],
        axis=1,
    )


def stencil(values, ghosts, tile_side):
    position = jnp.arange(values.shape[-1]) % tile_side
    zero_line = jnp.zeros_like(values[..., :1])
    upper_side = jnp.concatenate([ghosts[:, 0], values[..., :-tile_side]], axis=-1)
    lower_side = jnp.concatenate([values[..., tile_side:], ghosts[:, 1]], axis=-1)
    left_side = jnp.where(
        position == 0,
        jnp.repeat(ghosts[:, 2], tile_side, axis=-1),
        jnp.concatenate([zero_line, values[..., :-1]], axis=-1),
    )
    right_side = jnp.where(
        position == tile_side - 1,
        jnp.repeat(ghosts[:, 3], tile_side, axis=-1),
        jnp.concatenate([values[..., 1:], zero_line], axis=-1),
    )
    return -0.25 * (upper_side + lower_side + left_side + right_side)


def tile_total(filter_part):
    return lax.psum(filter_part, "tile")


def general_path(features, out_grad, filters, tile_map):
    slot_count = features.shape[0]
    group_channels = features.shape[1]
    tile_side = math.isqrt(features.shape[2])
    device_count = lax.axis_size("tile")
    total_tiles = slot_count * device_count
    side_count = math.isqrt(total_tiles // 12)
    scale_factor = 1.0 / math.sqrt(total_tiles * features.shape[2])
    highest = lax.Precision.HIGHEST
    slot_table, edge_table = neighbour_table(tile_map, total_tiles // 12, side_count)
    my_device = lax.axis_index("tile")
    first_slot = my_device * slot_count
    my_slots = lax.dynamic_slice_in_dim(slot_table, first_slot, slot_count, 0)
    my_edges = lax.dynamic_slice_in_dim(edge_table, first_slot, slot_count, 0)
    channel_start = lax.axis_index("sub") * group_channels
    weights = filters.astype(jnp.float32)
    distinct, position = peer_offsets(slot_count, device_count, total_tiles // 12, side_count)
    sender_gap = (my_device - my_slots // slot_count) % device_count
    local_rows = jnp.asarray(position)[sender_gap] * slot_count + my_slots % slot_count

    def laplace(values):
        border = edge_lines(values, tile_side).reshape(slot_count, 4, group_channels * tile_side)
        received = [border]
        for offset_value in distinct:
            received.append(from_behind(border, "tile", offset_value))
        stacked = jnp.concatenate(received, axis=0)
        stacked = stacked.reshape(stacked.shape[0], 4, group_channels, tile_side)
        rows = []
        for slot in range(slot_count):
            for side in range(4):
                start = (local_rows[slot, side], my_edges[slot, side], 0, 0)
                rows.append(
                    lax.dynamic_slice(stacked, start, (1, 1, group_channels, tile_side))
                )
        ghosts = jnp.concatenate(rows, axis=0)
        ghosts = ghosts.reshape(slot_count, 4, group_channels, tile_side)
        return stencil(values, ghosts, tile_side)

    whole_grad = lax.all_gather(out_grad, "sub", axis=1, tiled=True)
    cotangent = whole_grad.astype(jnp.float32)
    inputs = features.astype(jnp.float32)
    previous, current = (inputs, laplace(inputs))
    filter_terms = [
        jnp.einsum("sip,sop->io", inputs, cotangent, precision=highest),
        jnp.einsum("sip,sop->io", current, cotangent, precision=highest),
    ]
    for degree in range(2, K):
        previous, current = (current, 2.0 * laplace(current) - previous)
        filter_terms.append(jnp.einsum("sip,sop->io", current, cotangent, precision=highest))
    weight_grad = tile_total(jnp.stack(filter_terms)) * scale_factor
    row_block = lax.dynamic_slice_in_dim(weights, channel_start, group_channels, 1)

    def mixed(degree):
        return jnp.einsum("sop,io->sip", cotangent, row_block[degree], precision=highest)

    next_sum = mixed(K - 1)
    after_next = jnp.zeros_like(next_sum)
    for degree in range(K - 2, 0, -1):
        next_sum, after_next = (mixed(degree) + 2.0 * laplace(next_sum) - after_next, next_sum)
    in_grad = (mixed(0) + laplace(next_sum) - after_next).astype(jnp.bfloat16)
    return (in_grad, weight_grad)


DEPTH = K - 1
GHOST_SIDES = (0, 2, 3, 1)
OUTSIDE = 6


def face_graph(tile_side):
    tile_ids = np.arange(12, dtype=np.int64)
    target_list, edge_list = neighbour_codes(tile_ids, 1, 1)
    targets = np.stack(target_list, axis=1)
    edges = np.stack(edge_list, axis=1)
    pixels = tile_side * tile_side
    grid = np.arange(pixels).reshape(tile_side, tile_side)
    lines = [grid[0], grid[-1], grid[:, 0], grid[:, -1]]
    ghosts = np.zeros((12, 4, tile_side), dtype=np.int64)
    around = np.zeros((12, 4, tile_side, tile_side), dtype=np.int64)
    for tile in range(12):
        for side in range(4):
            ghosts[tile, side] = targets[tile, side] * pixels + lines[edges[tile, side]]
        whole = tile * pixels + grid
        around[tile, 0] = np.concatenate([ghosts[tile, 0][None], whole[:-1]], 0)
        around[tile, 1] = np.concatenate([whole[1:], ghosts[tile, 1][None]], 0)
        around[tile, 2] = np.concatenate([ghosts[tile, 2][:, None], whole[:, :-1]], 1)
        around[tile, 3] = np.concatenate([whole[:, 1:], ghosts[tile, 3][:, None]], 1)
    around = around.transpose(0, 2, 3, 1).reshape(12 * pixels, 4)
    return targets, edges, ghosts, around


@functools.lru_cache(None)
def ghost_tables(tile_side, slots, tiles_n):
    targets, edges, ghosts, around = face_graph(tile_side)
    pixels = tile_side * tile_side
    grid = np.arange(pixels).reshape(tile_side, tile_side)
    strips = np.stack(
        [
            grid[:DEPTH].ravel(),
            grid[-DEPTH:].ravel(),
            grid[:, :DEPTH].T.ravel(),
            grid[:, -DEPTH:].T.ravel(),
        ]
    )
    sources_of = []
    by_class = []
    for tile in range(12):
        wanted = np.concatenate([ghosts[tile, side] for side in GHOST_SIDES])
        power = np.zeros((wanted.size, 12 * pixels), dtype=np.int32)
        power[np.arange(wanted.size), wanted] = 1
        powers = [power]
        for _ in range(DEPTH - 1):
            powers.append(sum(powers[-1][:, around[:, side]] for side in range(4)))
        rows = np.concatenate(
            [powers[0], powers[1], powers[2] - 8 * powers[0], powers[3] - 12 * powers[1]]
        )
        support = np.flatnonzero(np.any(rows != 0, axis=0))
        sources = [(int(targets[tile, side]), int(edges[tile, side])) for side in range(4)]
        own = [(tile, side) for side in range(4)]
        covered = set(int(t) * pixels + int(p) for t, e in sources + own for p in strips[e])
        left = [int(p) for p in support if int(p) not in covered]
        corner_tiles = {}
        for pixel in left:
            corner_tiles.setdefault(pixel // pixels, []).append(pixel % pixels)
        first = lambda t: int(
            np.flatnonzero(np.any(rows[:, [t * pixels + p for p in corner_tiles[t]]] != 0, axis=1))[0]
        )
        for other in sorted(corner_tiles, key=first):
            choice = [e for e in range(4) if set(corner_tiles[other]) <= set(strips[e].tolist())]
            sources.append((other, choice[0]))
        assert len(sources) <= OUTSIDE
        while len(sources) < OUTSIDE:
            sources.append(sources[-1])
        sources_of.append(sources)
        lanes = np.concatenate([t * pixels + strips[e] for t, e in sources + own])
        seen, keep = set(), np.zeros(lanes.size, dtype=bool)
        for lane, pixel in enumerate(lanes.tolist()):
            keep[lane] = pixel not in seen
            seen.add(pixel)
        assert set(support.tolist()) <= seen
        matrix = (rows[:, lanes] * keep[None]).T
        assert np.abs(matrix).max() <= 127
        if tile % 4 == 0:
            by_class.append(matrix)
        else:
            assert np.array_equal(matrix, by_class[-1])
    wanted = {}
    for tile in range(12):
        for t, e in sources_of[tile]:
            pair = (t // slots, tile // slots)
            if pair[0] != pair[1]:
                held = wanted.setdefault(pair, [])
                if (t, e) not in held:
                    held.append((t, e))
    packed = max(len(held) for held in wanted.values())
    send = np.zeros((tiles_n, tiles_n, packed), dtype=np.int32)
    for (q, p), held in wanted.items():
        for order, (t, e) in enumerate(held):
            send[q, p, order] = (t - q * slots) * 4 + e
    take_from = np.zeros((12, OUTSIDE), dtype=np.int32)
    for tile in range(12):
        for order, (t, e) in enumerate(sources_of[tile]):
            q, p = t // slots, tile // slots
            if q == p:
                take_from[tile, order] = (t - q * slots) * 4 + e
            else:
                at = wanted[(q, p)].index((t, e))
                take_from[tile, order] = slots * 4 + q * packed + at
    table = np.concatenate([take_from.ravel(), send.ravel()])
    counts = tuple(len(wanted.get((q, 0), ())) for q in range(tiles_n))
    far = []
    for tile in range(slots):
        for order, (t, e) in enumerate(sources_of[tile]):
            if t // slots == tiles_n - 1 and (t, e) not in sources_of[tile][:order]:
                far.append((tile, order, int(take_from[tile, order])))
    spread = np.zeros((4, tile_side, tile_side, tile_side))
    step = np.arange(tile_side)
    spread[0, step, 0, step] = 1
    spread[1, step, step, 0] = 1
    spread[2, step, step, -1] = 1
    spread[3, step, -1, step] = 1
    local = np.zeros((pixels, pixels))
    for u in range(tile_side):
        for v in range(tile_side):
            for du, dv in ((1, 0), (-1, 0), (0, 1), (0, -1)):
                if 0 <= u + du < tile_side and 0 <= v + dv < tile_side:
                    local[grid[u, v], grid[u + du, v + dv]] = -0.25
    inward = [-0.25 * spread.reshape(4 * tile_side, pixels)]
    inward.append(2.0 * inward[0] @ local)
    for _ in range(DEPTH - 2):
        inward.append(2.0 * inward[-1] @ local - inward[-2])
    inward = np.concatenate(inward)
    assert np.array_equal(inward, inward.astype(jnp.bfloat16).astype(np.float64))
    take = np.zeros((pixels, 2 * DEPTH * tile_side), dtype=np.float32)
    take[np.concatenate([strips[2], strips[3]]), np.arange(2 * DEPTH * tile_side)] = 1
    return np.stack(by_class), table, (packed, counts, len(wanted.get((0, tiles_n - 1), ())), tuple(far)), inward, take


def split(value):
    high = value.astype(jnp.bfloat16).astype(jnp.float32)
    return high, value - high


def product(left, right):
    return lax.dot_general(
        left, right, (((1,), (1,)), ((), ())), preferred_element_type=jnp.float32
    )


def face_kernel(
    sizes,
    x_hbm,
    g_hbm,
    f_hbm,
    map_hbm,
    table_hbm,
    ghost_hbm,
    inward_hbm,
    take_hbm,
    in_ref,
    w_ref,
    xg_ref,
    g_all,
    x_mine,
    g_mine,
    x_pack,
    g_pack,
    x_ext,
    g_ext,
    block,
    block_in,
    result,
    ghost,
    inward,
    take,
    f_ref,
    map_ref,
    table_ref,
    ready,
    load_sem,
    x_send,
    x_recv,
    s_send,
    s_recv,
    g_send,
    g_recv,
    d_send,
    d_recv,
    f_send,
    f_recv,
    w_send,
    w_recv,
):
    slots, tiles_n, subs, side, (packed, counts, far_count, far), scale = sizes
    x_ref, g_ref = xg_ref.at[0], xg_ref.at[1]
    chans = x_ref.shape[1]
    total = subs * chans
    pixels = side * side
    width = DEPTH * side
    rows = slots * chans
    bf16, f32 = jnp.bfloat16, jnp.float32
    j = lax.axis_index("tile")
    s = lax.axis_index("sub")
    tile_peers = []
    for d in range(tiles_n - 1):
        up = d + (j <= d).astype(jnp.int32)
        back = tiles_n - 2 - d
        down = back + (j <= back).astype(jnp.int32)
        tile_peers.append(jnp.where(2 * j < tiles_n, down, up))
    sub_peers = [lax.rem(s + d, subs) for d in range(1, subs)]
    friends = len(tile_peers) + len(sub_peers)
    head = j == 0
    tail = j == tiles_n - 1
    kinds = [(slots * j + m) // 4 for m in range(slots)]

    def greet(friend):
        pl.semaphore_signal(
            pltpu.get_barrier_semaphore(),
            inc=1,
            device_id=friend,
            device_id_type=pl.DeviceIdType.MESH,
        )

    first_loads = [
        pltpu.make_async_copy(x_hbm, x_ref, load_sem.at[0]),
        pltpu.make_async_copy(g_hbm, g_ref, load_sem.at[0]),
        pltpu.make_async_copy(take_hbm, take, load_sem.at[1]),
        pltpu.make_async_copy(map_hbm, map_ref, load_sem.at[2]),
        pltpu.make_async_copy(table_hbm, table_ref, load_sem.at[3]),
    ]
    barrier = pltpu.get_barrier_semaphore()
    for d, peer in enumerate(tile_peers):

        @pl.when(jnp.logical_not(tail & (peer == 0)))
        def _():
            greet({"tile": peer})

    for peer in sub_peers:
        greet({"sub": peer})
    for copy in first_loads:
        copy.start()

    @pl.when(head)
    def _():
        for peer in tile_peers:
            for other in sub_peers:
                greet({"tile": peer, "sub": other})

    def remote(source, target, send, recv, device):
        return pltpu.make_async_remote_copy(
            source,
            target,
            send,
            recv,
            device_id=device,
            device_id_type=pl.DeviceIdType.MESH,
        )

    def g_copy(d, sender, peer):
        return remote(g_hbm, g_all.at[sender], g_send, g_recv, {"sub": peer})

    def open_up():
        pl.semaphore_wait(barrier, friends + jnp.where(head, -1, subs - 1))
        for d, peer in enumerate(sub_peers):
            g_copy(d, s, peer).start()

    @pl.when(tail)
    def _():
        open_up()
        for other in [s] + sub_peers:
            pl.semaphore_signal(
                ready,
                inc=1,
                device_id={"tile": 0, "sub": other},
                device_id_type=pl.DeviceIdType.MESH,
            )

    loads = [
        pltpu.make_async_copy(ghost_hbm.at[kinds[0]], ghost.at[0], load_sem.at[4]),
        pltpu.make_async_copy(ghost_hbm.at[kinds[-1]], ghost.at[1], load_sem.at[4]),
        pltpu.make_async_copy(inward_hbm, inward, load_sem.at[5]),
        pltpu.make_async_copy(f_hbm, f_ref, load_sem.at[6]),
        pltpu.make_async_copy(g_hbm, g_all.at[s], load_sem.at[7]),
    ]
    for copy in loads:
        copy.start()
    base = slots * j
    pltpu.make_async_copy(xg_ref, xg_ref, load_sem.at[0]).wait()
    for copy in first_loads[2:]:
        copy.wait()

    def slot_of(m):
        found = 0
        for slot in range(1, slots):
            found = jnp.where(map_ref[base + slot] == base + m, slot, found)
        return found

    slot_list = [slot_of(m) for m in range(slots)]
    x_own = jnp.concatenate([x_ref[slot_list[m]].astype(f32) for m in range(slots)], axis=0)
    g_own = jnp.concatenate([g_ref[slot_list[m]].astype(f32) for m in range(slots)], axis=0)
    both = jnp.concatenate([x_own, g_own], axis=0).astype(bf16)
    cut = jnp.dot(both, take[...], preferred_element_type=f32)

    def strips_of(value, cut_value):
        return [
            value[:, :width],
            value[:, pixels - width :],
            cut_value[:, :width],
            cut_value[:, width:],
        ]

    x_strips = strips_of(x_own, cut[:rows])
    g_strips = strips_of(g_own, cut[rows:])
    for m in range(slots):
        at = slice(m * chans, (m + 1) * chans)
        for e in range(4):
            x_mine[m * 4 + e] = x_strips[e][at].astype(bf16)
            g_mine[m * 4 + e] = g_strips[e][at].astype(bf16)
    sends = 12 * OUTSIDE
    for d, peer in enumerate(tile_peers):
        for i in range(packed):
            index = table_ref[sends + (j * tiles_n + peer) * packed + i]
            x_pack[d, i] = x_mine[index]
            g_pack[d, i] = g_mine[index]
    for m in range(slots):
        at = slice(m * chans, (m + 1) * chans)
        for e in range(4):
            x_ext[m * 4 + e] = x_strips[e][at].astype(bf16)

    def landing(sender):
        return pl.ds(slots * 4 + sender * packed, packed)

    def x_copy(d, sender, peer):
        return remote(
            x_pack.at[d], x_ext.at[landing(sender)], x_send, x_recv, {"tile": peer}
        )

    def strip_copy(d, sender, peer):
        return remote(
            g_pack.at[d],
            g_ext.at[s, landing(sender)],
            s_send,
            s_recv,
            {"tile": peer},
        )

    def forward_copy(q, d, sender, peer):
        held = g_ext.at[sender, landing(q)]
        return remote(held, held, f_send, f_recv, {"sub": peer})

    def block_copy(d, sender, peer):
        return remote(block, block_in.at[sender], w_send, w_recv, {"tile": peer})

    pl.when(jnp.logical_not(tail))(open_up)

    def x_crosses(sender, peer):
        return jnp.logical_not((sender == 0) & (peer == tiles_n - 1))

    def direct_copy(q, d, sender, peer):
        at = 0 if 2 * q >= tiles_n else tiles_n - 2
        return remote(
            g_pack.at[at, pl.ds(0, counts[q])],
            g_ext.at[sender, pl.ds(slots * 4 + q * packed, counts[q])],
            d_send,
            d_recv,
            {"tile": 0, "sub": peer},
        )

    for d, peer in enumerate(tile_peers):
        pl.when(x_crosses(j, peer))(x_copy(d, j, peer).start)

    def far_copy(peer):
        return remote(
            g_pack.at[0, pl.ds(0, far_count)],
            g_ext.at[s, pl.ds(slots * 4, far_count)],
            d_send,
            d_recv,
            {"tile": tiles_n - 1, "sub": peer},
        )

    def await_bytes(held, semaphore):
        pltpu.make_async_copy(held, held, semaphore).wait()

    def first_strips(rows_of, count):
        return g_ext.at[pl.ds(0, rows_of), pl.ds(0, count)]

    def for_direct(action):
        for q in range(1, tiles_n):

            @pl.when(j == q)
            def _():
                for d, peer in enumerate([s] + sub_peers):
                    action(direct_copy(q, d, s, peer))

    for_direct(lambda copy: copy.start())
    for d, peer in enumerate(tile_peers):
        pl.when((peer != 0) & x_crosses(j, peer))(strip_copy(d, j, peer).start)

    @pl.when(tail)
    def _():
        x_ext[landing(0)] = jnp.zeros((packed, chans, width), bf16)


    lane = lax.broadcasted_iota(jnp.int32, (rows, pixels), 1)
    y_at = lane % side

    def around(value):
        out = jnp.where(lane < side, 0.0, pltpu.roll(value, side, 1))
        out = out + jnp.where(lane >= pixels - side, 0.0, pltpu.roll(value, pixels - side, 1))
        out = out + jnp.where(y_at == 0, 0.0, pltpu.roll(value, 1, 1))
        return out + jnp.where(y_at == side - 1, 0.0, pltpu.roll(value, pixels - 1, 1))

    def of_slot(value, m, count):
        return value[m * count : (m + 1) * count]

    previous, current = x_own, -0.25 * around(x_own)
    held = [previous]
    for k in range(1, K):
        held += list(split(current))
        if k < K - 1:
            previous, current = current, -0.5 * around(current) - previous
    terms = [
        jnp.concatenate([of_slot(value, m, chans) for value in held], axis=0).astype(bf16)
        for m in range(slots)
    ]

    pltpu.make_async_copy(ghost, ghost, load_sem.at[4]).wait()
    for copy in loads[2:]:
        copy.wait()
    outer = OUTSIDE * width
    one_kind = kinds[0] == kinds[-1]
    mid_first = [kinds[m] == kinds[0] for m in range(slots)]
    scales = (1.0, -0.5, 0.25, -0.125)

    def ghost_lines(value, at, count, single=False):
        first = jnp.dot(value, ghost[0, at], preferred_element_type=f32)
        if single:
            return [of_slot(first, m, count) for m in range(slots)]
        last = jnp.dot(value, ghost[1, at], preferred_element_type=f32)
        return [
            jnp.where(mid_first[m], of_slot(first, m, count), of_slot(last, m, count))
            for m in range(slots)
        ]

    x_inner = ghost_lines(
        jnp.concatenate(x_strips, axis=1).astype(bf16), slice(outer, outer + 4 * width), chans
    )

    x_edge = product(x_own.astype(bf16), inward[...])
    filters = jnp.concatenate([f_ref[k].astype(f32) for k in range(K)], axis=1).astype(bf16)
    pick_row = lax.broadcasted_iota(jnp.int32, (chans, total), 0) + chans * s
    pick_col = lax.broadcasted_iota(jnp.int32, (chans, total), 1)
    mine = jnp.dot(
        jnp.where(pick_row == pick_col, 1.0, 0.0).astype(bf16),
        filters,
        preferred_element_type=f32,
    )
    mixing = jnp.concatenate(
        [mine[:, k * total : (k + 1) * total] for k in range(K)], axis=0
    ).astype(bf16)
    outside = []
    for m in range(DEPTH):
        pieces = [mine[:, (m + 1) * total :]]
        if m > 0:
            pieces.append(jnp.zeros((chans, m * total), f32))
        outside.append(jnp.concatenate(pieces, axis=1))
    outside = jnp.concatenate(outside, axis=0)
    outside = jnp.concatenate([outside, outside], axis=1).astype(bf16)

    await_bytes(g_all.at[pl.ds(0, subs - 1)], g_recv)

    @pl.when(head)
    def _():
        pl.semaphore_wait(ready, subs)
        for peer in [s] + sub_peers:
            far_copy(peer).start()

    g_full = [
        jnp.concatenate([g_all[e, slot_list[m]].astype(f32) for e in range(subs)], axis=0)
        for m in range(slots)
    ]
    g_bf = [value.astype(bf16) for value in g_full]
    grad = jnp.zeros((terms[0].shape[0], total), f32)
    for m in range(slots):
        grad = grad + product(terms[m], g_bf[m])
    edge = product(jnp.concatenate(g_full, axis=0).astype(bf16), inward[...])
    edge = jnp.concatenate(
        [
            jnp.concatenate(
                [
                    of_slot(edge, m, total)[:, n * width : (n + 1) * width]
                    for n in range(DEPTH)
                ],
                axis=0,
            )
            for m in range(slots)
        ],
        axis=1,
    )
    edge = jnp.concatenate(split(edge), axis=0).astype(bf16)


    @pl.when(tail)
    def _():
        await_bytes(x_ext.at[pl.ds(0, (tiles_n - 2) * packed)], x_recv)

    @pl.when(jnp.logical_not(tail))
    def _():
        await_bytes(x_ext.at[pl.ds(0, (tiles_n - 1) * packed)], x_recv)

    def pass_on():
        @pl.when(tail)
        def _():
            await_bytes(g_ext.at[0, pl.ds(0, (tiles_n - 2) * packed)], s_recv)

        @pl.when(jnp.logical_not(tail))
        def _():
            await_bytes(g_ext.at[0, pl.ds(0, (tiles_n - 1) * packed)], s_recv)

        for q, peer in enumerate(tile_peers):

            @pl.when(x_crosses(peer, j))
            def _():
                for d, other in enumerate(sub_peers):
                    forward_copy(peer, d, s, other).start()

    pl.when((2 * j < tiles_n) & (j != 0))(pass_on)
    wanted = [
        [table_ref[(base + m) * OUTSIDE + r] for r in range(OUTSIDE)] for m in range(slots)
    ]

    def outer_strips(read):
        return jnp.concatenate(
            [
                jnp.concatenate([read(wanted[m][r]).astype(f32) for r in range(OUTSIDE)], axis=1)
                for m in range(slots)
            ],
            axis=0,
        )

    def by_power(lines):
        return jnp.concatenate(
            [
                lines[:, n * width : (n + 1) * width] * scales[n] for n in range(DEPTH)
            ],
            axis=0,
        )

    half = DEPTH * chans

    def by_degree(across):
        across = across[:half] + across[half:]
        across = across[:, : DEPTH * total] + across[:, DEPTH * total :]
        place = lax.broadcasted_iota(jnp.int32, (chans, DEPTH * total), 1)
        out = of_slot(across, 0, chans)
        for n in range(1, DEPTH):
            shifted = pltpu.roll(of_slot(across, n, chans), n * total, 1)
            out = out + jnp.where(place < n * total, 0.0, shifted)
        return out

    def sum_weights(single):
        x_lines = ghost_lines(
            outer_strips(lambda index: x_ext[index]).astype(bf16), slice(0, outer), chans, single
        )
        x_lines = jnp.concatenate(
            [by_power(x_lines[m] + x_inner[m]) for m in range(slots)], axis=1
        )
        across = product(jnp.concatenate(split(x_lines), axis=0).astype(bf16), edge)
        later = [
            of_slot(grad, 2 * k - 1, chans) + of_slot(grad, 2 * k, chans) for k in range(1, K)
        ]
        later = (jnp.concatenate(later, axis=1) + by_degree(across)) * scale
        block[0] = later
        block[1] = jnp.concatenate(
            [grad[:chans] * scale, jnp.zeros((chans, width - total), f32)], axis=1
        )

    pl.when(one_kind)(functools.partial(sum_weights, True))
    pl.when(jnp.logical_not(one_kind))(functools.partial(sum_weights, False))

    def send_blocks():
        for d, peer in enumerate(tile_peers):
            block_copy(d, j, peer).start()

    pl.when(j != 0)(send_blocks)
    pl.when(2 * j >= tiles_n)(pass_on)

    def finish(single):
        mixed = [jnp.dot(mixing, g_bf[m], preferred_element_type=f32) for m in range(slots)]
        grads = [
            jnp.concatenate([of_slot(mixed[m], k, chans) for m in range(slots)], axis=0)
            for k in range(K)
        ]
        after, upper = grads[K - 1], grads[K - 2] - 0.5 * around(grads[K - 1])
        for k in range(K - 3, 0, -1):
            after, upper = upper, grads[k] - 0.5 * around(upper) - after
        inner = grads[0] - 0.25 * around(upper) - after

        whole = jnp.concatenate(g_full, axis=0)
        whole_strips = strips_of(
            whole, jnp.dot(whole.astype(bf16), take[...], preferred_element_type=f32)
        )
        for m in range(slots):
            for e in range(subs):
                at = slice(m * total + e * chans, m * total + (e + 1) * chans)
                for side_at in range(4):
                    g_ext[e, m * 4 + side_at] = whole_strips[side_at][at].astype(bf16)
        g_inner = ghost_lines(
            jnp.concatenate(whole_strips, axis=1).astype(bf16),
            slice(outer, outer + 4 * width),
            total,
            single,
        )

        if single:

            @pl.when(tail)
            def _():
                await_bytes(first_strips(subs, far_count), d_recv)
                await_bytes(first_strips(subs - 1, (tiles_n - 2) * packed), f_recv)

        @pl.when((j != 0) & jnp.logical_not(tail))
        def _():
            await_bytes(first_strips(subs - 1, (tiles_n - 1) * packed), f_recv)

        @pl.when(head)
        def _():
            await_bytes(first_strips(subs, sum(counts[1:])), d_recv)

        if single and far:
            far_lines, far_edge = [], []
            for m, r, index in far:
                held = jnp.concatenate(
                    [g_ext[e, index].astype(f32) for e in range(subs)], axis=0
                ).astype(bf16)
                rows_at = ghost[m // 4, r * width : (r + 1) * width]
                far_lines.append(by_power(jnp.dot(held, rows_at, preferred_element_type=f32)))
                mine_edge = of_slot(x_edge, m, chans)
                far_edge.append(
                    jnp.concatenate(
                        [mine_edge[:, n * width : (n + 1) * width] for n in range(DEPTH)], axis=0
                    )
                )
            far_lines = jnp.concatenate(split(jnp.concatenate(far_lines, axis=1)), axis=0)
            far_edge = jnp.concatenate(split(jnp.concatenate(far_edge, axis=1)), axis=0)
            crossed = by_degree(product(far_edge.astype(bf16), far_lines.astype(bf16)))
        if single:

            @pl.when(head)
            def _():
                if far:
                    block[0] = block[0] + crossed * scale
                send_blocks()

        gathered = outer_strips(
            lambda index: jnp.concatenate([g_ext[e, index].astype(f32) for e in range(subs)], axis=0)
        )
        g_lines = ghost_lines(gathered.astype(bf16), slice(0, outer), total, single)
        g_lines = jnp.concatenate(
            [by_power(g_lines[m] + g_inner[m]) for m in range(slots)], axis=1
        )
        mixed = jnp.dot(
            outside,
            jnp.concatenate(split(g_lines), axis=0).astype(bf16),
            preferred_element_type=f32,
        )
        mixed = jnp.concatenate(
            [
                jnp.concatenate(
                    [
                        of_slot(mixed, n, chans)[:, m * width : (m + 1) * width]
                        for n in range(DEPTH)
                    ],
                    axis=1,
                )
                for m in range(slots)
            ],
            axis=0,
        )
        spread = jnp.dot(
            jnp.concatenate(split(mixed), axis=0).astype(bf16),
            inward[...],
            preferred_element_type=f32,
        )
        inner = inner + spread[:rows] + spread[rows:]
        for m in range(slots):
            result[m] = of_slot(inner, m, chans)
        for slot in range(slots):
            in_ref[slot] = result[lax.rem(map_ref[base + slot], slots)].astype(bf16)
    pl.when(one_kind)(functools.partial(finish, True))
    pl.when(jnp.logical_not(one_kind))(functools.partial(finish, False))

    await_bytes(block_in.at[pl.ds(0, tiles_n - 1)], w_recv)
    block_in[j] = block[...]
    summed = block_in[0]
    for q in range(1, tiles_n):
        summed = summed + block_in[q]
    w_ref[0] = summed[1, :, :total]
    for k in range(1, K):
        w_ref[k] = summed[0, :, (k - 1) * total : k * total]

    await_bytes(block_in.at[pl.ds(0, tiles_n - 1)], w_send)
    await_bytes(g_all.at[pl.ds(0, subs - 1)], g_send)
    await_bytes(g_pack.at[pl.ds(0, tiles_n - 2)], s_send)

    @pl.when(head)
    def _():
        await_bytes(x_pack.at[pl.ds(0, tiles_n - 2)], x_send)
        await_bytes(first_strips(subs, far_count), d_send)

    @pl.when(j != 0)
    def _():
        await_bytes(x_pack, x_send)

    for q in range(1, tiles_n):

        @pl.when(j == q)
        def _():
            await_bytes(first_strips(subs, counts[q]), d_send)
            moved = tiles_n - 2 if q == tiles_n - 1 else tiles_n - 1
            await_bytes(first_strips(subs - 1, moved * packed), f_send)


def store_kernel(in_vmem, w_vmem, in_hbm, w_hbm, sem):
    copies = [
        pltpu.make_async_copy(in_vmem, in_hbm, sem.at[0]),
        pltpu.make_async_copy(w_vmem, w_hbm, sem.at[1]),
    ]
    for copy in copies:
        copy.start()
    for copy in copies:
        copy.wait()


def face_path(features, out_grad, filters, tile_map):
    slots, chans, pixels = features.shape
    side = math.isqrt(pixels)
    tiles_n, subs = lax.axis_size("tile"), lax.axis_size("sub")
    matrices, table, links, inward, take = ghost_tables(side, slots, tiles_n)
    scale = 1.0 / math.sqrt(slots * tiles_n * pixels)
    width = DEPTH * side
    vmem = pl.BlockSpec(memory_space=pltpu.VMEM)
    hbm = pl.BlockSpec(memory_space=pltpu.HBM)
    dma = pltpu.SemaphoreType.DMA
    bf16, f32 = jnp.bfloat16, jnp.float32
    held = slots * 4 + tiles_n * links[0]
    held_outs = pl.pallas_call(
        functools.partial(face_kernel, (slots, tiles_n, subs, side, links, scale)),
        out_shape=(
            pltpu.VMEM(features.shape, bf16),
            pltpu.VMEM((K, chans, filters.shape[2]), f32),
        ),
        in_specs=[hbm] * 8,
        out_specs=(vmem, vmem),
        scratch_shapes=[
            pltpu.VMEM((2,) + features.shape, bf16),
            pltpu.VMEM((subs,) + features.shape, bf16),
            pltpu.VMEM((slots * 4, chans, width), bf16),
            pltpu.VMEM((slots * 4, chans, width), bf16),
            pltpu.VMEM((tiles_n - 1, links[0], chans, width), bf16),
            pltpu.VMEM((tiles_n - 1, links[0], chans, width), bf16),
            pltpu.VMEM((held, chans, width), bf16),
            pltpu.VMEM((subs, held, chans, width), bf16),
            pltpu.VMEM((2, chans, width), f32),
            pltpu.VMEM((tiles_n, 2, chans, width), f32),
            pltpu.VMEM((slots, chans, pixels), f32),
            pltpu.VMEM((2,) + matrices.shape[1:], bf16),
            pltpu.VMEM(inward.shape, bf16),
            pltpu.VMEM(take.shape, bf16),
            pltpu.VMEM(filters.shape, bf16),
            pltpu.SMEM(tile_map.shape, jnp.int32),
            pltpu.SMEM(table.shape, jnp.int32),
            pltpu.SemaphoreType.REGULAR,
            dma((8,)),
        ]
        + [dma] * 12,
        compiler_params=pltpu.CompilerParams(
            collective_id=0, has_side_effects=True, vmem_limit_bytes=67043328 - 512 * 1024
        ),
    )(
        features,
        out_grad,
        filters,
        tile_map,
        jnp.asarray(table),
        jnp.asarray(matrices, bf16),
        jnp.asarray(inward, bf16),
        jnp.asarray(take, bf16),
    )
    held_outs = [pltpu.with_memory_space_constraint(value, pltpu.VMEM) for value in held_outs]
    return pl.pallas_call(
        store_kernel,
        out_shape=(
            jax.ShapeDtypeStruct(features.shape, bf16),
            jax.ShapeDtypeStruct((K, chans, filters.shape[2]), f32),
        ),
        in_specs=[vmem] * 2,
        out_specs=(hbm, hbm),
        scratch_shapes=[dma((2,))],
    )(*held_outs)


def on_device(features, out_grad, filters, tile_map):
    slots, chans, pixels = features.shape
    side = math.isqrt(pixels)
    whole_faces = slots * lax.axis_size("tile") == 12
    channels = chans * lax.axis_size("sub")
    if whole_faces and 1 < slots < 5 and DEPTH * side == 128 and chans % 8 == 0 and channels == 32:
        return face_path(features, out_grad, filters, tile_map)
    return general_path(features, out_grad, filters, tile_map)


def solution(mesh):
    placed = (P(("grp", "tile"), "sub", None), P(("grp", "tile"), "sub", None), P(), P())
    return jax.shard_map(
        on_device,
        mesh=mesh,
        in_specs=placed,
        out_specs=(P(("grp", "tile"), "sub", None), P("grp", "sub", None)),
        check_vma=False,
    )
```

```python
import functools
import math

import jax
import jax.numpy as jnp
import numpy as np
from jax import lax
from jax.experimental import pallas as pl
from jax.experimental.pallas import tpu as pltpu
from jax.sharding import PartitionSpec as P

K = 5


def from_behind(value, axis, steps):
    count = lax.axis_size(axis)
    pairs = [(source, (source + steps) % count) for source in range(count)]
    return lax.ppermute(value, axis, pairs)


def tile_coords(nested_code, bit_count):
    coord_x = nested_code * 0
    coord_y = nested_code * 0
    for bit_level in range(bit_count):
        coord_x = coord_x + nested_code // 4**bit_level % 2 * 2**bit_level
        coord_y = coord_y + nested_code // (2 * 4**bit_level) % 2 * 2**bit_level
    return (coord_x, coord_y)


def nested_index(coord_x, coord_y, bit_count):
    nested_code = coord_x * 0
    for bit_level in range(bit_count):
        nested_code = nested_code + coord_x // 2**bit_level % 2 * 4**bit_level
        nested_code = nested_code + coord_y // 2**bit_level % 2 * (2 * 4**bit_level)
    return nested_code


def pick(condition, when_true, when_false):
    return when_false + (when_true - when_false) * condition


def neighbour_codes(tile_ids, per_face, side_count):
    bit_count = side_count.bit_length() - 1
    face_id = tile_ids // per_face
    coord_x, coord_y = tile_coords(tile_ids % per_face, bit_count)
    column = face_id % 4
    is_north = face_id < 4
    is_south = face_id >= 8
    last_tile = side_count - 1

    def by_cycle(north_value, equator_value, south_value):
        return pick(is_north, north_value, pick(is_south, south_value, equator_value))

    side_rules = [
        (
            coord_x > 0,
            (face_id, coord_x - 1, coord_y, 1),
            (
                by_cycle(4 + column, 8 + (column + 3) % 4, 8 + (column + 3) % 4),
                by_cycle(last_tile, last_tile, coord_y),
                by_cycle(coord_y, coord_y, 0),
                by_cycle(1, 1, 2),
            ),
        ),
        (
            coord_x < last_tile,
            (face_id, coord_x + 1, coord_y, 0),
            (
                by_cycle((column + 1) % 4, column, 4 + (column + 1) % 4),
                by_cycle(coord_y, 0, 0),
                by_cycle(last_tile, coord_y, coord_y),
                by_cycle(3, 0, 0),
            ),
        ),
        (
            coord_y > 0,
            (face_id, coord_x, coord_y - 1, 3),
            (
                by_cycle(4 + (column + 1) % 4, 8 + column, 8 + (column + 1) % 4),
                by_cycle(coord_x, coord_x, 0),
                by_cycle(last_tile, last_tile, coord_x),
                by_cycle(3, 3, 0),
            ),
        ),
        (
            coord_y < last_tile,
            (face_id, coord_x, coord_y + 1, 2),
            (
                by_cycle((column + 3) % 4, (column + 3) % 4, 4 + column),
                by_cycle(last_tile, coord_x, coord_x),
                by_cycle(coord_x, 0, 0),
                by_cycle(1, 2, 2),
            ),
        ),
    ]
    target_list = []
    edge_list = []
    for inside, within, across in side_rules:
        chosen = [
            pick(inside, near_value, far_value) for near_value, far_value in zip(within, across)
        ]
        target_list.append(chosen[0] * per_face + nested_index(chosen[1], chosen[2], bit_count))
        edge_list.append(chosen[3] + tile_ids * 0)
    return (target_list, edge_list)


def neighbour_table(tile_map, per_face, side_count):
    target_list, edge_list = neighbour_codes(tile_map, per_face, side_count)
    targets = jnp.stack(target_list, axis=1).astype(jnp.int32)
    edges = jnp.stack(edge_list, axis=1).astype(jnp.int32)
    slot_of = jnp.argsort(tile_map).astype(jnp.int32)
    return (slot_of[targets].astype(jnp.int32), edges)


def peer_offsets(slot_count, device_count, per_face, side_count):
    tile_ids = np.arange(slot_count * device_count, dtype=np.int64)
    target_list, edge_list = neighbour_codes(tile_ids, per_face, side_count)
    targets = np.stack(target_list, axis=1)
    offsets = (tile_ids[:, None] // slot_count - targets // slot_count) % device_count
    distinct = sorted(set((int(value) for value in offsets.ravel())) - {0})
    position = np.zeros(device_count, dtype=np.int32)
    for order, value in enumerate(distinct):
        position[value] = order + 1
    return (distinct, position)


def edge_lines(values, tile_side):
    return jnp.stack(
        [
            values[..., :tile_side],
            values[..., -tile_side:],
            values[..., ::tile_side],
            values[..., tile_side - 1 :: tile_side],
        ],
        axis=1,
    )


def stencil(values, ghosts, tile_side):
    position = jnp.arange(values.shape[-1]) % tile_side
    zero_line = jnp.zeros_like(values[..., :1])
    upper_side = jnp.concatenate([ghosts[:, 0], values[..., :-tile_side]], axis=-1)
    lower_side = jnp.concatenate([values[..., tile_side:], ghosts[:, 1]], axis=-1)
    left_side = jnp.where(
        position == 0,
        jnp.repeat(ghosts[:, 2], tile_side, axis=-1),
        jnp.concatenate([zero_line, values[..., :-1]], axis=-1),
    )
    right_side = jnp.where(
        position == tile_side - 1,
        jnp.repeat(ghosts[:, 3], tile_side, axis=-1),
        jnp.concatenate([values[..., 1:], zero_line], axis=-1),
    )
    return -0.25 * (upper_side + lower_side + left_side + right_side)


def tile_total(filter_part):
    return lax.psum(filter_part, "tile")


def general_path(features, out_grad, filters, tile_map):
    slot_count = features.shape[0]
    group_channels = features.shape[1]
    tile_side = math.isqrt(features.shape[2])
    device_count = lax.axis_size("tile")
    total_tiles = slot_count * device_count
    side_count = math.isqrt(total_tiles // 12)
    scale_factor = 1.0 / math.sqrt(total_tiles * features.shape[2])
    highest = lax.Precision.HIGHEST
    slot_table, edge_table = neighbour_table(tile_map, total_tiles // 12, side_count)
    my_device = lax.axis_index("tile")
    first_slot = my_device * slot_count
    my_slots = lax.dynamic_slice_in_dim(slot_table, first_slot, slot_count, 0)
    my_edges = lax.dynamic_slice_in_dim(edge_table, first_slot, slot_count, 0)
    channel_start = lax.axis_index("sub") * group_channels
    weights = filters.astype(jnp.float32)
    distinct, position = peer_offsets(slot_count, device_count, total_tiles // 12, side_count)
    sender_gap = (my_device - my_slots // slot_count) % device_count
    local_rows = jnp.asarray(position)[sender_gap] * slot_count + my_slots % slot_count

    def laplace(values):
        border = edge_lines(values, tile_side).reshape(slot_count, 4, group_channels * tile_side)
        received = [border]
        for offset_value in distinct:
            received.append(from_behind(border, "tile", offset_value))
        stacked = jnp.concatenate(received, axis=0)
        stacked = stacked.reshape(stacked.shape[0], 4, group_channels, tile_side)
        rows = []
        for slot in range(slot_count):
            for side in range(4):
                start = (local_rows[slot, side], my_edges[slot, side], 0, 0)
                rows.append(
                    lax.dynamic_slice(stacked, start, (1, 1, group_channels, tile_side))
                )
        ghosts = jnp.concatenate(rows, axis=0)
        ghosts = ghosts.reshape(slot_count, 4, group_channels, tile_side)
        return stencil(values, ghosts, tile_side)

    whole_grad = lax.all_gather(out_grad, "sub", axis=1, tiled=True)
    cotangent = whole_grad.astype(jnp.float32)
    inputs = features.astype(jnp.float32)
    previous, current = (inputs, laplace(inputs))
    filter_terms = [
        jnp.einsum("sip,sop->io", inputs, cotangent, precision=highest),
        jnp.einsum("sip,sop->io", current, cotangent, precision=highest),
    ]
    for degree in range(2, K):
        previous, current = (current, 2.0 * laplace(current) - previous)
        filter_terms.append(jnp.einsum("sip,sop->io", current, cotangent, precision=highest))
    weight_grad = tile_total(jnp.stack(filter_terms)) * scale_factor
    row_block = lax.dynamic_slice_in_dim(weights, channel_start, group_channels, 1)

    def mixed(degree):
        return jnp.einsum("sop,io->sip", cotangent, row_block[degree], precision=highest)

    next_sum = mixed(K - 1)
    after_next = jnp.zeros_like(next_sum)
    for degree in range(K - 2, 0, -1):
        next_sum, after_next = (mixed(degree) + 2.0 * laplace(next_sum) - after_next, next_sum)
    in_grad = (mixed(0) + laplace(next_sum) - after_next).astype(jnp.bfloat16)
    return (in_grad, weight_grad)


DEPTH = K - 1
GHOST_SIDES = (0, 2, 3, 1)
OUTSIDE = 6


def face_graph(tile_side):
    tile_ids = np.arange(12, dtype=np.int64)
    target_list, edge_list = neighbour_codes(tile_ids, 1, 1)
    targets = np.stack(target_list, axis=1)
    edges = np.stack(edge_list, axis=1)
    pixels = tile_side * tile_side
    grid = np.arange(pixels).reshape(tile_side, tile_side)
    lines = [grid[0], grid[-1], grid[:, 0], grid[:, -1]]
    ghosts = np.zeros((12, 4, tile_side), dtype=np.int64)
    around = np.zeros((12, 4, tile_side, tile_side), dtype=np.int64)
    for tile in range(12):
        for side in range(4):
            ghosts[tile, side] = targets[tile, side] * pixels + lines[edges[tile, side]]
        whole = tile * pixels + grid
        around[tile, 0] = np.concatenate([ghosts[tile, 0][None], whole[:-1]], 0)
        around[tile, 1] = np.concatenate([whole[1:], ghosts[tile, 1][None]], 0)
        around[tile, 2] = np.concatenate([ghosts[tile, 2][:, None], whole[:, :-1]], 1)
        around[tile, 3] = np.concatenate([whole[:, 1:], ghosts[tile, 3][:, None]], 1)
    around = around.transpose(0, 2, 3, 1).reshape(12 * pixels, 4)
    return targets, edges, ghosts, around


@functools.lru_cache(None)
def ghost_tables(tile_side, slots, tiles_n):
    targets, edges, ghosts, around = face_graph(tile_side)
    pixels = tile_side * tile_side
    grid = np.arange(pixels).reshape(tile_side, tile_side)
    strips = np.stack(
        [
            grid[:DEPTH].ravel(),
            grid[-DEPTH:].ravel(),
            grid[:, :DEPTH].T.ravel(),
            grid[:, -DEPTH:].T.ravel(),
        ]
    )
    sources_of = []
    by_class = []
    for tile in range(12):
        wanted = np.concatenate([ghosts[tile, side] for side in GHOST_SIDES])
        power = np.zeros((wanted.size, 12 * pixels), dtype=np.int32)
        power[np.arange(wanted.size), wanted] = 1
        powers = [power]
        for _ in range(DEPTH - 1):
            powers.append(sum(powers[-1][:, around[:, side]] for side in range(4)))
        rows = np.concatenate(
            [powers[0], powers[1], powers[2] - 8 * powers[0], powers[3] - 12 * powers[1]]
        )
        support = np.flatnonzero(np.any(rows != 0, axis=0))
        sources = [(int(targets[tile, side]), int(edges[tile, side])) for side in range(4)]
        own = [(tile, side) for side in range(4)]
        covered = set(int(t) * pixels + int(p) for t, e in sources + own for p in strips[e])
        left = [int(p) for p in support if int(p) not in covered]
        corner_tiles = {}
        for pixel in left:
            corner_tiles.setdefault(pixel // pixels, []).append(pixel % pixels)
        first = lambda t: int(
            np.flatnonzero(np.any(rows[:, [t * pixels + p for p in corner_tiles[t]]] != 0, axis=1))[0]
        )
        for other in sorted(corner_tiles, key=first):
            choice = [e for e in range(4) if set(corner_tiles[other]) <= set(strips[e].tolist())]
            sources.append((other, choice[0]))
        assert len(sources) <= OUTSIDE
        while len(sources) < OUTSIDE:
            sources.append(sources[-1])
        sources_of.append(sources)
        lanes = np.concatenate([t * pixels + strips[e] for t, e in sources + own])
        seen, keep = set(), np.zeros(lanes.size, dtype=bool)
        for lane, pixel in enumerate(lanes.tolist()):
            keep[lane] = pixel not in seen
            seen.add(pixel)
        assert set(support.tolist()) <= seen
        matrix = (rows[:, lanes] * keep[None]).T
        assert np.abs(matrix).max() <= 127
        if tile % 4 == 0:
            by_class.append(matrix)
        else:
            assert np.array_equal(matrix, by_class[-1])
    wanted = {}
    for tile in range(12):
        for t, e in sources_of[tile]:
            pair = (t // slots, tile // slots)
            if pair[0] != pair[1]:
                held = wanted.setdefault(pair, [])
                if (t, e) not in held:
                    held.append((t, e))
    packed = max(len(held) for held in wanted.values())
    send = np.zeros((tiles_n, tiles_n, packed), dtype=np.int32)
    for (q, p), held in wanted.items():
        for order, (t, e) in enumerate(held):
            send[q, p, order] = (t - q * slots) * 4 + e
    take_from = np.zeros((12, OUTSIDE), dtype=np.int32)
    for tile in range(12):
        for order, (t, e) in enumerate(sources_of[tile]):
            q, p = t // slots, tile // slots
            if q == p:
                take_from[tile, order] = (t - q * slots) * 4 + e
            else:
                at = wanted[(q, p)].index((t, e))
                take_from[tile, order] = slots * 4 + q * packed + at
    table = np.concatenate([take_from.ravel(), send.ravel()])
    counts = tuple(len(wanted.get((q, 0), ())) for q in range(tiles_n))
    far = []
    for tile in range(slots):
        for order, (t, e) in enumerate(sources_of[tile]):
            if t // slots == tiles_n - 1 and (t, e) not in sources_of[tile][:order]:
                far.append((tile, order, int(take_from[tile, order])))
    spread = np.zeros((4, tile_side, tile_side, tile_side))
    step = np.arange(tile_side)
    spread[0, step, 0, step] = 1
    spread[1, step, step, 0] = 1
    spread[2, step, step, -1] = 1
    spread[3, step, -1, step] = 1
    local = np.zeros((pixels, pixels))
    for u in range(tile_side):
        for v in range(tile_side):
            for du, dv in ((1, 0), (-1, 0), (0, 1), (0, -1)):
                if 0 <= u + du < tile_side and 0 <= v + dv < tile_side:
                    local[grid[u, v], grid[u + du, v + dv]] = -0.25
    inward = [-0.25 * spread.reshape(4 * tile_side, pixels)]
    inward.append(2.0 * inward[0] @ local)
    for _ in range(DEPTH - 2):
        inward.append(2.0 * inward[-1] @ local - inward[-2])
    inward = np.concatenate(inward)
    assert np.array_equal(inward, inward.astype(jnp.bfloat16).astype(np.float64))
    return np.stack(by_class), table, (packed, counts, len(wanted.get((0, tiles_n - 1), ())), tuple(far)), inward


def split(value):
    high = value.astype(jnp.bfloat16).astype(jnp.float32)
    return high, value - high


def product(left, right):
    return lax.dot_general(
        left, right, (((1,), (1,)), ((), ())), preferred_element_type=jnp.float32
    )


def face_kernel(
    sizes,
    x_hbm,
    g_hbm,
    f_hbm,
    map_hbm,
    table_hbm,
    ghost_hbm,
    inward_hbm,
    in_ref,
    w_ref,
    xg_ref,
    g_all,
    x_mine,
    g_mine,
    x_pack,
    g_pack,
    x_ext,
    g_ext,
    block,
    block_in,
    result,
    g_lines_own,
    ghost,
    inward,
    take,
    f_ref,
    map_ref,
    table_ref,
    ready,
    load_sem,
    x_send,
    x_recv,
    s_send,
    s_recv,
    g_send,
    g_recv,
    d_send,
    d_recv,
    f_send,
    f_recv,
    w_send,
    w_recv,
):
    slots, tiles_n, subs, side, (packed, counts, far_count, far), scale = sizes
    x_ref, g_ref = xg_ref.at[0], xg_ref.at[1]
    chans = x_ref.shape[1]
    total = subs * chans
    pixels = side * side
    width = DEPTH * side
    rows = slots * chans
    bf16, f32 = jnp.bfloat16, jnp.float32
    j = lax.axis_index("tile")
    s = lax.axis_index("sub")
    tile_peers = []
    for d in range(tiles_n - 1):
        up = d + (j <= d).astype(jnp.int32)
        back = tiles_n - 2 - d
        down = back + (j <= back).astype(jnp.int32)
        tile_peers.append(jnp.where(2 * j < tiles_n, down, up))
    core_peer = s + 1 - 2 * lax.rem(s, 2)
    sub_peers = [lax.rem(s + 2, subs), lax.rem(core_peer + 2, subs), core_peer]
    friends = len(tile_peers) + len(sub_peers)
    head = j == 0
    tail = j == tiles_n - 1
    kinds = [(slots * j + m) // 4 for m in range(slots)]

    def greet(friend):
        pl.semaphore_signal(
            pltpu.get_barrier_semaphore(),
            inc=1,
            device_id=friend,
            device_id_type=pl.DeviceIdType.MESH,
        )

    first_loads = [
        pltpu.make_async_copy(x_hbm, x_ref, load_sem.at[0]),
        pltpu.make_async_copy(g_hbm, g_ref, load_sem.at[0]),
        pltpu.make_async_copy(map_hbm, map_ref, load_sem.at[2]),
        pltpu.make_async_copy(table_hbm, table_ref, load_sem.at[3]),
    ]
    barrier = pltpu.get_barrier_semaphore()
    for d, peer in enumerate(tile_peers):

        @pl.when(jnp.logical_not(tail & (peer == 0)))
        def _():
            greet({"tile": peer})

    for peer in sub_peers:
        greet({"sub": peer})
    for copy in first_loads:
        copy.start()

    one_kind = kinds[0] == kinds[-1]
    loads = [
        pltpu.make_async_copy(ghost_hbm.at[kinds[0]], ghost.at[0], load_sem.at[4]),
        pltpu.make_async_copy(inward_hbm, inward, load_sem.at[5]),
        pltpu.make_async_copy(f_hbm, f_ref, load_sem.at[6]),
        pltpu.make_async_copy(g_hbm, g_all.at[s], load_sem.at[7]),
    ]
    second = pltpu.make_async_copy(ghost_hbm.at[kinds[-1]], ghost.at[1], load_sem.at[8])
    for copy in loads:
        copy.start()
    pl.when(jnp.logical_not(one_kind))(second.start)

    @pl.when(head)
    def _():
        for peer in tile_peers:
            for other in sub_peers:
                greet({"tile": peer, "sub": other})

    def remote(source, target, send, recv, device):
        return pltpu.make_async_remote_copy(
            source,
            target,
            send,
            recv,
            device_id=device,
            device_id_type=pl.DeviceIdType.MESH,
        )

    def g_copy(d, sender, peer):
        return remote(g_hbm, g_all.at[sender], g_send, g_recv, {"sub": peer})

    def open_up():
        pl.semaphore_wait(barrier, friends + jnp.where(head, -1, subs - 1))

    base = slots * j
    column = lax.broadcasted_iota(jnp.int32, (pixels, 2 * width), 1)
    wanted_pixel = column % side * side + column % width // side
    wanted_pixel = wanted_pixel + jnp.where(column < width, 0, side - DEPTH)
    pixel = lax.broadcasted_iota(jnp.int32, (pixels, 2 * width), 0)
    take[...] = jnp.where(pixel == wanted_pixel, 1.0, 0.0).astype(bf16)
    pltpu.make_async_copy(xg_ref, xg_ref, load_sem.at[0]).wait()
    for copy in first_loads[2:]:
        copy.wait()

    def slot_of(m):
        found = 0
        for slot in range(1, slots):
            found = jnp.where(map_ref[base + slot] == base + m, slot, found)
        return found

    slot_list = [slot_of(m) for m in range(slots)]
    x_own = jnp.concatenate([x_ref[slot_list[m]].astype(f32) for m in range(slots)], axis=0)
    g_own = jnp.concatenate([g_ref[slot_list[m]].astype(f32) for m in range(slots)], axis=0)
    both = jnp.concatenate([x_own, g_own], axis=0).astype(bf16)
    cut = jnp.dot(both, take[...], preferred_element_type=f32)

    def strips_of(value, cut_value):
        return [
            value[:, :width],
            value[:, pixels - width :],
            cut_value[:, :width],
            cut_value[:, width:],
        ]

    x_strips = strips_of(x_own, cut[:rows])
    g_strips = strips_of(g_own, cut[rows:])
    for m in range(slots):
        at = slice(m * chans, (m + 1) * chans)
        for e in range(4):
            x_mine[m * 4 + e] = x_strips[e][at].astype(bf16)
            g_mine[m * 4 + e] = g_strips[e][at].astype(bf16)
    sends = 12 * OUTSIDE
    for d, peer in enumerate(tile_peers):
        for i in range(packed):
            index = table_ref[sends + (j * tiles_n + peer) * packed + i]
            x_pack[d, i] = x_mine[index]
            g_pack[d, i] = g_mine[index]
    for m in range(slots):
        at = slice(m * chans, (m + 1) * chans)
        for e in range(4):
            x_ext[m * 4 + e] = x_strips[e][at].astype(bf16)

    def landing(sender):
        return pl.ds(slots * 4 + sender * packed, packed)

    def x_copy(d, sender, peer):
        return remote(
            x_pack.at[d], x_ext.at[landing(sender)], x_send, x_recv, {"tile": peer}
        )

    def strip_copy(d, sender, peer):
        return remote(
            g_pack.at[d],
            g_ext.at[s, landing(sender)],
            s_send,
            s_recv,
            {"tile": peer},
        )

    def forward_copy(q, d, sender, peer):
        held = g_ext.at[sender, landing(q)]
        return remote(held, held, f_send, f_recv, {"sub": peer})

    def block_copy(d, sender, peer):
        return remote(block, block_in.at[sender], w_send, w_recv, {"tile": peer})

    def x_crosses(sender, peer):
        return jnp.logical_not((sender == 0) & (peer == tiles_n - 1))

    def direct_copy(q, d, sender, peer):
        at = 0 if 2 * q >= tiles_n else tiles_n - 2
        return remote(
            g_pack.at[at, pl.ds(0, counts[q])],
            g_ext.at[sender, pl.ds(slots * 4 + q * packed, counts[q])],
            d_send,
            d_recv,
            {"tile": 0, "sub": peer},
        )

    def far_copy(peer):
        return remote(
            g_pack.at[0, pl.ds(0, far_count)],
            g_ext.at[s, pl.ds(slots * 4, far_count)],
            d_send,
            d_recv,
            {"tile": tiles_n - 1, "sub": peer},
        )

    def await_bytes(held, semaphore):
        pltpu.make_async_copy(held, held, semaphore).wait()

    def first_strips(rows_of, count):
        return g_ext.at[pl.ds(0, rows_of), pl.ds(0, count)]

    def for_direct(action):
        for q in range(1, tiles_n):

            @pl.when(j == q)
            def _():
                for d, peer in enumerate([s] + sub_peers):
                    action(direct_copy(q, d, s, peer))

    def send_strips():
        for_direct(lambda copy: copy.start())
        for d, peer in enumerate(tile_peers):
            pl.when((peer != 0) & x_crosses(j, peer))(strip_copy(d, j, peer).start)

    @pl.when(tail)
    def _():
        x_ext[landing(0)] = jnp.zeros((packed, chans, width), bf16)


    lane = lax.broadcasted_iota(jnp.int32, (rows, pixels), 1)
    y_at = lane % side

    def around(value):
        out = jnp.where(lane < side, 0.0, pltpu.roll(value, side, 1))
        out = out + jnp.where(lane >= pixels - side, 0.0, pltpu.roll(value, pixels - side, 1))
        out = out + jnp.where(y_at == 0, 0.0, pltpu.roll(value, 1, 1))
        return out + jnp.where(y_at == side - 1, 0.0, pltpu.roll(value, pixels - 1, 1))

    def of_slot(value, m, count):
        return value[m * count : (m + 1) * count]

    open_up()
    for d, peer in enumerate(tile_peers):
        pl.when(x_crosses(j, peer))(x_copy(d, j, peer).start)
    for d, peer in enumerate(sub_peers):
        g_copy(d, s, peer).start()
    send_strips()

    @pl.when(tail)
    def _():
        for other in [s] + sub_peers:
            pl.semaphore_signal(
                ready,
                inc=1,
                device_id={"tile": 0, "sub": other},
                device_id_type=pl.DeviceIdType.MESH,
            )

    chain = [x_own, -0.25 * around(x_own)]
    for k in range(2, K):
        chain.append(-0.5 * around(chain[k - 1]) - chain[k - 2])

    for copy in loads:
        copy.wait()
    pl.when(jnp.logical_not(one_kind))(second.wait)
    outer = OUTSIDE * width
    mid_first = [kinds[m] == kinds[0] for m in range(slots)]
    scales = (1.0, -0.5, 0.25, -0.125)

    def ghost_lines(value, at, count, single=False):
        first = jnp.dot(value, ghost[0, at], preferred_element_type=f32)
        if single:
            return [of_slot(first, m, count) for m in range(slots)]
        last = jnp.dot(value, ghost[1, at], preferred_element_type=f32)
        return [
            jnp.where(mid_first[m], of_slot(first, m, count), of_slot(last, m, count))
            for m in range(slots)
        ]

    x_inner = ghost_lines(
        jnp.concatenate(x_strips, axis=1).astype(bf16), slice(outer, outer + 4 * width), chans
    )

    x_edge = product(x_own.astype(bf16), inward[...])
    filters = jnp.concatenate([f_ref[k].astype(f32) for k in range(K)], axis=1).astype(bf16)
    pick_row = lax.broadcasted_iota(jnp.int32, (chans, total), 0) + chans * s
    pick_col = lax.broadcasted_iota(jnp.int32, (chans, total), 1)
    mine = jnp.dot(
        jnp.where(pick_row == pick_col, 1.0, 0.0).astype(bf16),
        filters,
        preferred_element_type=f32,
    )
    mixing = jnp.concatenate(
        [mine[:, k * total : (k + 1) * total] for k in range(K)], axis=0
    ).astype(bf16)
    outside = []
    for m in range(DEPTH):
        pieces = [mine[:, (m + 1) * total :]]
        if m > 0:
            pieces.append(jnp.zeros((chans, m * total), f32))
        outside.append(jnp.concatenate(pieces, axis=1))
    outside = jnp.concatenate(outside, axis=0)
    outside = jnp.concatenate([outside, outside], axis=1).astype(bf16)

    def load_g():
        return [
            jnp.concatenate([g_all[e, slot_list[m]].astype(f32) for e in range(subs)], axis=0)
            for m in range(slots)
        ]

    def await_g():
        await_bytes(g_all.at[pl.ds(0, subs - 1)], g_recv)

    def local_part(single):
        g_full = load_g()
        g_bf = [value.astype(bf16) for value in g_full]
        mixed = [jnp.dot(mixing, g_bf[m], preferred_element_type=f32) for m in range(slots)]
        grads = [
            jnp.concatenate([of_slot(mixed[m], k, chans) for m in range(slots)], axis=0)
            for k in range(K)
        ]
        after, upper = grads[K - 1], grads[K - 2] - 0.5 * around(grads[K - 1])
        for k in range(K - 3, 0, -1):
            after, upper = upper, grads[k] - 0.5 * around(upper) - after
        inner = grads[0] - 0.25 * around(upper) - after

        for m in range(slots):
            result[m] = of_slot(inner, m, chans)
        whole = jnp.concatenate(g_full, axis=0)
        whole_strips = strips_of(
            whole, jnp.dot(whole.astype(bf16), take[...], preferred_element_type=f32)
        )
        for m in range(slots):
            for e in range(subs):
                at = slice(m * total + e * chans, m * total + (e + 1) * chans)
                for side_at in range(4):
                    g_ext[e, m * 4 + side_at] = whole_strips[side_at][at].astype(bf16)
        g_inner = ghost_lines(
            jnp.concatenate(whole_strips, axis=1).astype(bf16),
            slice(outer, outer + 4 * width),
            total,
            single,
        )
        for m in range(slots):
            g_lines_own[m] = g_inner[m]

    @pl.when(head)
    def _():
        await_g()
        pl.semaphore_wait(ready, subs)
        for peer in [s] + sub_peers:
            far_copy(peer).start()
        local_part(True)


    @pl.when(tail)
    def _():
        await_bytes(x_ext.at[pl.ds(0, (tiles_n - 2) * packed)], x_recv)

    @pl.when(jnp.logical_not(tail))
    def _():
        await_bytes(x_ext.at[pl.ds(0, (tiles_n - 1) * packed)], x_recv)

    def pass_on():
        @pl.when(tail)
        def _():
            await_bytes(g_ext.at[0, pl.ds(0, (tiles_n - 2) * packed)], s_recv)

        @pl.when(jnp.logical_not(tail))
        def _():
            await_bytes(g_ext.at[0, pl.ds(0, (tiles_n - 1) * packed)], s_recv)

        for q, peer in enumerate(tile_peers):

            @pl.when(x_crosses(peer, j))
            def _():
                for d, other in enumerate(sub_peers):
                    forward_copy(peer, d, s, other).start()

    wanted = [
        [table_ref[(base + m) * OUTSIDE + r] for r in range(OUTSIDE)] for m in range(slots)
    ]

    def outer_strips(read):
        return jnp.concatenate(
            [
                jnp.concatenate([read(wanted[m][r]).astype(f32) for r in range(OUTSIDE)], axis=1)
                for m in range(slots)
            ],
            axis=0,
        )

    def by_power(lines):
        return jnp.concatenate(
            [
                lines[:, n * width : (n + 1) * width] * scales[n] for n in range(DEPTH)
            ],
            axis=0,
        )

    half = DEPTH * chans

    def by_degree(across):
        across = across[:half] + across[half:]
        across = across[:, : DEPTH * total] + across[:, DEPTH * total :]
        place = lax.broadcasted_iota(jnp.int32, (chans, DEPTH * total), 1)
        out = of_slot(across, 0, chans)
        for n in range(1, DEPTH):
            shifted = pltpu.roll(of_slot(across, n, chans), n * total, 1)
            out = out + jnp.where(place < n * total, 0.0, shifted)
        return out

    x_lines = ghost_lines(
        outer_strips(lambda index: x_ext[index]).astype(bf16), slice(0, outer), chans
    )
    x_lines = [by_power(x_lines[m] + x_inner[m]) for m in range(slots)]
    entering = []
    for k in range(1, K):
        for m in range(slots):
            pieces = [of_slot(x_lines[m], k - 1 - n, chans) for n in range(k)]
            if k < DEPTH:
                pieces.append(jnp.zeros((chans, (DEPTH - k) * width), f32))
            entering.append(jnp.concatenate(pieces, axis=1))
    entering = jnp.concatenate(split(jnp.concatenate(entering, axis=0)), axis=0)
    entering = jnp.dot(entering.astype(bf16), inward[...], preferred_element_type=f32)
    entering = entering[: DEPTH * rows] + entering[DEPTH * rows :]
    held = [x_own]
    for k in range(1, K):
        held += list(split(chain[k] + of_slot(entering, k - 1, rows)))
    terms = [
        jnp.concatenate([of_slot(value, m, chans) for value in held], axis=0).astype(bf16)
        for m in range(slots)
    ]
    pl.when(jnp.logical_not(head))(await_g)
    g_bf = [value.astype(bf16) for value in load_g()]
    grad = product(terms[0], g_bf[0])
    for m in range(1, slots):
        grad = grad + product(terms[m], g_bf[m])
    later = [
        of_slot(grad, 2 * k - 1, chans) + of_slot(grad, 2 * k, chans) for k in range(1, K)
    ]
    block[0] = jnp.concatenate(later, axis=1) * scale
    block[1] = jnp.concatenate(
        [grad[:chans] * scale, jnp.zeros((chans, width - total), f32)], axis=1
    )

    def send_blocks():
        for d, peer in enumerate(tile_peers):
            block_copy(d, j, peer).start()

    @pl.when(j != 0)
    def _():
        send_blocks()
        pass_on()
        local_part(False)


    def finish(single):
        if single:

            @pl.when(tail)
            def _():
                await_bytes(first_strips(subs, far_count), d_recv)
                await_bytes(first_strips(subs - 1, (tiles_n - 2) * packed), f_recv)

        @pl.when((j != 0) & jnp.logical_not(tail))
        def _():
            await_bytes(first_strips(subs - 1, (tiles_n - 1) * packed), f_recv)

        @pl.when(head)
        def _():
            await_bytes(first_strips(subs, sum(counts[1:])), d_recv)

        if single and far:
            far_lines, far_edge = [], []
            for m, r, index in far:
                held = jnp.concatenate(
                    [g_ext[e, index].astype(f32) for e in range(subs)], axis=0
                ).astype(bf16)
                rows_at = ghost[m // 4, r * width : (r + 1) * width]
                far_lines.append(by_power(jnp.dot(held, rows_at, preferred_element_type=f32)))
                mine_edge = of_slot(x_edge, m, chans)
                far_edge.append(
                    jnp.concatenate(
                        [mine_edge[:, n * width : (n + 1) * width] for n in range(DEPTH)], axis=0
                    )
                )
            far_lines = jnp.concatenate(split(jnp.concatenate(far_lines, axis=1)), axis=0)
            far_edge = jnp.concatenate(split(jnp.concatenate(far_edge, axis=1)), axis=0)
            crossed = by_degree(product(far_edge.astype(bf16), far_lines.astype(bf16)))
        if single:

            @pl.when(head)
            def _():
                if far:
                    block[0] = block[0] + crossed * scale
                send_blocks()

        gathered = outer_strips(
            lambda index: jnp.concatenate([g_ext[e, index].astype(f32) for e in range(subs)], axis=0)
        )
        g_lines = ghost_lines(gathered.astype(bf16), slice(0, outer), total, single)
        g_lines = jnp.concatenate(
            [by_power(g_lines[m] + g_lines_own[m]) for m in range(slots)], axis=1
        )
        mixed = jnp.dot(
            outside,
            jnp.concatenate(split(g_lines), axis=0).astype(bf16),
            preferred_element_type=f32,
        )
        mixed = jnp.concatenate(
            [
                jnp.concatenate(
                    [
                        of_slot(mixed, n, chans)[:, m * width : (m + 1) * width]
                        for n in range(DEPTH)
                    ],
                    axis=1,
                )
                for m in range(slots)
            ],
            axis=0,
        )
        spread = jnp.dot(
            jnp.concatenate(split(mixed), axis=0).astype(bf16),
            inward[...],
            preferred_element_type=f32,
        )
        inner = spread[:rows] + spread[rows:]
        for m in range(slots):
            result[m] = result[m] + of_slot(inner, m, chans)
        for slot in range(slots):
            in_ref[slot] = result[lax.rem(map_ref[base + slot], slots)].astype(bf16)
    pl.when(one_kind)(functools.partial(finish, True))
    pl.when(jnp.logical_not(one_kind))(functools.partial(finish, False))

    await_bytes(block_in.at[pl.ds(0, tiles_n - 1)], w_recv)
    block_in[j] = block[...]
    summed = block_in[0]
    for q in range(1, tiles_n):
        summed = summed + block_in[q]
    w_ref[0] = summed[1, :, :total]
    for k in range(1, K):
        w_ref[k] = summed[0, :, (k - 1) * total : k * total]

    await_bytes(block_in.at[pl.ds(0, tiles_n - 1)], w_send)
    await_bytes(g_all.at[pl.ds(0, subs - 1)], g_send)
    await_bytes(g_pack.at[pl.ds(0, tiles_n - 2)], s_send)

    @pl.when(head)
    def _():
        await_bytes(x_pack.at[pl.ds(0, tiles_n - 2)], x_send)
        await_bytes(first_strips(subs, far_count), d_send)

    @pl.when(j != 0)
    def _():
        await_bytes(x_pack, x_send)

    for q in range(1, tiles_n):

        @pl.when(j == q)
        def _():
            await_bytes(first_strips(subs, counts[q]), d_send)
            moved = tiles_n - 2 if q == tiles_n - 1 else tiles_n - 1
            await_bytes(first_strips(subs - 1, moved * packed), f_send)


def store_kernel(in_vmem, w_vmem, in_hbm, w_hbm, sem):
    copies = [
        pltpu.make_async_copy(in_vmem, in_hbm, sem.at[0]),
        pltpu.make_async_copy(w_vmem, w_hbm, sem.at[1]),
    ]
    for copy in copies:
        copy.start()
    for copy in copies:
        copy.wait()


def face_path(features, out_grad, filters, tile_map):
    slots, chans, pixels = features.shape
    side = math.isqrt(pixels)
    tiles_n, subs = lax.axis_size("tile"), lax.axis_size("sub")
    matrices, table, links, inward = ghost_tables(side, slots, tiles_n)
    scale = 1.0 / math.sqrt(slots * tiles_n * pixels)
    width = DEPTH * side
    vmem = pl.BlockSpec(memory_space=pltpu.VMEM)
    hbm = pl.BlockSpec(memory_space=pltpu.HBM)
    dma = pltpu.SemaphoreType.DMA
    bf16, f32 = jnp.bfloat16, jnp.float32
    held = slots * 4 + tiles_n * links[0]
    held_outs = pl.pallas_call(
        functools.partial(face_kernel, (slots, tiles_n, subs, side, links, scale)),
        out_shape=(
            pltpu.VMEM(features.shape, bf16),
            pltpu.VMEM((K, chans, filters.shape[2]), f32),
        ),
        in_specs=[hbm] * 7,
        out_specs=(vmem, vmem),
        scratch_shapes=[
            pltpu.VMEM((2,) + features.shape, bf16),
            pltpu.VMEM((subs,) + features.shape, bf16),
            pltpu.VMEM((slots * 4, chans, width), bf16),
            pltpu.VMEM((slots * 4, chans, width), bf16),
            pltpu.VMEM((tiles_n - 1, links[0], chans, width), bf16),
            pltpu.VMEM((tiles_n - 1, links[0], chans, width), bf16),
            pltpu.VMEM((held, chans, width), bf16),
            pltpu.VMEM((subs, held, chans, width), bf16),
            pltpu.VMEM((2, chans, width), f32),
            pltpu.VMEM((tiles_n, 2, chans, width), f32),
            pltpu.VMEM((slots, chans, pixels), f32),
            pltpu.VMEM((slots, chans * subs, DEPTH * width), f32),
            pltpu.VMEM((2,) + matrices.shape[1:], bf16),
            pltpu.VMEM(inward.shape, bf16),
            pltpu.VMEM((pixels, 2 * width), bf16),
            pltpu.VMEM(filters.shape, bf16),
            pltpu.SMEM(tile_map.shape, jnp.int32),
            pltpu.SMEM(table.shape, jnp.int32),
            pltpu.SemaphoreType.REGULAR,
            dma((9,)),
        ]
        + [dma] * 12,
        compiler_params=pltpu.CompilerParams(
            collective_id=0, has_side_effects=True, vmem_limit_bytes=67043328 - 512 * 1024
        ),
    )(
        features,
        out_grad,
        filters,
        tile_map,
        jnp.asarray(table),
        jnp.asarray(matrices, bf16),
        jnp.asarray(inward, bf16),
    )
    held_outs = [pltpu.with_memory_space_constraint(value, pltpu.VMEM) for value in held_outs]
    return pl.pallas_call(
        store_kernel,
        out_shape=(
            jax.ShapeDtypeStruct(features.shape, bf16),
            jax.ShapeDtypeStruct((K, chans, filters.shape[2]), f32),
        ),
        in_specs=[vmem] * 2,
        out_specs=(hbm, hbm),
        scratch_shapes=[dma((2,))],
    )(*held_outs)


def on_device(features, out_grad, filters, tile_map):
    slots, chans, pixels = features.shape
    side = math.isqrt(pixels)
    whole_faces = slots * lax.axis_size("tile") == 12
    channels = chans * lax.axis_size("sub")
    if whole_faces and 1 < slots < 5 and DEPTH * side == 128 and chans % 8 == 0 and channels == 32:
        return face_path(features, out_grad, filters, tile_map)
    return general_path(features, out_grad, filters, tile_map)


def solution(mesh):
    placed = (P(("grp", "tile"), "sub", None), P(("grp", "tile"), "sub", None), P(), P())
    return jax.shard_map(
        on_device,
        mesh=mesh,
        in_specs=placed,
        out_specs=(P(("grp", "tile"), "sub", None), P("grp", "sub", None)),
        check_vma=False,
    )
```

```python
import functools
import math

import jax
import jax.numpy as jnp
import numpy as np
from jax import lax
from jax.experimental import pallas as pl
from jax.experimental.pallas import tpu as pltpu
from jax.sharding import PartitionSpec as P

K = 5


def from_behind(value, axis, steps):
    count = lax.axis_size(axis)
    pairs = [(source, (source + steps) % count) for source in range(count)]
    return lax.ppermute(value, axis, pairs)


def tile_coords(nested_code, bit_count):
    coord_x = nested_code * 0
    coord_y = nested_code * 0
    for bit_level in range(bit_count):
        coord_x = coord_x + nested_code // 4**bit_level % 2 * 2**bit_level
        coord_y = coord_y + nested_code // (2 * 4**bit_level) % 2 * 2**bit_level
    return (coord_x, coord_y)


def nested_index(coord_x, coord_y, bit_count):
    nested_code = coord_x * 0
    for bit_level in range(bit_count):
        nested_code = nested_code + coord_x // 2**bit_level % 2 * 4**bit_level
        nested_code = nested_code + coord_y // 2**bit_level % 2 * (2 * 4**bit_level)
    return nested_code


def pick(condition, when_true, when_false):
    return when_false + (when_true - when_false) * condition


def neighbour_codes(tile_ids, per_face, side_count):
    bit_count = side_count.bit_length() - 1
    face_id = tile_ids // per_face
    coord_x, coord_y = tile_coords(tile_ids % per_face, bit_count)
    column = face_id % 4
    is_north = face_id < 4
    is_south = face_id >= 8
    last_tile = side_count - 1

    def by_cycle(north_value, equator_value, south_value):
        return pick(is_north, north_value, pick(is_south, south_value, equator_value))

    side_rules = [
        (
            coord_x > 0,
            (face_id, coord_x - 1, coord_y, 1),
            (
                by_cycle(4 + column, 8 + (column + 3) % 4, 8 + (column + 3) % 4),
                by_cycle(last_tile, last_tile, coord_y),
                by_cycle(coord_y, coord_y, 0),
                by_cycle(1, 1, 2),
            ),
        ),
        (
            coord_x < last_tile,
            (face_id, coord_x + 1, coord_y, 0),
            (
                by_cycle((column + 1) % 4, column, 4 + (column + 1) % 4),
                by_cycle(coord_y, 0, 0),
                by_cycle(last_tile, coord_y, coord_y),
                by_cycle(3, 0, 0),
            ),
        ),
        (
            coord_y > 0,
            (face_id, coord_x, coord_y - 1, 3),
            (
                by_cycle(4 + (column + 1) % 4, 8 + column, 8 + (column + 1) % 4),
                by_cycle(coord_x, coord_x, 0),
                by_cycle(last_tile, last_tile, coord_x),
                by_cycle(3, 3, 0),
            ),
        ),
        (
            coord_y < last_tile,
            (face_id, coord_x, coord_y + 1, 2),
            (
                by_cycle((column + 3) % 4, (column + 3) % 4, 4 + column),
                by_cycle(last_tile, coord_x, coord_x),
                by_cycle(coord_x, 0, 0),
                by_cycle(1, 2, 2),
            ),
        ),
    ]
    target_list = []
    edge_list = []
    for inside, within, across in side_rules:
        chosen = [
            pick(inside, near_value, far_value) for near_value, far_value in zip(within, across)
        ]
        target_list.append(chosen[0] * per_face + nested_index(chosen[1], chosen[2], bit_count))
        edge_list.append(chosen[3] + tile_ids * 0)
    return (target_list, edge_list)


def neighbour_table(tile_map, per_face, side_count):
    target_list, edge_list = neighbour_codes(tile_map, per_face, side_count)
    targets = jnp.stack(target_list, axis=1).astype(jnp.int32)
    edges = jnp.stack(edge_list, axis=1).astype(jnp.int32)
    slot_of = jnp.argsort(tile_map).astype(jnp.int32)
    return (slot_of[targets].astype(jnp.int32), edges)


def peer_offsets(slot_count, device_count, per_face, side_count):
    tile_ids = np.arange(slot_count * device_count, dtype=np.int64)
    target_list, edge_list = neighbour_codes(tile_ids, per_face, side_count)
    targets = np.stack(target_list, axis=1)
    offsets = (tile_ids[:, None] // slot_count - targets // slot_count) % device_count
    distinct = sorted(set((int(value) for value in offsets.ravel())) - {0})
    position = np.zeros(device_count, dtype=np.int32)
    for order, value in enumerate(distinct):
        position[value] = order + 1
    return (distinct, position)


def edge_lines(values, tile_side):
    return jnp.stack(
        [
            values[..., :tile_side],
            values[..., -tile_side:],
            values[..., ::tile_side],
            values[..., tile_side - 1 :: tile_side],
        ],
        axis=1,
    )


def stencil(values, ghosts, tile_side):
    position = jnp.arange(values.shape[-1]) % tile_side
    zero_line = jnp.zeros_like(values[..., :1])
    upper_side = jnp.concatenate([ghosts[:, 0], values[..., :-tile_side]], axis=-1)
    lower_side = jnp.concatenate([values[..., tile_side:], ghosts[:, 1]], axis=-1)
    left_side = jnp.where(
        position == 0,
        jnp.repeat(ghosts[:, 2], tile_side, axis=-1),
        jnp.concatenate([zero_line, values[..., :-1]], axis=-1),
    )
    right_side = jnp.where(
        position == tile_side - 1,
        jnp.repeat(ghosts[:, 3], tile_side, axis=-1),
        jnp.concatenate([values[..., 1:], zero_line], axis=-1),
    )
    return -0.25 * (upper_side + lower_side + left_side + right_side)


def tile_total(filter_part):
    return lax.psum(filter_part, "tile")


def general_path(features, out_grad, filters, tile_map):
    slot_count = features.shape[0]
    group_channels = features.shape[1]
    tile_side = math.isqrt(features.shape[2])
    device_count = lax.axis_size("tile")
    total_tiles = slot_count * device_count
    side_count = math.isqrt(total_tiles // 12)
    scale_factor = 1.0 / math.sqrt(total_tiles * features.shape[2])
    highest = lax.Precision.HIGHEST
    slot_table, edge_table = neighbour_table(tile_map, total_tiles // 12, side_count)
    my_device = lax.axis_index("tile")
    first_slot = my_device * slot_count
    my_slots = lax.dynamic_slice_in_dim(slot_table, first_slot, slot_count, 0)
    my_edges = lax.dynamic_slice_in_dim(edge_table, first_slot, slot_count, 0)
    channel_start = lax.axis_index("sub") * group_channels
    weights = filters.astype(jnp.float32)
    distinct, position = peer_offsets(slot_count, device_count, total_tiles // 12, side_count)
    sender_gap = (my_device - my_slots // slot_count) % device_count
    local_rows = jnp.asarray(position)[sender_gap] * slot_count + my_slots % slot_count

    def laplace(values):
        border = edge_lines(values, tile_side).reshape(slot_count, 4, group_channels * tile_side)
        received = [border]
        for offset_value in distinct:
            received.append(from_behind(border, "tile", offset_value))
        stacked = jnp.concatenate(received, axis=0)
        stacked = stacked.reshape(stacked.shape[0], 4, group_channels, tile_side)
        rows = []
        for slot in range(slot_count):
            for side in range(4):
                start = (local_rows[slot, side], my_edges[slot, side], 0, 0)
                rows.append(
                    lax.dynamic_slice(stacked, start, (1, 1, group_channels, tile_side))
                )
        ghosts = jnp.concatenate(rows, axis=0)
        ghosts = ghosts.reshape(slot_count, 4, group_channels, tile_side)
        return stencil(values, ghosts, tile_side)

    whole_grad = lax.all_gather(out_grad, "sub", axis=1, tiled=True)
    cotangent = whole_grad.astype(jnp.float32)
    inputs = features.astype(jnp.float32)
    previous, current = (inputs, laplace(inputs))
    filter_terms = [
        jnp.einsum("sip,sop->io", inputs, cotangent, precision=highest),
        jnp.einsum("sip,sop->io", current, cotangent, precision=highest),
    ]
    for degree in range(2, K):
        previous, current = (current, 2.0 * laplace(current) - previous)
        filter_terms.append(jnp.einsum("sip,sop->io", current, cotangent, precision=highest))
    weight_grad = tile_total(jnp.stack(filter_terms)) * scale_factor
    row_block = lax.dynamic_slice_in_dim(weights, channel_start, group_channels, 1)

    def mixed(degree):
        return jnp.einsum("sop,io->sip", cotangent, row_block[degree], precision=highest)

    next_sum = mixed(K - 1)
    after_next = jnp.zeros_like(next_sum)
    for degree in range(K - 2, 0, -1):
        next_sum, after_next = (mixed(degree) + 2.0 * laplace(next_sum) - after_next, next_sum)
    in_grad = (mixed(0) + laplace(next_sum) - after_next).astype(jnp.bfloat16)
    return (in_grad, weight_grad)


DEPTH = K - 1
GHOST_SIDES = (0, 2, 3, 1)
OUTSIDE = 6


def face_graph(tile_side):
    tile_ids = np.arange(12, dtype=np.int64)
    target_list, edge_list = neighbour_codes(tile_ids, 1, 1)
    targets = np.stack(target_list, axis=1)
    edges = np.stack(edge_list, axis=1)
    pixels = tile_side * tile_side
    grid = np.arange(pixels).reshape(tile_side, tile_side)
    lines = [grid[0], grid[-1], grid[:, 0], grid[:, -1]]
    ghosts = np.zeros((12, 4, tile_side), dtype=np.int64)
    around = np.zeros((12, 4, tile_side, tile_side), dtype=np.int64)
    for tile in range(12):
        for side in range(4):
            ghosts[tile, side] = targets[tile, side] * pixels + lines[edges[tile, side]]
        whole = tile * pixels + grid
        around[tile, 0] = np.concatenate([ghosts[tile, 0][None], whole[:-1]], 0)
        around[tile, 1] = np.concatenate([whole[1:], ghosts[tile, 1][None]], 0)
        around[tile, 2] = np.concatenate([ghosts[tile, 2][:, None], whole[:, :-1]], 1)
        around[tile, 3] = np.concatenate([whole[:, 1:], ghosts[tile, 3][:, None]], 1)
    around = around.transpose(0, 2, 3, 1).reshape(12 * pixels, 4)
    return targets, edges, ghosts, around


@functools.lru_cache(None)
def ghost_tables(tile_side, slots, tiles_n):
    targets, edges, ghosts, around = face_graph(tile_side)
    pixels = tile_side * tile_side
    grid = np.arange(pixels).reshape(tile_side, tile_side)
    strips = np.stack(
        [
            grid[:DEPTH].ravel(),
            grid[-DEPTH:].ravel(),
            grid[:, :DEPTH].T.ravel(),
            grid[:, -DEPTH:].T.ravel(),
        ]
    )
    sources_of = []
    by_class = []
    for tile in range(12):
        wanted = np.concatenate([ghosts[tile, side] for side in GHOST_SIDES])
        power = np.zeros((wanted.size, 12 * pixels), dtype=np.int32)
        power[np.arange(wanted.size), wanted] = 1
        powers = [power]
        for _ in range(DEPTH - 1):
            powers.append(sum(powers[-1][:, around[:, side]] for side in range(4)))
        rows = np.concatenate(
            [powers[0], powers[1], powers[2] - 8 * powers[0], powers[3] - 12 * powers[1]]
        )
        support = np.flatnonzero(np.any(rows != 0, axis=0))
        sources = [(int(targets[tile, side]), int(edges[tile, side])) for side in range(4)]
        own = [(tile, side) for side in range(4)]
        covered = set(int(t) * pixels + int(p) for t, e in sources + own for p in strips[e])
        left = [int(p) for p in support if int(p) not in covered]
        corner_tiles = {}
        for pixel in left:
            corner_tiles.setdefault(pixel // pixels, []).append(pixel % pixels)
        first = lambda t: int(
            np.flatnonzero(np.any(rows[:, [t * pixels + p for p in corner_tiles[t]]] != 0, axis=1))[0]
        )
        for other in sorted(corner_tiles, key=first):
            choice = [e for e in range(4) if set(corner_tiles[other]) <= set(strips[e].tolist())]
            sources.append((other, choice[0]))
        assert len(sources) <= OUTSIDE
        while len(sources) < OUTSIDE:
            sources.append(sources[-1])
        sources_of.append(sources)
        lanes = np.concatenate([t * pixels + strips[e] for t, e in sources + own])
        seen, keep = set(), np.zeros(lanes.size, dtype=bool)
        for lane, pixel in enumerate(lanes.tolist()):
            keep[lane] = pixel not in seen
            seen.add(pixel)
        assert set(support.tolist()) <= seen
        matrix = (rows[:, lanes] * keep[None]).T
        assert np.abs(matrix).max() <= 127
        if tile % 4 == 0:
            by_class.append(matrix)
        else:
            assert np.array_equal(matrix, by_class[-1])
    wanted = {}
    for tile in range(12):
        for t, e in sources_of[tile]:
            pair = (t // slots, tile // slots)
            if pair[0] != pair[1]:
                held = wanted.setdefault(pair, [])
                if (t, e) not in held:
                    held.append((t, e))
    packed = max(len(held) for held in wanted.values())
    send = np.zeros((tiles_n, tiles_n, packed), dtype=np.int32)
    for (q, p), held in wanted.items():
        for order, (t, e) in enumerate(held):
            send[q, p, order] = (t - q * slots) * 4 + e
    take_from = np.zeros((12, OUTSIDE), dtype=np.int32)
    for tile in range(12):
        for order, (t, e) in enumerate(sources_of[tile]):
            q, p = t // slots, tile // slots
            if q == p:
                take_from[tile, order] = (t - q * slots) * 4 + e
            else:
                at = wanted[(q, p)].index((t, e))
                take_from[tile, order] = slots * 4 + q * packed + at
    table = np.concatenate([take_from.ravel(), send.ravel()])
    counts = tuple(len(wanted.get((q, 0), ())) for q in range(tiles_n))
    far = []
    for tile in range(slots):
        for order, (t, e) in enumerate(sources_of[tile]):
            if t // slots == tiles_n - 1 and (t, e) not in sources_of[tile][:order]:
                far.append((tile, order, int(take_from[tile, order])))
    spread = np.zeros((4, tile_side, tile_side, tile_side))
    step = np.arange(tile_side)
    spread[0, step, 0, step] = 1
    spread[1, step, step, 0] = 1
    spread[2, step, step, -1] = 1
    spread[3, step, -1, step] = 1
    local = np.zeros((pixels, pixels))
    for u in range(tile_side):
        for v in range(tile_side):
            for du, dv in ((1, 0), (-1, 0), (0, 1), (0, -1)):
                if 0 <= u + du < tile_side and 0 <= v + dv < tile_side:
                    local[grid[u, v], grid[u + du, v + dv]] = -0.25
    inward = [-0.25 * spread.reshape(4 * tile_side, pixels)]
    inward.append(2.0 * inward[0] @ local)
    for _ in range(DEPTH - 2):
        inward.append(2.0 * inward[-1] @ local - inward[-2])
    inward = np.concatenate(inward)
    assert np.array_equal(inward, inward.astype(jnp.bfloat16).astype(np.float64))
    return np.stack(by_class), table, (packed, counts, len(wanted.get((0, tiles_n - 1), ())), tuple(far)), inward


def split(value):
    high = value.astype(jnp.bfloat16).astype(jnp.float32)
    return high, value - high


def product(left, right):
    return lax.dot_general(
        left, right, (((1,), (1,)), ((), ())), preferred_element_type=jnp.float32
    )


def face_kernel(
    sizes,
    x_hbm,
    g_hbm,
    f_hbm,
    map_hbm,
    table_hbm,
    ghost_hbm,
    inward_hbm,
    in_ref,
    w_ref,
    xg_ref,
    g_all,
    x_mine,
    g_mine,
    x_pack,
    g_pack,
    x_ext,
    g_ext,
    block,
    block_in,
    result,
    g_lines_own,
    ghost,
    inward,
    take,
    f_ref,
    map_ref,
    table_ref,
    ready,
    load_sem,
    x_send,
    x_recv,
    s_send,
    s_recv,
    g_send,
    g_recv,
    d_send,
    d_recv,
    f_send,
    f_recv,
    w_send,
    w_recv,
):
    slots, tiles_n, subs, side, (packed, counts, far_count, far), scale = sizes
    x_ref, g_ref = xg_ref.at[0], xg_ref.at[1]
    chans = x_ref.shape[1]
    total = subs * chans
    pixels = side * side
    width = DEPTH * side
    rows = slots * chans
    bf16, f32 = jnp.bfloat16, jnp.float32
    j = lax.axis_index("tile")
    s = lax.axis_index("sub")
    tile_peers = []
    for d in range(tiles_n - 1):
        up = d + (j <= d).astype(jnp.int32)
        back = tiles_n - 2 - d
        down = back + (j <= back).astype(jnp.int32)
        tile_peers.append(jnp.where(2 * j < tiles_n, down, up))
    core_peer = s + 1 - 2 * lax.rem(s, 2)
    sub_peers = [lax.rem(s + 2, subs), lax.rem(core_peer + 2, subs), core_peer]
    friends = len(tile_peers) + len(sub_peers)
    head = j == 0
    tail = j == tiles_n - 1
    kinds = [(slots * j + m) // 4 for m in range(slots)]

    def greet(friend):
        pl.semaphore_signal(
            pltpu.get_barrier_semaphore(),
            inc=1,
            device_id=friend,
            device_id_type=pl.DeviceIdType.MESH,
        )

    first_loads = [
        pltpu.make_async_copy(x_hbm, x_ref, load_sem.at[0]),
        pltpu.make_async_copy(g_hbm, g_ref, load_sem.at[0]),
        pltpu.make_async_copy(map_hbm, map_ref, load_sem.at[2]),
        pltpu.make_async_copy(table_hbm, table_ref, load_sem.at[3]),
    ]
    barrier = pltpu.get_barrier_semaphore()
    for peer in sub_peers:
        greet({"sub": peer})
    for d, peer in enumerate(tile_peers):

        @pl.when(jnp.logical_not(tail & (peer == 0)))
        def _():
            greet({"tile": peer})

    for copy in first_loads:
        copy.start()

    one_kind = kinds[0] == kinds[-1]
    loads = [
        pltpu.make_async_copy(ghost_hbm.at[kinds[0]], ghost.at[0], load_sem.at[4]),
        pltpu.make_async_copy(inward_hbm, inward, load_sem.at[5]),
        pltpu.make_async_copy(f_hbm, f_ref, load_sem.at[6]),
        pltpu.make_async_copy(g_hbm, g_all.at[s], load_sem.at[7]),
    ]
    second = pltpu.make_async_copy(ghost_hbm.at[kinds[-1]], ghost.at[1], load_sem.at[8])
    for copy in loads:
        copy.start()
    pl.when(jnp.logical_not(one_kind))(second.start)

    @pl.when(head)
    def _():
        for peer in tile_peers:
            for other in sub_peers:
                greet({"tile": peer, "sub": other})

    def remote(source, target, send, recv, device):
        return pltpu.make_async_remote_copy(
            source,
            target,
            send,
            recv,
            device_id=device,
            device_id_type=pl.DeviceIdType.MESH,
        )

    def g_copy(d, sender, peer):
        return remote(g_hbm, g_all.at[sender], g_send, g_recv, {"sub": peer})

    def open_up():
        pl.semaphore_wait(barrier, friends + jnp.where(head, -1, subs - 1))

    base = slots * j
    column = lax.broadcasted_iota(jnp.int32, (pixels, 2 * width), 1)
    wanted_pixel = column % side * side + column % width // side
    wanted_pixel = wanted_pixel + jnp.where(column < width, 0, side - DEPTH)
    pixel = lax.broadcasted_iota(jnp.int32, (pixels, 2 * width), 0)
    take[...] = jnp.where(pixel == wanted_pixel, 1.0, 0.0).astype(bf16)
    pltpu.make_async_copy(xg_ref, xg_ref, load_sem.at[0]).wait()
    for copy in first_loads[2:]:
        copy.wait()

    def slot_of(m):
        found = 0
        for slot in range(1, slots):
            found = jnp.where(map_ref[base + slot] == base + m, slot, found)
        return found

    slot_list = [slot_of(m) for m in range(slots)]
    x_own = jnp.concatenate([x_ref[slot_list[m]].astype(f32) for m in range(slots)], axis=0)
    g_own = jnp.concatenate([g_ref[slot_list[m]].astype(f32) for m in range(slots)], axis=0)
    both = jnp.concatenate([x_own, g_own], axis=0).astype(bf16)
    cut = jnp.dot(both, take[...], preferred_element_type=f32)

    def strips_of(value, cut_value):
        return [
            value[:, :width],
            value[:, pixels - width :],
            cut_value[:, :width],
            cut_value[:, width:],
        ]

    x_strips = strips_of(x_own, cut[:rows])
    g_strips = strips_of(g_own, cut[rows:])
    for m in range(slots):
        at = slice(m * chans, (m + 1) * chans)
        for e in range(4):
            x_mine[m * 4 + e] = x_strips[e][at].astype(bf16)
            g_mine[m * 4 + e] = g_strips[e][at].astype(bf16)
    sends = 12 * OUTSIDE
    for d, peer in enumerate(tile_peers):
        for i in range(packed):
            index = table_ref[sends + (j * tiles_n + peer) * packed + i]
            x_pack[d, i] = x_mine[index]
            g_pack[d, i] = g_mine[index]
    for m in range(slots):
        at = slice(m * chans, (m + 1) * chans)
        for e in range(4):
            x_ext[m * 4 + e] = x_strips[e][at].astype(bf16)

    def landing(sender):
        return pl.ds(slots * 4 + sender * packed, packed)

    def x_copy(d, sender, peer):
        return remote(
            x_pack.at[d], x_ext.at[landing(sender)], x_send, x_recv, {"tile": peer}
        )

    def strip_copy(d, sender, peer):
        return remote(
            g_pack.at[d],
            g_ext.at[s, landing(sender)],
            s_send,
            s_recv,
            {"tile": peer},
        )

    def forward_copy(q, d, sender, peer):
        held = g_ext.at[sender, landing(q)]
        return remote(held, held, f_send, f_recv, {"sub": peer})

    def block_copy(d, sender, peer):
        return remote(block, block_in.at[sender], w_send, w_recv, {"tile": peer})

    def x_crosses(sender, peer):
        return jnp.logical_not((sender == 0) & (peer == tiles_n - 1))

    def direct_copy(q, d, sender, peer):
        at = 0 if 2 * q >= tiles_n else tiles_n - 2
        return remote(
            g_pack.at[at, pl.ds(0, counts[q])],
            g_ext.at[sender, pl.ds(slots * 4 + q * packed, counts[q])],
            d_send,
            d_recv,
            {"tile": 0, "sub": peer},
        )

    def far_copy(peer):
        return remote(
            g_pack.at[0, pl.ds(0, far_count)],
            g_ext.at[s, pl.ds(slots * 4, far_count)],
            d_send,
            d_recv,
            {"tile": tiles_n - 1, "sub": peer},
        )

    def await_bytes(held, semaphore):
        pltpu.make_async_copy(held, held, semaphore).wait()

    def first_strips(rows_of, count):
        return g_ext.at[pl.ds(0, rows_of), pl.ds(0, count)]

    def for_direct(action):
        for q in range(1, tiles_n):

            @pl.when(j == q)
            def _():
                for d, peer in enumerate([s] + sub_peers):
                    action(direct_copy(q, d, s, peer))

    def send_strips():
        for_direct(lambda copy: copy.start())
        for d, peer in enumerate(tile_peers):
            pl.when((peer != 0) & x_crosses(j, peer))(strip_copy(d, j, peer).start)

    @pl.when(tail)
    def _():
        x_ext[landing(0)] = jnp.zeros((packed, chans, width), bf16)


    lane = lax.broadcasted_iota(jnp.int32, (rows, pixels), 1)
    y_at = lane % side

    def around(value):
        out = jnp.where(lane < side, 0.0, pltpu.roll(value, side, 1))
        out = out + jnp.where(lane >= pixels - side, 0.0, pltpu.roll(value, pixels - side, 1))
        out = out + jnp.where(y_at == 0, 0.0, pltpu.roll(value, 1, 1))
        return out + jnp.where(y_at == side - 1, 0.0, pltpu.roll(value, pixels - 1, 1))

    def of_slot(value, m, count):
        return value[m * count : (m + 1) * count]

    open_up()
    for d, peer in enumerate(tile_peers):
        pl.when(x_crosses(j, peer))(x_copy(d, j, peer).start)
    for d, peer in enumerate(sub_peers):
        g_copy(d, s, peer).start()
    send_strips()

    @pl.when(tail)
    def _():
        for other in [s] + sub_peers:
            pl.semaphore_signal(
                ready,
                inc=1,
                device_id={"tile": 0, "sub": other},
                device_id_type=pl.DeviceIdType.MESH,
            )

    chain = [x_own, -0.25 * around(x_own)]
    for k in range(2, K):
        chain.append(-0.5 * around(chain[k - 1]) - chain[k - 2])

    for copy in loads:
        copy.wait()
    pl.when(jnp.logical_not(one_kind))(second.wait)
    outer = OUTSIDE * width
    mid_first = [kinds[m] == kinds[0] for m in range(slots)]
    scales = (1.0, -0.5, 0.25, -0.125)

    def ghost_lines(value, at, count, single=False):
        first = jnp.dot(value, ghost[0, at], preferred_element_type=f32)
        if single:
            return [of_slot(first, m, count) for m in range(slots)]
        last = jnp.dot(value, ghost[1, at], preferred_element_type=f32)
        return [
            jnp.where(mid_first[m], of_slot(first, m, count), of_slot(last, m, count))
            for m in range(slots)
        ]

    x_inner = ghost_lines(
        jnp.concatenate(x_strips, axis=1).astype(bf16), slice(outer, outer + 4 * width), chans
    )

    x_edge = product(x_own.astype(bf16), inward[...])
    filters = jnp.concatenate([f_ref[k].astype(f32) for k in range(K)], axis=1).astype(bf16)
    pick_row = lax.broadcasted_iota(jnp.int32, (chans, total), 0) + chans * s
    pick_col = lax.broadcasted_iota(jnp.int32, (chans, total), 1)
    mine = jnp.dot(
        jnp.where(pick_row == pick_col, 1.0, 0.0).astype(bf16),
        filters,
        preferred_element_type=f32,
    )
    mixing = jnp.concatenate(
        [mine[:, k * total : (k + 1) * total] for k in range(K)], axis=0
    ).astype(bf16)
    outside = []
    for m in range(DEPTH):
        pieces = [mine[:, (m + 1) * total :]]
        if m > 0:
            pieces.append(jnp.zeros((chans, m * total), f32))
        outside.append(jnp.concatenate(pieces, axis=1))
    outside = jnp.concatenate(outside, axis=0)
    outside = jnp.concatenate([outside, outside], axis=1).astype(bf16)

    def load_g():
        return [
            jnp.concatenate([g_all[e, slot_list[m]].astype(f32) for e in range(subs)], axis=0)
            for m in range(slots)
        ]

    def await_g():
        await_bytes(g_all.at[pl.ds(0, subs - 1)], g_recv)

    def local_part(single):
        g_full = load_g()
        g_bf = [value.astype(bf16) for value in g_full]
        mixed = [jnp.dot(mixing, g_bf[m], preferred_element_type=f32) for m in range(slots)]
        grads = [
            jnp.concatenate([of_slot(mixed[m], k, chans) for m in range(slots)], axis=0)
            for k in range(K)
        ]
        after, upper = grads[K - 1], grads[K - 2] - 0.5 * around(grads[K - 1])
        for k in range(K - 3, 0, -1):
            after, upper = upper, grads[k] - 0.5 * around(upper) - after
        inner = grads[0] - 0.25 * around(upper) - after

        for m in range(slots):
            result[m] = of_slot(inner, m, chans)
        whole = jnp.concatenate(g_full, axis=0)
        whole_strips = strips_of(
            whole, jnp.dot(whole.astype(bf16), take[...], preferred_element_type=f32)
        )
        for m in range(slots):
            for e in range(subs):
                at = slice(m * total + e * chans, m * total + (e + 1) * chans)
                for side_at in range(4):
                    g_ext[e, m * 4 + side_at] = whole_strips[side_at][at].astype(bf16)
        g_inner = ghost_lines(
            jnp.concatenate(whole_strips, axis=1).astype(bf16),
            slice(outer, outer + 4 * width),
            total,
            single,
        )
        for m in range(slots):
            g_lines_own[m] = g_inner[m]

    @pl.when(head)
    def _():
        await_g()
        pl.semaphore_wait(ready, subs)
        for peer in [s] + sub_peers:
            far_copy(peer).start()
        local_part(True)


    @pl.when(tail)
    def _():
        await_bytes(x_ext.at[pl.ds(0, (tiles_n - 2) * packed)], x_recv)

    @pl.when(jnp.logical_not(tail))
    def _():
        await_bytes(x_ext.at[pl.ds(0, (tiles_n - 1) * packed)], x_recv)

    def pass_on():
        @pl.when(tail)
        def _():
            await_bytes(g_ext.at[0, pl.ds(0, (tiles_n - 2) * packed)], s_recv)

        @pl.when(jnp.logical_not(tail))
        def _():
            await_bytes(g_ext.at[0, pl.ds(0, (tiles_n - 1) * packed)], s_recv)

        for q, peer in enumerate(tile_peers):

            @pl.when(x_crosses(peer, j))
            def _():
                for d, other in enumerate(sub_peers):
                    forward_copy(peer, d, s, other).start()

    wanted = [
        [table_ref[(base + m) * OUTSIDE + r] for r in range(OUTSIDE)] for m in range(slots)
    ]

    def outer_strips(read):
        return jnp.concatenate(
            [
                jnp.concatenate([read(wanted[m][r]).astype(f32) for r in range(OUTSIDE)], axis=1)
                for m in range(slots)
            ],
            axis=0,
        )

    def by_power(lines):
        return jnp.concatenate(
            [
                lines[:, n * width : (n + 1) * width] * scales[n] for n in range(DEPTH)
            ],
            axis=0,
        )

    half = DEPTH * chans

    def by_degree(across):
        across = across[:half] + across[half:]
        across = across[:, : DEPTH * total] + across[:, DEPTH * total :]
        place = lax.broadcasted_iota(jnp.int32, (chans, DEPTH * total), 1)
        out = of_slot(across, 0, chans)
        for n in range(1, DEPTH):
            shifted = pltpu.roll(of_slot(across, n, chans), n * total, 1)
            out = out + jnp.where(place < n * total, 0.0, shifted)
        return out

    x_lines = ghost_lines(
        outer_strips(lambda index: x_ext[index]).astype(bf16), slice(0, outer), chans
    )
    x_lines = [by_power(x_lines[m] + x_inner[m]) for m in range(slots)]
    entering = []
    for k in range(1, K):
        for m in range(slots):
            pieces = [of_slot(x_lines[m], k - 1 - n, chans) for n in range(k)]
            if k < DEPTH:
                pieces.append(jnp.zeros((chans, (DEPTH - k) * width), f32))
            entering.append(jnp.concatenate(pieces, axis=1))
    high, low = split(jnp.concatenate(entering, axis=0))
    entering = jnp.concatenate([high, low[rows:]], axis=0)
    entering = jnp.dot(entering.astype(bf16), inward[...], preferred_element_type=f32)
    held = [x_own]
    for k in range(1, K):
        full = chain[k] + of_slot(entering, k - 1, rows)
        if k > 1:
            full = full + of_slot(entering, K - 3 + k, rows)
        held += list(split(full))
    terms = [
        jnp.concatenate([of_slot(value, m, chans) for value in held], axis=0).astype(bf16)
        for m in range(slots)
    ]
    pl.when(jnp.logical_not(head))(await_g)
    g_bf = [value.astype(bf16) for value in load_g()]
    grad = product(terms[0], g_bf[0])
    for m in range(1, slots):
        grad = grad + product(terms[m], g_bf[m])
    later = [
        of_slot(grad, 2 * k - 1, chans) + of_slot(grad, 2 * k, chans) for k in range(1, K)
    ]
    block[0] = jnp.concatenate(later, axis=1) * scale
    block[1] = jnp.concatenate(
        [grad[:chans] * scale, jnp.zeros((chans, width - total), f32)], axis=1
    )

    def send_blocks():
        for d, peer in enumerate(tile_peers):
            block_copy(d, j, peer).start()

    @pl.when(j != 0)
    def _():
        send_blocks()
        pass_on()
        local_part(False)


    def finish(single):
        if single:

            @pl.when(tail)
            def _():
                await_bytes(first_strips(subs, far_count), d_recv)
                await_bytes(first_strips(subs - 1, (tiles_n - 2) * packed), f_recv)

        @pl.when((j != 0) & jnp.logical_not(tail))
        def _():
            await_bytes(first_strips(subs - 1, (tiles_n - 1) * packed), f_recv)

        @pl.when(head)
        def _():
            await_bytes(first_strips(subs, sum(counts[1:])), d_recv)

        if single and far:
            far_lines, far_edge = [], []
            for m, r, index in far:
                held = jnp.concatenate(
                    [g_ext[e, index].astype(f32) for e in range(subs)], axis=0
                ).astype(bf16)
                rows_at = ghost[m // 4, r * width : (r + 1) * width]
                far_lines.append(by_power(jnp.dot(held, rows_at, preferred_element_type=f32)))
                mine_edge = of_slot(x_edge, m, chans)
                far_edge.append(
                    jnp.concatenate(
                        [mine_edge[:, n * width : (n + 1) * width] for n in range(DEPTH)], axis=0
                    )
                )
            far_lines = jnp.concatenate(split(jnp.concatenate(far_lines, axis=1)), axis=0)
            far_edge = jnp.concatenate(split(jnp.concatenate(far_edge, axis=1)), axis=0)
            crossed = by_degree(product(far_edge.astype(bf16), far_lines.astype(bf16)))
        if single:

            @pl.when(head)
            def _():
                if far:
                    block[0] = block[0] + crossed * scale
                send_blocks()

        gathered = outer_strips(
            lambda index: jnp.concatenate([g_ext[e, index].astype(f32) for e in range(subs)], axis=0)
        )
        g_lines = ghost_lines(gathered.astype(bf16), slice(0, outer), total, single)
        g_lines = jnp.concatenate(
            [by_power(g_lines[m] + g_lines_own[m]) for m in range(slots)], axis=1
        )
        mixed = jnp.dot(
            outside,
            jnp.concatenate(split(g_lines), axis=0).astype(bf16),
            preferred_element_type=f32,
        )
        mixed = jnp.concatenate(
            [
                jnp.concatenate(
                    [
                        of_slot(mixed, n, chans)[:, m * width : (m + 1) * width]
                        for n in range(DEPTH)
                    ],
                    axis=1,
                )
                for m in range(slots)
            ],
            axis=0,
        )
        spread = jnp.dot(
            jnp.concatenate(split(mixed), axis=0).astype(bf16),
            inward[...],
            preferred_element_type=f32,
        )
        inner = spread[:rows] + spread[rows:]
        for m in range(slots):
            result[m] = result[m] + of_slot(inner, m, chans)
        for slot in range(slots):
            in_ref[slot] = result[lax.rem(map_ref[base + slot], slots)].astype(bf16)
    pl.when(one_kind)(functools.partial(finish, True))
    pl.when(jnp.logical_not(one_kind))(functools.partial(finish, False))

    await_bytes(block_in.at[pl.ds(0, tiles_n - 1)], w_recv)
    block_in[j] = block[...]
    summed = block_in[0]
    for q in range(1, tiles_n):
        summed = summed + block_in[q]
    w_ref[0] = summed[1, :, :total]
    for k in range(1, K):
        w_ref[k] = summed[0, :, (k - 1) * total : k * total]

    await_bytes(block_in.at[pl.ds(0, tiles_n - 1)], w_send)
    await_bytes(g_all.at[pl.ds(0, subs - 1)], g_send)
    await_bytes(g_pack.at[pl.ds(0, tiles_n - 2)], s_send)

    @pl.when(head)
    def _():
        await_bytes(x_pack.at[pl.ds(0, tiles_n - 2)], x_send)
        await_bytes(first_strips(subs, far_count), d_send)

    @pl.when(j != 0)
    def _():
        await_bytes(x_pack, x_send)

    for q in range(1, tiles_n):

        @pl.when(j == q)
        def _():
            await_bytes(first_strips(subs, counts[q]), d_send)
            moved = tiles_n - 2 if q == tiles_n - 1 else tiles_n - 1
            await_bytes(first_strips(subs - 1, moved * packed), f_send)


def store_kernel(in_vmem, w_vmem, in_hbm, w_hbm, sem):
    copies = [
        pltpu.make_async_copy(in_vmem, in_hbm, sem.at[0]),
        pltpu.make_async_copy(w_vmem, w_hbm, sem.at[1]),
    ]
    for copy in copies:
        copy.start()
    for copy in copies:
        copy.wait()


def face_path(features, out_grad, filters, tile_map):
    slots, chans, pixels = features.shape
    side = math.isqrt(pixels)
    tiles_n, subs = lax.axis_size("tile"), lax.axis_size("sub")
    matrices, table, links, inward = ghost_tables(side, slots, tiles_n)
    scale = 1.0 / math.sqrt(slots * tiles_n * pixels)
    width = DEPTH * side
    vmem = pl.BlockSpec(memory_space=pltpu.VMEM)
    hbm = pl.BlockSpec(memory_space=pltpu.HBM)
    dma = pltpu.SemaphoreType.DMA
    bf16, f32 = jnp.bfloat16, jnp.float32
    held = slots * 4 + tiles_n * links[0]
    held_outs = pl.pallas_call(
        functools.partial(face_kernel, (slots, tiles_n, subs, side, links, scale)),
        out_shape=(
            pltpu.VMEM(features.shape, bf16),
            pltpu.VMEM((K, chans, filters.shape[2]), f32),
        ),
        in_specs=[hbm] * 7,
        out_specs=(vmem, vmem),
        scratch_shapes=[
            pltpu.VMEM((2,) + features.shape, bf16),
            pltpu.VMEM((subs,) + features.shape, bf16),
            pltpu.VMEM((slots * 4, chans, width), bf16),
            pltpu.VMEM((slots * 4, chans, width), bf16),
            pltpu.VMEM((tiles_n - 1, links[0], chans, width), bf16),
            pltpu.VMEM((tiles_n - 1, links[0], chans, width), bf16),
            pltpu.VMEM((held, chans, width), bf16),
            pltpu.VMEM((subs, held, chans, width), bf16),
            pltpu.VMEM((2, chans, width), f32),
            pltpu.VMEM((tiles_n, 2, chans, width), f32),
            pltpu.VMEM((slots, chans, pixels), f32),
            pltpu.VMEM((slots, chans * subs, DEPTH * width), f32),
            pltpu.VMEM((2,) + matrices.shape[1:], bf16),
            pltpu.VMEM(inward.shape, bf16),
            pltpu.VMEM((pixels, 2 * width), bf16),
            pltpu.VMEM(filters.shape, bf16),
            pltpu.SMEM(tile_map.shape, jnp.int32),
            pltpu.SMEM(table.shape, jnp.int32),
            pltpu.SemaphoreType.REGULAR,
            dma((9,)),
        ]
        + [dma] * 12,
        compiler_params=pltpu.CompilerParams(
            collective_id=0, has_side_effects=True, vmem_limit_bytes=67043328 - 512 * 1024
        ),
    )(
        features,
        out_grad,
        filters,
        tile_map,
        jnp.asarray(table),
        jnp.asarray(matrices, bf16),
        jnp.asarray(inward, bf16),
    )
    held_outs = [pltpu.with_memory_space_constraint(value, pltpu.VMEM) for value in held_outs]
    return pl.pallas_call(
        store_kernel,
        out_shape=(
            jax.ShapeDtypeStruct(features.shape, bf16),
            jax.ShapeDtypeStruct((K, chans, filters.shape[2]), f32),
        ),
        in_specs=[vmem] * 2,
        out_specs=(hbm, hbm),
        scratch_shapes=[dma((2,))],
    )(*held_outs)


def on_device(features, out_grad, filters, tile_map):
    slots, chans, pixels = features.shape
    side = math.isqrt(pixels)
    whole_faces = slots * lax.axis_size("tile") == 12
    channels = chans * lax.axis_size("sub")
    if whole_faces and 1 < slots < 5 and DEPTH * side == 128 and chans % 8 == 0 and channels == 32:
        return face_path(features, out_grad, filters, tile_map)
    return general_path(features, out_grad, filters, tile_map)


def solution(mesh):
    placed = (P(("grp", "tile"), "sub", None), P(("grp", "tile"), "sub", None), P(), P())
    return jax.shard_map(
        on_device,
        mesh=mesh,
        in_specs=placed,
        out_specs=(P(("grp", "tile"), "sub", None), P("grp", "sub", None)),
        check_vma=False,
    )
```

```python
import functools
import math

import jax
import jax.numpy as jnp
import numpy as np
from jax import lax
from jax.experimental import pallas as pl
from jax.experimental.pallas import tpu as pltpu
from jax.sharding import PartitionSpec as P

K = 5


def from_behind(value, axis, steps):
    count = lax.axis_size(axis)
    pairs = [(source, (source + steps) % count) for source in range(count)]
    return lax.ppermute(value, axis, pairs)


def tile_coords(nested_code, bit_count):
    coord_x = nested_code * 0
    coord_y = nested_code * 0
    for bit_level in range(bit_count):
        coord_x = coord_x + nested_code // 4**bit_level % 2 * 2**bit_level
        coord_y = coord_y + nested_code // (2 * 4**bit_level) % 2 * 2**bit_level
    return (coord_x, coord_y)


def nested_index(coord_x, coord_y, bit_count):
    nested_code = coord_x * 0
    for bit_level in range(bit_count):
        nested_code = nested_code + coord_x // 2**bit_level % 2 * 4**bit_level
        nested_code = nested_code + coord_y // 2**bit_level % 2 * (2 * 4**bit_level)
    return nested_code


def pick(condition, when_true, when_false):
    return when_false + (when_true - when_false) * condition


def neighbour_codes(tile_ids, per_face, side_count):
    bit_count = side_count.bit_length() - 1
    face_id = tile_ids // per_face
    coord_x, coord_y = tile_coords(tile_ids % per_face, bit_count)
    column = face_id % 4
    is_north = face_id < 4
    is_south = face_id >= 8
    last_tile = side_count - 1

    def by_cycle(north_value, equator_value, south_value):
        return pick(is_north, north_value, pick(is_south, south_value, equator_value))

    side_rules = [
        (
            coord_x > 0,
            (face_id, coord_x - 1, coord_y, 1),
            (
                by_cycle(4 + column, 8 + (column + 3) % 4, 8 + (column + 3) % 4),
                by_cycle(last_tile, last_tile, coord_y),
                by_cycle(coord_y, coord_y, 0),
                by_cycle(1, 1, 2),
            ),
        ),
        (
            coord_x < last_tile,
            (face_id, coord_x + 1, coord_y, 0),
            (
                by_cycle((column + 1) % 4, column, 4 + (column + 1) % 4),
                by_cycle(coord_y, 0, 0),
                by_cycle(last_tile, coord_y, coord_y),
                by_cycle(3, 0, 0),
            ),
        ),
        (
            coord_y > 0,
            (face_id, coord_x, coord_y - 1, 3),
            (
                by_cycle(4 + (column + 1) % 4, 8 + column, 8 + (column + 1) % 4),
                by_cycle(coord_x, coord_x, 0),
                by_cycle(last_tile, last_tile, coord_x),
                by_cycle(3, 3, 0),
            ),
        ),
        (
            coord_y < last_tile,
            (face_id, coord_x, coord_y + 1, 2),
            (
                by_cycle((column + 3) % 4, (column + 3) % 4, 4 + column),
                by_cycle(last_tile, coord_x, coord_x),
                by_cycle(coord_x, 0, 0),
                by_cycle(1, 2, 2),
            ),
        ),
    ]
    target_list = []
    edge_list = []
    for inside, within, across in side_rules:
        chosen = [
            pick(inside, near_value, far_value) for near_value, far_value in zip(within, across)
        ]
        target_list.append(chosen[0] * per_face + nested_index(chosen[1], chosen[2], bit_count))
        edge_list.append(chosen[3] + tile_ids * 0)
    return (target_list, edge_list)


def neighbour_table(tile_map, per_face, side_count):
    target_list, edge_list = neighbour_codes(tile_map, per_face, side_count)
    targets = jnp.stack(target_list, axis=1).astype(jnp.int32)
    edges = jnp.stack(edge_list, axis=1).astype(jnp.int32)
    slot_of = jnp.argsort(tile_map).astype(jnp.int32)
    return (slot_of[targets].astype(jnp.int32), edges)


def peer_offsets(slot_count, device_count, per_face, side_count):
    tile_ids = np.arange(slot_count * device_count, dtype=np.int64)
    target_list, edge_list = neighbour_codes(tile_ids, per_face, side_count)
    targets = np.stack(target_list, axis=1)
    offsets = (tile_ids[:, None] // slot_count - targets // slot_count) % device_count
    distinct = sorted(set((int(value) for value in offsets.ravel())) - {0})
    position = np.zeros(device_count, dtype=np.int32)
    for order, value in enumerate(distinct):
        position[value] = order + 1
    return (distinct, position)


def edge_lines(values, tile_side):
    return jnp.stack(
        [
            values[..., :tile_side],
            values[..., -tile_side:],
            values[..., ::tile_side],
            values[..., tile_side - 1 :: tile_side],
        ],
        axis=1,
    )


def stencil(values, ghosts, tile_side):
    position = jnp.arange(values.shape[-1]) % tile_side
    zero_line = jnp.zeros_like(values[..., :1])
    upper_side = jnp.concatenate([ghosts[:, 0], values[..., :-tile_side]], axis=-1)
    lower_side = jnp.concatenate([values[..., tile_side:], ghosts[:, 1]], axis=-1)
    left_side = jnp.where(
        position == 0,
        jnp.repeat(ghosts[:, 2], tile_side, axis=-1),
        jnp.concatenate([zero_line, values[..., :-1]], axis=-1),
    )
    right_side = jnp.where(
        position == tile_side - 1,
        jnp.repeat(ghosts[:, 3], tile_side, axis=-1),
        jnp.concatenate([values[..., 1:], zero_line], axis=-1),
    )
    return -0.25 * (upper_side + lower_side + left_side + right_side)


def tile_total(filter_part):
    return lax.psum(filter_part, "tile")


def general_path(features, out_grad, filters, tile_map):
    slot_count = features.shape[0]
    group_channels = features.shape[1]
    tile_side = math.isqrt(features.shape[2])
    device_count = lax.axis_size("tile")
    total_tiles = slot_count * device_count
    side_count = math.isqrt(total_tiles // 12)
    scale_factor = 1.0 / math.sqrt(total_tiles * features.shape[2])
    highest = lax.Precision.HIGHEST
    slot_table, edge_table = neighbour_table(tile_map, total_tiles // 12, side_count)
    my_device = lax.axis_index("tile")
    first_slot = my_device * slot_count
    my_slots = lax.dynamic_slice_in_dim(slot_table, first_slot, slot_count, 0)
    my_edges = lax.dynamic_slice_in_dim(edge_table, first_slot, slot_count, 0)
    channel_start = lax.axis_index("sub") * group_channels
    weights = filters.astype(jnp.float32)
    distinct, position = peer_offsets(slot_count, device_count, total_tiles // 12, side_count)
    sender_gap = (my_device - my_slots // slot_count) % device_count
    local_rows = jnp.asarray(position)[sender_gap] * slot_count + my_slots % slot_count

    def laplace(values):
        border = edge_lines(values, tile_side).reshape(slot_count, 4, group_channels * tile_side)
        received = [border]
        for offset_value in distinct:
            received.append(from_behind(border, "tile", offset_value))
        stacked = jnp.concatenate(received, axis=0)
        stacked = stacked.reshape(stacked.shape[0], 4, group_channels, tile_side)
        rows = []
        for slot in range(slot_count):
            for side in range(4):
                start = (local_rows[slot, side], my_edges[slot, side], 0, 0)
                rows.append(
                    lax.dynamic_slice(stacked, start, (1, 1, group_channels, tile_side))
                )
        ghosts = jnp.concatenate(rows, axis=0)
        ghosts = ghosts.reshape(slot_count, 4, group_channels, tile_side)
        return stencil(values, ghosts, tile_side)

    whole_grad = lax.all_gather(out_grad, "sub", axis=1, tiled=True)
    cotangent = whole_grad.astype(jnp.float32)
    inputs = features.astype(jnp.float32)
    previous, current = (inputs, laplace(inputs))
    filter_terms = [
        jnp.einsum("sip,sop->io", inputs, cotangent, precision=highest),
        jnp.einsum("sip,sop->io", current, cotangent, precision=highest),
    ]
    for degree in range(2, K):
        previous, current = (current, 2.0 * laplace(current) - previous)
        filter_terms.append(jnp.einsum("sip,sop->io", current, cotangent, precision=highest))
    weight_grad = tile_total(jnp.stack(filter_terms)) * scale_factor
    row_block = lax.dynamic_slice_in_dim(weights, channel_start, group_channels, 1)

    def mixed(degree):
        return jnp.einsum("sop,io->sip", cotangent, row_block[degree], precision=highest)

    next_sum = mixed(K - 1)
    after_next = jnp.zeros_like(next_sum)
    for degree in range(K - 2, 0, -1):
        next_sum, after_next = (mixed(degree) + 2.0 * laplace(next_sum) - after_next, next_sum)
    in_grad = (mixed(0) + laplace(next_sum) - after_next).astype(jnp.bfloat16)
    return (in_grad, weight_grad)


DEPTH = K - 1
GHOST_SIDES = (0, 2, 3, 1)
OUTSIDE = 6


def face_graph(tile_side):
    tile_ids = np.arange(12, dtype=np.int64)
    target_list, edge_list = neighbour_codes(tile_ids, 1, 1)
    targets = np.stack(target_list, axis=1)
    edges = np.stack(edge_list, axis=1)
    pixels = tile_side * tile_side
    grid = np.arange(pixels).reshape(tile_side, tile_side)
    lines = [grid[0], grid[-1], grid[:, 0], grid[:, -1]]
    ghosts = np.zeros((12, 4, tile_side), dtype=np.int64)
    around = np.zeros((12, 4, tile_side, tile_side), dtype=np.int64)
    for tile in range(12):
        for side in range(4):
            ghosts[tile, side] = targets[tile, side] * pixels + lines[edges[tile, side]]
        whole = tile * pixels + grid
        around[tile, 0] = np.concatenate([ghosts[tile, 0][None], whole[:-1]], 0)
        around[tile, 1] = np.concatenate([whole[1:], ghosts[tile, 1][None]], 0)
        around[tile, 2] = np.concatenate([ghosts[tile, 2][:, None], whole[:, :-1]], 1)
        around[tile, 3] = np.concatenate([whole[:, 1:], ghosts[tile, 3][:, None]], 1)
    around = around.transpose(0, 2, 3, 1).reshape(12 * pixels, 4)
    return targets, edges, ghosts, around


@functools.lru_cache(None)
def ghost_tables(tile_side, slots, tiles_n):
    targets, edges, ghosts, around = face_graph(tile_side)
    pixels = tile_side * tile_side
    grid = np.arange(pixels).reshape(tile_side, tile_side)
    strips = np.stack(
        [
            grid[:DEPTH].ravel(),
            grid[-DEPTH:].ravel(),
            grid[:, :DEPTH].T.ravel(),
            grid[:, -DEPTH:].T.ravel(),
        ]
    )
    sources_of = []
    by_class = []
    for tile in range(12):
        wanted = np.concatenate([ghosts[tile, side] for side in GHOST_SIDES])
        power = np.zeros((wanted.size, 12 * pixels), dtype=np.int32)
        power[np.arange(wanted.size), wanted] = 1
        powers = [power]
        for _ in range(DEPTH - 1):
            powers.append(sum(powers[-1][:, around[:, side]] for side in range(4)))
        rows = np.concatenate(
            [powers[0], powers[1], powers[2] - 8 * powers[0], powers[3] - 12 * powers[1]]
        )
        support = np.flatnonzero(np.any(rows != 0, axis=0))
        sources = [(int(targets[tile, side]), int(edges[tile, side])) for side in range(4)]
        own = [(tile, side) for side in range(4)]
        covered = set(int(t) * pixels + int(p) for t, e in sources + own for p in strips[e])
        left = [int(p) for p in support if int(p) not in covered]
        corner_tiles = {}
        for pixel in left:
            corner_tiles.setdefault(pixel // pixels, []).append(pixel % pixels)
        first = lambda t: int(
            np.flatnonzero(np.any(rows[:, [t * pixels + p for p in corner_tiles[t]]] != 0, axis=1))[0]
        )
        for other in sorted(corner_tiles, key=first):
            choice = [e for e in range(4) if set(corner_tiles[other]) <= set(strips[e].tolist())]
            sources.append((other, choice[0]))
        assert len(sources) <= OUTSIDE
        while len(sources) < OUTSIDE:
            sources.append(sources[-1])
        sources_of.append(sources)
        lanes = np.concatenate([t * pixels + strips[e] for t, e in sources + own])
        seen, keep = set(), np.zeros(lanes.size, dtype=bool)
        for lane, pixel in enumerate(lanes.tolist()):
            keep[lane] = pixel not in seen
            seen.add(pixel)
        assert set(support.tolist()) <= seen
        matrix = (rows[:, lanes] * keep[None]).T
        assert np.abs(matrix).max() <= 127
        if tile % 4 == 0:
            by_class.append(matrix)
        else:
            assert np.array_equal(matrix, by_class[-1])
    wanted = {}
    for tile in range(12):
        for t, e in sources_of[tile]:
            pair = (t // slots, tile // slots)
            if pair[0] != pair[1]:
                held = wanted.setdefault(pair, [])
                if (t, e) not in held:
                    held.append((t, e))
    packed = max(len(held) for held in wanted.values())
    send = np.zeros((tiles_n, tiles_n, packed), dtype=np.int32)
    for (q, p), held in wanted.items():
        for order, (t, e) in enumerate(held):
            send[q, p, order] = (t - q * slots) * 4 + e
    take_from = np.zeros((12, OUTSIDE), dtype=np.int32)
    for tile in range(12):
        for order, (t, e) in enumerate(sources_of[tile]):
            q, p = t // slots, tile // slots
            if q == p:
                take_from[tile, order] = (t - q * slots) * 4 + e
            else:
                at = wanted[(q, p)].index((t, e))
                take_from[tile, order] = slots * 4 + q * packed + at
    table = np.concatenate([take_from.ravel(), send.ravel()])
    counts = tuple(len(wanted.get((q, 0), ())) for q in range(tiles_n))
    far = []
    for tile in range(slots):
        for order, (t, e) in enumerate(sources_of[tile]):
            if t // slots == tiles_n - 1 and (t, e) not in sources_of[tile][:order]:
                far.append((tile, order, int(take_from[tile, order])))
    spread = np.zeros((4, tile_side, tile_side, tile_side))
    step = np.arange(tile_side)
    spread[0, step, 0, step] = 1
    spread[1, step, step, 0] = 1
    spread[2, step, step, -1] = 1
    spread[3, step, -1, step] = 1
    local = np.zeros((pixels, pixels))
    for u in range(tile_side):
        for v in range(tile_side):
            for du, dv in ((1, 0), (-1, 0), (0, 1), (0, -1)):
                if 0 <= u + du < tile_side and 0 <= v + dv < tile_side:
                    local[grid[u, v], grid[u + du, v + dv]] = -0.25
    inward = [-0.25 * spread.reshape(4 * tile_side, pixels)]
    inward.append(2.0 * inward[0] @ local)
    for _ in range(DEPTH - 2):
        inward.append(2.0 * inward[-1] @ local - inward[-2])
    inward = np.concatenate(inward)
    assert np.array_equal(inward, inward.astype(jnp.bfloat16).astype(np.float64))
    return np.stack(by_class), table, (packed, counts, len(wanted.get((0, tiles_n - 1), ())), tuple(far)), inward


def split(value):
    high = value.astype(jnp.bfloat16).astype(jnp.float32)
    return high, value - high


def product(left, right):
    return lax.dot_general(
        left, right, (((1,), (1,)), ((), ())), preferred_element_type=jnp.float32
    )


def face_kernel(
    sizes,
    x_hbm,
    g_hbm,
    f_hbm,
    map_hbm,
    table_hbm,
    ghost_hbm,
    inward_hbm,
    in_ref,
    w_ref,
    xg_ref,
    g_all,
    x_mine,
    g_mine,
    x_pack,
    g_pack,
    x_ext,
    g_ext,
    block,
    block_in,
    result,
    g_lines_own,
    x_lines_ref,
    ghost,
    inward,
    take,
    f_ref,
    map_ref,
    table_ref,
    ready,
    load_sem,
    x_send,
    x_recv,
    s_send,
    s_recv,
    g_send,
    g_recv,
    d_send,
    d_recv,
    f_send,
    f_recv,
    w_send,
    w_recv,
):
    slots, tiles_n, subs, side, (packed, counts, far_count, far), scale = sizes
    x_ref, g_ref = xg_ref.at[0], xg_ref.at[1]
    chans = x_ref.shape[1]
    total = subs * chans
    pixels = side * side
    width = DEPTH * side
    rows = slots * chans
    bf16, f32 = jnp.bfloat16, jnp.float32
    j = lax.axis_index("tile")
    s = lax.axis_index("sub")
    tile_peers = []
    for d in range(tiles_n - 1):
        up = d + (j <= d).astype(jnp.int32)
        back = tiles_n - 2 - d
        down = back + (j <= back).astype(jnp.int32)
        tile_peers.append(jnp.where(2 * j < tiles_n, down, up))
    core_peer = s + 1 - 2 * lax.rem(s, 2)
    sub_peers = [lax.rem(s + 2, subs), lax.rem(core_peer + 2, subs), core_peer]
    friends = len(tile_peers) + len(sub_peers)
    head = j == 0
    tail = j == tiles_n - 1
    kinds = [(slots * j + m) // 4 for m in range(slots)]

    def greet(friend):
        pl.semaphore_signal(
            pltpu.get_barrier_semaphore(),
            inc=1,
            device_id=friend,
            device_id_type=pl.DeviceIdType.MESH,
        )

    first_loads = [
        pltpu.make_async_copy(x_hbm, x_ref, load_sem.at[0]),
        pltpu.make_async_copy(g_hbm, g_ref, load_sem.at[0]),
        pltpu.make_async_copy(map_hbm, map_ref, load_sem.at[2]),
        pltpu.make_async_copy(table_hbm, table_ref, load_sem.at[3]),
    ]
    barrier = pltpu.get_barrier_semaphore()
    for peer in sub_peers:
        greet({"sub": peer})
    for d, peer in enumerate(tile_peers):

        @pl.when(jnp.logical_not(tail & (peer == 0)))
        def _():
            greet({"tile": peer})

    for copy in first_loads:
        copy.start()

    one_kind = kinds[0] == kinds[-1]
    loads = [
        pltpu.make_async_copy(ghost_hbm.at[kinds[0]], ghost.at[0], load_sem.at[4]),
        pltpu.make_async_copy(inward_hbm, inward, load_sem.at[5]),
        pltpu.make_async_copy(f_hbm, f_ref, load_sem.at[6]),
        pltpu.make_async_copy(g_hbm, g_all.at[s], load_sem.at[7]),
    ]
    second = pltpu.make_async_copy(ghost_hbm.at[kinds[-1]], ghost.at[1], load_sem.at[8])
    for copy in loads:
        copy.start()
    pl.when(jnp.logical_not(one_kind))(second.start)

    @pl.when(head)
    def _():
        for peer in tile_peers:
            for other in sub_peers:
                greet({"tile": peer, "sub": other})

    def remote(source, target, send, recv, device):
        return pltpu.make_async_remote_copy(
            source,
            target,
            send,
            recv,
            device_id=device,
            device_id_type=pl.DeviceIdType.MESH,
        )

    def g_copy(d, sender, peer):
        return remote(g_hbm, g_all.at[sender], g_send, g_recv, {"sub": peer})

    def open_up():
        pl.semaphore_wait(barrier, friends + jnp.where(head, -1, subs - 1))

    base = slots * j
    column = lax.broadcasted_iota(jnp.int32, (pixels, 2 * width), 1)
    wanted_pixel = column % side * side + column % width // side
    wanted_pixel = wanted_pixel + jnp.where(column < width, 0, side - DEPTH)
    pixel = lax.broadcasted_iota(jnp.int32, (pixels, 2 * width), 0)
    take[...] = jnp.where(pixel == wanted_pixel, 1.0, 0.0).astype(bf16)
    pltpu.make_async_copy(xg_ref, xg_ref, load_sem.at[0]).wait()
    for copy in first_loads[2:]:
        copy.wait()

    def slot_of(m):
        found = 0
        for slot in range(1, slots):
            found = jnp.where(map_ref[base + slot] == base + m, slot, found)
        return found

    slot_list = [slot_of(m) for m in range(slots)]
    x_own = jnp.concatenate([x_ref[slot_list[m]].astype(f32) for m in range(slots)], axis=0)
    g_own = jnp.concatenate([g_ref[slot_list[m]].astype(f32) for m in range(slots)], axis=0)
    both = jnp.concatenate([x_own, g_own], axis=0).astype(bf16)
    cut = jnp.dot(both, take[...], preferred_element_type=f32)

    def strips_of(value, cut_value):
        return [
            value[:, :width],
            value[:, pixels - width :],
            cut_value[:, :width],
            cut_value[:, width:],
        ]

    x_strips = strips_of(x_own, cut[:rows])
    g_strips = strips_of(g_own, cut[rows:])
    for m in range(slots):
        at = slice(m * chans, (m + 1) * chans)
        for e in range(4):
            x_mine[m * 4 + e] = x_strips[e][at].astype(bf16)
            g_mine[m * 4 + e] = g_strips[e][at].astype(bf16)
    sends = 12 * OUTSIDE
    for d, peer in enumerate(tile_peers):
        for i in range(packed):
            index = table_ref[sends + (j * tiles_n + peer) * packed + i]
            x_pack[d, i] = x_mine[index]
            g_pack[d, i] = g_mine[index]
    for m in range(slots):
        at = slice(m * chans, (m + 1) * chans)
        for e in range(4):
            x_ext[m * 4 + e] = x_strips[e][at].astype(bf16)

    def landing(sender):
        return pl.ds(slots * 4 + sender * packed, packed)

    def x_copy(d, sender, peer):
        return remote(
            x_pack.at[d], x_ext.at[landing(sender)], x_send, x_recv, {"tile": peer}
        )

    def strip_copy(d, sender, peer):
        return remote(
            g_pack.at[d],
            g_ext.at[s, landing(sender)],
            s_send,
            s_recv,
            {"tile": peer},
        )

    def forward_copy(q, d, sender, peer):
        held = g_ext.at[sender, landing(q)]
        return remote(held, held, f_send, f_recv, {"sub": peer})

    def block_copy(d, sender, peer):
        return remote(block, block_in.at[sender], w_send, w_recv, {"tile": peer})

    def x_crosses(sender, peer):
        return jnp.logical_not((sender == 0) & (peer == tiles_n - 1))

    def direct_copy(q, d, sender, peer):
        at = 0 if 2 * q >= tiles_n else tiles_n - 2
        return remote(
            g_pack.at[at, pl.ds(0, counts[q])],
            g_ext.at[sender, pl.ds(slots * 4 + q * packed, counts[q])],
            d_send,
            d_recv,
            {"tile": 0, "sub": peer},
        )

    def far_copy(peer):
        return remote(
            g_pack.at[0, pl.ds(0, far_count)],
            g_ext.at[s, pl.ds(slots * 4, far_count)],
            d_send,
            d_recv,
            {"tile": tiles_n - 1, "sub": peer},
        )

    def await_bytes(held, semaphore):
        pltpu.make_async_copy(held, held, semaphore).wait()

    def first_strips(rows_of, count):
        return g_ext.at[pl.ds(0, rows_of), pl.ds(0, count)]

    def for_direct(action):
        for q in range(1, tiles_n):

            @pl.when(j == q)
            def _():
                for d, peer in enumerate([s] + sub_peers):
                    action(direct_copy(q, d, s, peer))

    def send_strips():
        for_direct(lambda copy: copy.start())
        for d, peer in enumerate(tile_peers):
            pl.when((peer != 0) & x_crosses(j, peer))(strip_copy(d, j, peer).start)

    @pl.when(tail)
    def _():
        x_ext[landing(0)] = jnp.zeros((packed, chans, width), bf16)


    lane = lax.broadcasted_iota(jnp.int32, (rows, pixels), 1)
    y_at = lane % side

    def around(value):
        out = jnp.where(lane < side, 0.0, pltpu.roll(value, side, 1))
        out = out + jnp.where(lane >= pixels - side, 0.0, pltpu.roll(value, pixels - side, 1))
        out = out + jnp.where(y_at == 0, 0.0, pltpu.roll(value, 1, 1))
        return out + jnp.where(y_at == side - 1, 0.0, pltpu.roll(value, pixels - 1, 1))

    def of_slot(value, m, count):
        return value[m * count : (m + 1) * count]

    open_up()
    for d, peer in enumerate(tile_peers):
        pl.when(x_crosses(j, peer))(x_copy(d, j, peer).start)
    for d, peer in enumerate(sub_peers):
        g_copy(d, s, peer).start()
    send_strips()

    @pl.when(tail)
    def _():
        for other in [s] + sub_peers:
            pl.semaphore_signal(
                ready,
                inc=1,
                device_id={"tile": 0, "sub": other},
                device_id_type=pl.DeviceIdType.MESH,
            )

    chain = [x_own, -0.25 * around(x_own)]
    for k in range(2, K):
        chain.append(-0.5 * around(chain[k - 1]) - chain[k - 2])

    for copy in loads:
        copy.wait()
    pl.when(jnp.logical_not(one_kind))(second.wait)
    outer = OUTSIDE * width
    mid_first = [kinds[m] == kinds[0] for m in range(slots)]
    scales = (1.0, -0.5, 0.25, -0.125)

    def ghost_lines(value, at, count, single=False):
        first = jnp.dot(value, ghost[0, at], preferred_element_type=f32)
        if single:
            return [of_slot(first, m, count) for m in range(slots)]
        last = jnp.dot(value, ghost[1, at], preferred_element_type=f32)
        return [
            jnp.where(mid_first[m], of_slot(first, m, count), of_slot(last, m, count))
            for m in range(slots)
        ]

    x_inner = ghost_lines(
        jnp.concatenate(x_strips, axis=1).astype(bf16), slice(outer, outer + 4 * width), chans
    )

    x_edge = product(x_own.astype(bf16), inward[...])
    filters = jnp.concatenate([f_ref[k].astype(f32) for k in range(K)], axis=1).astype(bf16)
    pick_row = lax.broadcasted_iota(jnp.int32, (chans, total), 0) + chans * s
    pick_col = lax.broadcasted_iota(jnp.int32, (chans, total), 1)
    mine = jnp.dot(
        jnp.where(pick_row == pick_col, 1.0, 0.0).astype(bf16),
        filters,
        preferred_element_type=f32,
    )
    mixing = jnp.concatenate(
        [mine[:, k * total : (k + 1) * total] for k in range(K)], axis=0
    ).astype(bf16)
    outside = []
    for m in range(DEPTH):
        pieces = [mine[:, (m + 1) * total :]]
        if m > 0:
            pieces.append(jnp.zeros((chans, m * total), f32))
        outside.append(jnp.concatenate(pieces, axis=1))
    outside = jnp.concatenate(outside, axis=0)
    outside = jnp.concatenate([outside, outside], axis=1).astype(bf16)

    def load_g():
        return [
            jnp.concatenate([g_all[e, slot_list[m]].astype(f32) for e in range(subs)], axis=0)
            for m in range(slots)
        ]

    def await_g():
        await_bytes(g_all.at[pl.ds(0, subs - 1)], g_recv)

    def local_part(single):
        g_full = load_g()
        g_bf = [value.astype(bf16) for value in g_full]
        mixed = [jnp.dot(mixing, g_bf[m], preferred_element_type=f32) for m in range(slots)]
        grads = [
            jnp.concatenate([of_slot(mixed[m], k, chans) for m in range(slots)], axis=0)
            for k in range(K)
        ]
        after, upper = grads[K - 1], grads[K - 2] - 0.5 * around(grads[K - 1])
        for k in range(K - 3, 0, -1):
            after, upper = upper, grads[k] - 0.5 * around(upper) - after
        inner = grads[0] - 0.25 * around(upper) - after

        for m in range(slots):
            result[m] = of_slot(inner, m, chans)
        whole = jnp.concatenate(g_full, axis=0)
        whole_strips = strips_of(
            whole, jnp.dot(whole.astype(bf16), take[...], preferred_element_type=f32)
        )
        for m in range(slots):
            for e in range(subs):
                at = slice(m * total + e * chans, m * total + (e + 1) * chans)
                for side_at in range(4):
                    g_ext[e, m * 4 + side_at] = whole_strips[side_at][at].astype(bf16)
        g_inner = ghost_lines(
            jnp.concatenate(whole_strips, axis=1).astype(bf16),
            slice(outer, outer + 4 * width),
            total,
            single,
        )
        for m in range(slots):
            g_lines_own[m] = g_inner[m]

    @pl.when(head)
    def _():
        await_g()
        pl.semaphore_wait(ready, subs)
        for peer in [s] + sub_peers:
            far_copy(peer).start()
        local_part(True)


    @pl.when(tail)
    def _():
        await_bytes(x_ext.at[pl.ds(0, (tiles_n - 2) * packed)], x_recv)

    @pl.when(jnp.logical_not(tail))
    def _():
        await_bytes(x_ext.at[pl.ds(0, (tiles_n - 1) * packed)], x_recv)

    def pass_on():
        @pl.when(tail)
        def _():
            await_bytes(g_ext.at[0, pl.ds(0, (tiles_n - 2) * packed)], s_recv)

        @pl.when(jnp.logical_not(tail))
        def _():
            await_bytes(g_ext.at[0, pl.ds(0, (tiles_n - 1) * packed)], s_recv)

        for q, peer in enumerate(tile_peers):

            @pl.when(x_crosses(peer, j))
            def _():
                for d, other in enumerate(sub_peers):
                    forward_copy(peer, d, s, other).start()

    wanted = [
        [table_ref[(base + m) * OUTSIDE + r] for r in range(OUTSIDE)] for m in range(slots)
    ]

    def outer_strips(read):
        return jnp.concatenate(
            [
                jnp.concatenate([read(wanted[m][r]).astype(f32) for r in range(OUTSIDE)], axis=1)
                for m in range(slots)
            ],
            axis=0,
        )

    def by_power(lines):
        return jnp.concatenate(
            [
                lines[:, n * width : (n + 1) * width] * scales[n] for n in range(DEPTH)
            ],
            axis=0,
        )

    half = DEPTH * chans

    def by_degree(across):
        across = across[:half] + across[half:]
        across = across[:, : DEPTH * total] + across[:, DEPTH * total :]
        place = lax.broadcasted_iota(jnp.int32, (chans, DEPTH * total), 1)
        out = of_slot(across, 0, chans)
        for n in range(1, DEPTH):
            shifted = pltpu.roll(of_slot(across, n, chans), n * total, 1)
            out = out + jnp.where(place < n * total, 0.0, shifted)
        return out

    x_outer = outer_strips(lambda index: x_ext[index]).astype(bf16)

    def find_lines(single):
        found = ghost_lines(x_outer, slice(0, outer), chans, single)
        for m in range(slots):
            x_lines_ref[m] = found[m] + x_inner[m]

    pl.when(one_kind)(functools.partial(find_lines, True))
    pl.when(jnp.logical_not(one_kind))(functools.partial(find_lines, False))
    x_lines = [by_power(x_lines_ref[m]) for m in range(slots)]
    entering = []
    for k in range(1, K):
        for m in range(slots):
            pieces = [of_slot(x_lines[m], k - 1 - n, chans) for n in range(k)]
            if k < DEPTH:
                pieces.append(jnp.zeros((chans, (DEPTH - k) * width), f32))
            entering.append(jnp.concatenate(pieces, axis=1))
    high, low = split(jnp.concatenate(entering, axis=0))
    entering = jnp.concatenate([high, low[rows:]], axis=0)
    entering = jnp.dot(entering.astype(bf16), inward[...], preferred_element_type=f32)
    held = [x_own]
    for k in range(1, K):
        full = chain[k] + of_slot(entering, k - 1, rows)
        if k > 1:
            full = full + of_slot(entering, K - 3 + k, rows)
        held += list(split(full))
    terms = [
        jnp.concatenate([of_slot(value, m, chans) for value in held], axis=0).astype(bf16)
        for m in range(slots)
    ]
    pl.when(jnp.logical_not(head))(await_g)
    g_bf = [value.astype(bf16) for value in load_g()]
    grad = product(terms[0], g_bf[0])
    for m in range(1, slots):
        grad = grad + product(terms[m], g_bf[m])
    later = [
        of_slot(grad, 2 * k - 1, chans) + of_slot(grad, 2 * k, chans) for k in range(1, K)
    ]
    block[0] = jnp.concatenate(later, axis=1) * scale
    block[1] = jnp.concatenate(
        [grad[:chans] * scale, jnp.zeros((chans, width - total), f32)], axis=1
    )

    def send_blocks():
        for d, peer in enumerate(tile_peers):
            block_copy(d, j, peer).start()

    @pl.when(j != 0)
    def _():
        send_blocks()
        pass_on()
        local_part(False)


    def finish(single):
        if single:

            @pl.when(tail)
            def _():
                await_bytes(first_strips(subs, far_count), d_recv)
                await_bytes(first_strips(subs - 1, (tiles_n - 2) * packed), f_recv)

        @pl.when((j != 0) & jnp.logical_not(tail))
        def _():
            await_bytes(first_strips(subs - 1, (tiles_n - 1) * packed), f_recv)

        @pl.when(head)
        def _():
            await_bytes(first_strips(subs, sum(counts[1:])), d_recv)

        if single and far:
            far_lines, far_edge = [], []
            for m, r, index in far:
                held = jnp.concatenate(
                    [g_ext[e, index].astype(f32) for e in range(subs)], axis=0
                ).astype(bf16)
                rows_at = ghost[m // 4, r * width : (r + 1) * width]
                far_lines.append(by_power(jnp.dot(held, rows_at, preferred_element_type=f32)))
                mine_edge = of_slot(x_edge, m, chans)
                far_edge.append(
                    jnp.concatenate(
                        [mine_edge[:, n * width : (n + 1) * width] for n in range(DEPTH)], axis=0
                    )
                )
            far_lines = jnp.concatenate(split(jnp.concatenate(far_lines, axis=1)), axis=0)
            far_edge = jnp.concatenate(split(jnp.concatenate(far_edge, axis=1)), axis=0)
            crossed = by_degree(product(far_edge.astype(bf16), far_lines.astype(bf16)))
        if single:

            @pl.when(head)
            def _():
                if far:
                    block[0] = block[0] + crossed * scale
                send_blocks()

        gathered = outer_strips(
            lambda index: jnp.concatenate([g_ext[e, index].astype(f32) for e in range(subs)], axis=0)
        )
        g_lines = ghost_lines(gathered.astype(bf16), slice(0, outer), total, single)
        g_lines = jnp.concatenate(
            [by_power(g_lines[m] + g_lines_own[m]) for m in range(slots)], axis=1
        )
        mixed = jnp.dot(
            outside,
            jnp.concatenate(split(g_lines), axis=0).astype(bf16),
            preferred_element_type=f32,
        )
        mixed = jnp.concatenate(
            [
                jnp.concatenate(
                    [
                        of_slot(mixed, n, chans)[:, m * width : (m + 1) * width]
                        for n in range(DEPTH)
                    ],
                    axis=1,
                )
                for m in range(slots)
            ],
            axis=0,
        )
        spread = jnp.dot(
            jnp.concatenate(split(mixed), axis=0).astype(bf16),
            inward[...],
            preferred_element_type=f32,
        )
        inner = spread[:rows] + spread[rows:]
        for m in range(slots):
            result[m] = result[m] + of_slot(inner, m, chans)
        for slot in range(slots):
            in_ref[slot] = result[lax.rem(map_ref[base + slot], slots)].astype(bf16)
    pl.when(one_kind)(functools.partial(finish, True))
    pl.when(jnp.logical_not(one_kind))(functools.partial(finish, False))

    await_bytes(block_in.at[pl.ds(0, tiles_n - 1)], w_recv)
    block_in[j] = block[...]
    summed = block_in[0]
    for q in range(1, tiles_n):
        summed = summed + block_in[q]
    w_ref[0] = summed[1, :, :total]
    for k in range(1, K):
        w_ref[k] = summed[0, :, (k - 1) * total : k * total]

    await_bytes(block_in.at[pl.ds(0, tiles_n - 1)], w_send)
    await_bytes(g_all.at[pl.ds(0, subs - 1)], g_send)
    await_bytes(g_pack.at[pl.ds(0, tiles_n - 2)], s_send)

    @pl.when(head)
    def _():
        await_bytes(x_pack.at[pl.ds(0, tiles_n - 2)], x_send)
        await_bytes(first_strips(subs, far_count), d_send)

    @pl.when(j != 0)
    def _():
        await_bytes(x_pack, x_send)

    for q in range(1, tiles_n):

        @pl.when(j == q)
        def _():
            await_bytes(first_strips(subs, counts[q]), d_send)
            moved = tiles_n - 2 if q == tiles_n - 1 else tiles_n - 1
            await_bytes(first_strips(subs - 1, moved * packed), f_send)


def store_kernel(in_vmem, w_vmem, in_hbm, w_hbm, sem):
    copies = [
        pltpu.make_async_copy(in_vmem, in_hbm, sem.at[0]),
        pltpu.make_async_copy(w_vmem, w_hbm, sem.at[1]),
    ]
    for copy in copies:
        copy.start()
    for copy in copies:
        copy.wait()


def face_path(features, out_grad, filters, tile_map):
    slots, chans, pixels = features.shape
    side = math.isqrt(pixels)
    tiles_n, subs = lax.axis_size("tile"), lax.axis_size("sub")
    matrices, table, links, inward = ghost_tables(side, slots, tiles_n)
    scale = 1.0 / math.sqrt(slots * tiles_n * pixels)
    width = DEPTH * side
    vmem = pl.BlockSpec(memory_space=pltpu.VMEM)
    hbm = pl.BlockSpec(memory_space=pltpu.HBM)
    dma = pltpu.SemaphoreType.DMA
    bf16, f32 = jnp.bfloat16, jnp.float32
    held = slots * 4 + tiles_n * links[0]
    held_outs = pl.pallas_call(
        functools.partial(face_kernel, (slots, tiles_n, subs, side, links, scale)),
        out_shape=(
            pltpu.VMEM(features.shape, bf16),
            pltpu.VMEM((K, chans, filters.shape[2]), f32),
        ),
        in_specs=[hbm] * 7,
        out_specs=(vmem, vmem),
        scratch_shapes=[
            pltpu.VMEM((2,) + features.shape, bf16),
            pltpu.VMEM((subs,) + features.shape, bf16),
            pltpu.VMEM((slots * 4, chans, width), bf16),
            pltpu.VMEM((slots * 4, chans, width), bf16),
            pltpu.VMEM((tiles_n - 1, links[0], chans, width), bf16),
            pltpu.VMEM((tiles_n - 1, links[0], chans, width), bf16),
            pltpu.VMEM((held, chans, width), bf16),
            pltpu.VMEM((subs, held, chans, width), bf16),
            pltpu.VMEM((2, chans, width), f32),
            pltpu.VMEM((tiles_n, 2, chans, width), f32),
            pltpu.VMEM((slots, chans, pixels), f32),
            pltpu.VMEM((slots, chans * subs, DEPTH * width), f32),
            pltpu.VMEM((slots, chans, DEPTH * width), f32),
            pltpu.VMEM((2,) + matrices.shape[1:], bf16),
            pltpu.VMEM(inward.shape, bf16),
            pltpu.VMEM((pixels, 2 * width), bf16),
            pltpu.VMEM(filters.shape, bf16),
            pltpu.SMEM(tile_map.shape, jnp.int32),
            pltpu.SMEM(table.shape, jnp.int32),
            pltpu.SemaphoreType.REGULAR,
            dma((9,)),
        ]
        + [dma] * 12,
        compiler_params=pltpu.CompilerParams(
            collective_id=0, has_side_effects=True, vmem_limit_bytes=67043328 - 512 * 1024
        ),
    )(
        features,
        out_grad,
        filters,
        tile_map,
        jnp.asarray(table),
        jnp.asarray(matrices, bf16),
        jnp.asarray(inward, bf16),
    )
    held_outs = [pltpu.with_memory_space_constraint(value, pltpu.VMEM) for value in held_outs]
    return pl.pallas_call(
        store_kernel,
        out_shape=(
            jax.ShapeDtypeStruct(features.shape, bf16),
            jax.ShapeDtypeStruct((K, chans, filters.shape[2]), f32),
        ),
        in_specs=[vmem] * 2,
        out_specs=(hbm, hbm),
        scratch_shapes=[dma((2,))],
    )(*held_outs)


def on_device(features, out_grad, filters, tile_map):
    slots, chans, pixels = features.shape
    side = math.isqrt(pixels)
    whole_faces = slots * lax.axis_size("tile") == 12
    channels = chans * lax.axis_size("sub")
    if whole_faces and 1 < slots < 5 and DEPTH * side == 128 and chans % 8 == 0 and channels == 32:
        return face_path(features, out_grad, filters, tile_map)
    return general_path(features, out_grad, filters, tile_map)


def solution(mesh):
    placed = (P(("grp", "tile"), "sub", None), P(("grp", "tile"), "sub", None), P(), P())
    return jax.shard_map(
        on_device,
        mesh=mesh,
        in_specs=placed,
        out_specs=(P(("grp", "tile"), "sub", None), P("grp", "sub", None)),
        check_vma=False,
    )
```

```python
import functools
import math

import jax
import jax.numpy as jnp
import numpy as np
from jax import lax
from jax.experimental import pallas as pl
from jax.experimental.pallas import tpu as pltpu
from jax.sharding import PartitionSpec as P

K = 5


def from_behind(value, axis, steps):
    count = lax.axis_size(axis)
    pairs = [(source, (source + steps) % count) for source in range(count)]
    return lax.ppermute(value, axis, pairs)


def tile_coords(nested_code, bit_count):
    coord_x = nested_code * 0
    coord_y = nested_code * 0
    for bit_level in range(bit_count):
        coord_x = coord_x + nested_code // 4**bit_level % 2 * 2**bit_level
        coord_y = coord_y + nested_code // (2 * 4**bit_level) % 2 * 2**bit_level
    return (coord_x, coord_y)


def nested_index(coord_x, coord_y, bit_count):
    nested_code = coord_x * 0
    for bit_level in range(bit_count):
        nested_code = nested_code + coord_x // 2**bit_level % 2 * 4**bit_level
        nested_code = nested_code + coord_y // 2**bit_level % 2 * (2 * 4**bit_level)
    return nested_code


def pick(condition, when_true, when_false):
    return when_false + (when_true - when_false) * condition


def neighbour_codes(tile_ids, per_face, side_count):
    bit_count = side_count.bit_length() - 1
    face_id = tile_ids // per_face
    coord_x, coord_y = tile_coords(tile_ids % per_face, bit_count)
    column = face_id % 4
    is_north = face_id < 4
    is_south = face_id >= 8
    last_tile = side_count - 1

    def by_cycle(north_value, equator_value, south_value):
        return pick(is_north, north_value, pick(is_south, south_value, equator_value))

    side_rules = [
        (
            coord_x > 0,
            (face_id, coord_x - 1, coord_y, 1),
            (
                by_cycle(4 + column, 8 + (column + 3) % 4, 8 + (column + 3) % 4),
                by_cycle(last_tile, last_tile, coord_y),
                by_cycle(coord_y, coord_y, 0),
                by_cycle(1, 1, 2),
            ),
        ),
        (
            coord_x < last_tile,
            (face_id, coord_x + 1, coord_y, 0),
            (
                by_cycle((column + 1) % 4, column, 4 + (column + 1) % 4),
                by_cycle(coord_y, 0, 0),
                by_cycle(last_tile, coord_y, coord_y),
                by_cycle(3, 0, 0),
            ),
        ),
        (
            coord_y > 0,
            (face_id, coord_x, coord_y - 1, 3),
            (
                by_cycle(4 + (column + 1) % 4, 8 + column, 8 + (column + 1) % 4),
                by_cycle(coord_x, coord_x, 0),
                by_cycle(last_tile, last_tile, coord_x),
                by_cycle(3, 3, 0),
            ),
        ),
        (
            coord_y < last_tile,
            (face_id, coord_x, coord_y + 1, 2),
            (
                by_cycle((column + 3) % 4, (column + 3) % 4, 4 + column),
                by_cycle(last_tile, coord_x, coord_x),
                by_cycle(coord_x, 0, 0),
                by_cycle(1, 2, 2),
            ),
        ),
    ]
    target_list = []
    edge_list = []
    for inside, within, across in side_rules:
        chosen = [
            pick(inside, near_value, far_value) for near_value, far_value in zip(within, across)
        ]
        target_list.append(chosen[0] * per_face + nested_index(chosen[1], chosen[2], bit_count))
        edge_list.append(chosen[3] + tile_ids * 0)
    return (target_list, edge_list)


def neighbour_table(tile_map, per_face, side_count):
    target_list, edge_list = neighbour_codes(tile_map, per_face, side_count)
    targets = jnp.stack(target_list, axis=1).astype(jnp.int32)
    edges = jnp.stack(edge_list, axis=1).astype(jnp.int32)
    slot_of = jnp.argsort(tile_map).astype(jnp.int32)
    return (slot_of[targets].astype(jnp.int32), edges)


def peer_offsets(slot_count, device_count, per_face, side_count):
    tile_ids = np.arange(slot_count * device_count, dtype=np.int64)
    target_list, edge_list = neighbour_codes(tile_ids, per_face, side_count)
    targets = np.stack(target_list, axis=1)
    offsets = (tile_ids[:, None] // slot_count - targets // slot_count) % device_count
    distinct = sorted(set((int(value) for value in offsets.ravel())) - {0})
    position = np.zeros(device_count, dtype=np.int32)
    for order, value in enumerate(distinct):
        position[value] = order + 1
    return (distinct, position)


def edge_lines(values, tile_side):
    return jnp.stack(
        [
            values[..., :tile_side],
            values[..., -tile_side:],
            values[..., ::tile_side],
            values[..., tile_side - 1 :: tile_side],
        ],
        axis=1,
    )


def stencil(values, ghosts, tile_side):
    position = jnp.arange(values.shape[-1]) % tile_side
    zero_line = jnp.zeros_like(values[..., :1])
    upper_side = jnp.concatenate([ghosts[:, 0], values[..., :-tile_side]], axis=-1)
    lower_side = jnp.concatenate([values[..., tile_side:], ghosts[:, 1]], axis=-1)
    left_side = jnp.where(
        position == 0,
        jnp.repeat(ghosts[:, 2], tile_side, axis=-1),
        jnp.concatenate([zero_line, values[..., :-1]], axis=-1),
    )
    right_side = jnp.where(
        position == tile_side - 1,
        jnp.repeat(ghosts[:, 3], tile_side, axis=-1),
        jnp.concatenate([values[..., 1:], zero_line], axis=-1),
    )
    return -0.25 * (upper_side + lower_side + left_side + right_side)


def tile_total(filter_part):
    return lax.psum(filter_part, "tile")


def general_path(features, out_grad, filters, tile_map):
    slot_count = features.shape[0]
    group_channels = features.shape[1]
    tile_side = math.isqrt(features.shape[2])
    device_count = lax.axis_size("tile")
    total_tiles = slot_count * device_count
    side_count = math.isqrt(total_tiles // 12)
    scale_factor = 1.0 / math.sqrt(total_tiles * features.shape[2])
    highest = lax.Precision.HIGHEST
    slot_table, edge_table = neighbour_table(tile_map, total_tiles // 12, side_count)
    my_device = lax.axis_index("tile")
    first_slot = my_device * slot_count
    my_slots = lax.dynamic_slice_in_dim(slot_table, first_slot, slot_count, 0)
    my_edges = lax.dynamic_slice_in_dim(edge_table, first_slot, slot_count, 0)
    channel_start = lax.axis_index("sub") * group_channels
    weights = filters.astype(jnp.float32)
    distinct, position = peer_offsets(slot_count, device_count, total_tiles // 12, side_count)
    sender_gap = (my_device - my_slots // slot_count) % device_count
    local_rows = jnp.asarray(position)[sender_gap] * slot_count + my_slots % slot_count

    def laplace(values):
        border = edge_lines(values, tile_side).reshape(slot_count, 4, group_channels * tile_side)
        received = [border]
        for offset_value in distinct:
            received.append(from_behind(border, "tile", offset_value))
        stacked = jnp.concatenate(received, axis=0)
        stacked = stacked.reshape(stacked.shape[0], 4, group_channels, tile_side)
        rows = []
        for slot in range(slot_count):
            for side in range(4):
                start = (local_rows[slot, side], my_edges[slot, side], 0, 0)
                rows.append(
                    lax.dynamic_slice(stacked, start, (1, 1, group_channels, tile_side))
                )
        ghosts = jnp.concatenate(rows, axis=0)
        ghosts = ghosts.reshape(slot_count, 4, group_channels, tile_side)
        return stencil(values, ghosts, tile_side)

    whole_grad = lax.all_gather(out_grad, "sub", axis=1, tiled=True)
    cotangent = whole_grad.astype(jnp.float32)
    inputs = features.astype(jnp.float32)
    previous, current = (inputs, laplace(inputs))
    filter_terms = [
        jnp.einsum("sip,sop->io", inputs, cotangent, precision=highest),
        jnp.einsum("sip,sop->io", current, cotangent, precision=highest),
    ]
    for degree in range(2, K):
        previous, current = (current, 2.0 * laplace(current) - previous)
        filter_terms.append(jnp.einsum("sip,sop->io", current, cotangent, precision=highest))
    weight_grad = tile_total(jnp.stack(filter_terms)) * scale_factor
    row_block = lax.dynamic_slice_in_dim(weights, channel_start, group_channels, 1)

    def mixed(degree):
        return jnp.einsum("sop,io->sip", cotangent, row_block[degree], precision=highest)

    next_sum = mixed(K - 1)
    after_next = jnp.zeros_like(next_sum)
    for degree in range(K - 2, 0, -1):
        next_sum, after_next = (mixed(degree) + 2.0 * laplace(next_sum) - after_next, next_sum)
    in_grad = (mixed(0) + laplace(next_sum) - after_next).astype(jnp.bfloat16)
    return (in_grad, weight_grad)


DEPTH = K - 1
GHOST_SIDES = (0, 2, 3, 1)
OUTSIDE = 6


def face_graph(tile_side):
    tile_ids = np.arange(12, dtype=np.int64)
    target_list, edge_list = neighbour_codes(tile_ids, 1, 1)
    targets = np.stack(target_list, axis=1)
    edges = np.stack(edge_list, axis=1)
    pixels = tile_side * tile_side
    grid = np.arange(pixels).reshape(tile_side, tile_side)
    lines = [grid[0], grid[-1], grid[:, 0], grid[:, -1]]
    ghosts = np.zeros((12, 4, tile_side), dtype=np.int64)
    around = np.zeros((12, 4, tile_side, tile_side), dtype=np.int64)
    for tile in range(12):
        for side in range(4):
            ghosts[tile, side] = targets[tile, side] * pixels + lines[edges[tile, side]]
        whole = tile * pixels + grid
        around[tile, 0] = np.concatenate([ghosts[tile, 0][None], whole[:-1]], 0)
        around[tile, 1] = np.concatenate([whole[1:], ghosts[tile, 1][None]], 0)
        around[tile, 2] = np.concatenate([ghosts[tile, 2][:, None], whole[:, :-1]], 1)
        around[tile, 3] = np.concatenate([whole[:, 1:], ghosts[tile, 3][:, None]], 1)
    around = around.transpose(0, 2, 3, 1).reshape(12 * pixels, 4)
    return targets, edges, ghosts, around


@functools.lru_cache(None)
def ghost_tables(tile_side, slots, tiles_n):
    targets, edges, ghosts, around = face_graph(tile_side)
    pixels = tile_side * tile_side
    grid = np.arange(pixels).reshape(tile_side, tile_side)
    strips = np.stack(
        [
            grid[:DEPTH].ravel(),
            grid[-DEPTH:].ravel(),
            grid[:, :DEPTH].T.ravel(),
            grid[:, -DEPTH:].T.ravel(),
        ]
    )
    sources_of = []
    by_class = []
    for tile in range(12):
        wanted = np.concatenate([ghosts[tile, side] for side in GHOST_SIDES])
        power = np.zeros((wanted.size, 12 * pixels), dtype=np.int32)
        power[np.arange(wanted.size), wanted] = 1
        powers = [power]
        for _ in range(DEPTH - 1):
            powers.append(sum(powers[-1][:, around[:, side]] for side in range(4)))
        rows = np.concatenate(
            [powers[0], powers[1], powers[2] - 8 * powers[0], powers[3] - 12 * powers[1]]
        )
        support = np.flatnonzero(np.any(rows != 0, axis=0))
        sources = [(int(targets[tile, side]), int(edges[tile, side])) for side in range(4)]
        own = [(tile, side) for side in range(4)]
        covered = set(int(t) * pixels + int(p) for t, e in sources + own for p in strips[e])
        left = [int(p) for p in support if int(p) not in covered]
        corner_tiles = {}
        for pixel in left:
            corner_tiles.setdefault(pixel // pixels, []).append(pixel % pixels)
        first = lambda t: int(
            np.flatnonzero(np.any(rows[:, [t * pixels + p for p in corner_tiles[t]]] != 0, axis=1))[0]
        )
        for other in sorted(corner_tiles, key=first):
            choice = [e for e in range(4) if set(corner_tiles[other]) <= set(strips[e].tolist())]
            sources.append((other, choice[0]))
        assert len(sources) <= OUTSIDE
        while len(sources) < OUTSIDE:
            sources.append(sources[-1])
        sources_of.append(sources)
        lanes = np.concatenate([t * pixels + strips[e] for t, e in sources + own])
        seen, keep = set(), np.zeros(lanes.size, dtype=bool)
        for lane, pixel in enumerate(lanes.tolist()):
            keep[lane] = pixel not in seen
            seen.add(pixel)
        assert set(support.tolist()) <= seen
        matrix = (rows[:, lanes] * keep[None]).T
        assert np.abs(matrix).max() <= 127
        if tile % 4 == 0:
            by_class.append(matrix)
        else:
            assert np.array_equal(matrix, by_class[-1])
    wanted = {}
    for tile in range(12):
        for t, e in sources_of[tile]:
            pair = (t // slots, tile // slots)
            if pair[0] != pair[1]:
                held = wanted.setdefault(pair, [])
                if (t, e) not in held:
                    held.append((t, e))
    packed = max(len(held) for held in wanted.values())
    send = np.zeros((tiles_n, tiles_n, packed), dtype=np.int32)
    for (q, p), held in wanted.items():
        for order, (t, e) in enumerate(held):
            send[q, p, order] = (t - q * slots) * 4 + e
    take_from = np.zeros((12, OUTSIDE), dtype=np.int32)
    for tile in range(12):
        for order, (t, e) in enumerate(sources_of[tile]):
            q, p = t // slots, tile // slots
            if q == p:
                take_from[tile, order] = (t - q * slots) * 4 + e
            else:
                at = wanted[(q, p)].index((t, e))
                take_from[tile, order] = slots * 4 + q * packed + at
    table = np.concatenate([take_from.ravel(), send.ravel()])
    counts = tuple(len(wanted.get((q, 0), ())) for q in range(tiles_n))
    far = []
    for tile in range(slots):
        for order, (t, e) in enumerate(sources_of[tile]):
            if t // slots == tiles_n - 1 and (t, e) not in sources_of[tile][:order]:
                far.append((tile, order, int(take_from[tile, order])))
    spread = np.zeros((4, tile_side, tile_side, tile_side))
    step = np.arange(tile_side)
    spread[0, step, 0, step] = 1
    spread[1, step, step, 0] = 1
    spread[2, step, step, -1] = 1
    spread[3, step, -1, step] = 1
    local = np.zeros((pixels, pixels))
    for u in range(tile_side):
        for v in range(tile_side):
            for du, dv in ((1, 0), (-1, 0), (0, 1), (0, -1)):
                if 0 <= u + du < tile_side and 0 <= v + dv < tile_side:
                    local[grid[u, v], grid[u + du, v + dv]] = -0.25
    inward = [-0.25 * spread.reshape(4 * tile_side, pixels)]
    inward.append(2.0 * inward[0] @ local)
    for _ in range(DEPTH - 2):
        inward.append(2.0 * inward[-1] @ local - inward[-2])
    inward = np.concatenate(inward)
    assert np.array_equal(inward, inward.astype(jnp.bfloat16).astype(np.float64))
    return np.stack(by_class), table, (packed, counts, len(wanted.get((0, tiles_n - 1), ())), tuple(far)), inward


def split(value):
    high = value.astype(jnp.bfloat16).astype(jnp.float32)
    return high, value - high


def product(left, right):
    return lax.dot_general(
        left, right, (((1,), (1,)), ((), ())), preferred_element_type=jnp.float32
    )


def face_kernel(
    sizes,
    x_hbm,
    g_hbm,
    f_hbm,
    map_hbm,
    table_hbm,
    ghost_hbm,
    inward_hbm,
    in_ref,
    w_ref,
    xg_ref,
    g_all,
    x_mine,
    g_mine,
    x_pack,
    g_pack,
    x_ext,
    g_ext,
    block,
    block_in,
    result,
    g_lines_own,
    ghost,
    inward,
    take,
    f_ref,
    map_ref,
    table_ref,
    ready,
    load_sem,
    x_send,
    x_recv,
    s_send,
    s_recv,
    g_send,
    g_recv,
    d_send,
    d_recv,
    f_send,
    f_recv,
    w_send,
    w_recv,
):
    slots, tiles_n, subs, side, (packed, counts, far_count, far), scale = sizes
    x_ref, g_ref = xg_ref.at[0], xg_ref.at[1]
    chans = x_ref.shape[1]
    total = subs * chans
    pixels = side * side
    width = DEPTH * side
    rows = slots * chans
    bf16, f32 = jnp.bfloat16, jnp.float32
    j = lax.axis_index("tile")
    s = lax.axis_index("sub")
    tile_peers = []
    for d in range(tiles_n - 1):
        up = d + (j <= d).astype(jnp.int32)
        back = tiles_n - 2 - d
        down = back + (j <= back).astype(jnp.int32)
        tile_peers.append(jnp.where(2 * j < tiles_n, down, up))
    core_peer = s + 1 - 2 * lax.rem(s, 2)
    sub_peers = [lax.rem(s + 2, subs), lax.rem(core_peer + 2, subs), core_peer]
    friends = len(tile_peers) + len(sub_peers)
    head = j == 0
    tail = j == tiles_n - 1
    kinds = [(slots * j + m) // 4 for m in range(slots)]

    def greet(friend):
        pl.semaphore_signal(
            pltpu.get_barrier_semaphore(),
            inc=1,
            device_id=friend,
            device_id_type=pl.DeviceIdType.MESH,
        )

    first_loads = [
        pltpu.make_async_copy(x_hbm, x_ref, load_sem.at[0]),
        pltpu.make_async_copy(g_hbm, g_ref, load_sem.at[0]),
        pltpu.make_async_copy(map_hbm, map_ref, load_sem.at[2]),
        pltpu.make_async_copy(table_hbm, table_ref, load_sem.at[3]),
    ]
    barrier = pltpu.get_barrier_semaphore()
    for peer in sub_peers:
        greet({"sub": peer})
    for d, peer in enumerate(tile_peers):

        @pl.when(jnp.logical_not(tail & (peer == 0)))
        def _():
            greet({"tile": peer})

    for copy in first_loads:
        copy.start()

    one_kind = kinds[0] == kinds[-1]
    loads = [
        pltpu.make_async_copy(ghost_hbm.at[kinds[0]], ghost.at[0], load_sem.at[4]),
        pltpu.make_async_copy(inward_hbm, inward, load_sem.at[5]),
        pltpu.make_async_copy(f_hbm, f_ref, load_sem.at[6]),
        pltpu.make_async_copy(g_hbm, g_all.at[s], load_sem.at[7]),
    ]
    second = pltpu.make_async_copy(ghost_hbm.at[kinds[-1]], ghost.at[1], load_sem.at[8])
    for copy in loads:
        copy.start()
    pl.when(jnp.logical_not(one_kind))(second.start)

    @pl.when(head)
    def _():
        for peer in tile_peers:
            for other in sub_peers:
                greet({"tile": peer, "sub": other})

    def remote(source, target, send, recv, device):
        return pltpu.make_async_remote_copy(
            source,
            target,
            send,
            recv,
            device_id=device,
            device_id_type=pl.DeviceIdType.MESH,
        )

    def g_copy(d, sender, peer):
        return remote(g_hbm, g_all.at[sender], g_send, g_recv, {"sub": peer})

    def open_up():
        pl.semaphore_wait(barrier, friends + jnp.where(head, -1, subs - 1))

    base = slots * j
    column = lax.broadcasted_iota(jnp.int32, (pixels, 2 * width), 1)
    wanted_pixel = column % side * side + column % width // side
    wanted_pixel = wanted_pixel + jnp.where(column < width, 0, side - DEPTH)
    pixel = lax.broadcasted_iota(jnp.int32, (pixels, 2 * width), 0)
    take[...] = jnp.where(pixel == wanted_pixel, 1.0, 0.0).astype(bf16)
    pltpu.make_async_copy(xg_ref, xg_ref, load_sem.at[0]).wait()
    for copy in first_loads[2:]:
        copy.wait()

    def slot_of(m):
        found = 0
        for slot in range(1, slots):
            found = jnp.where(map_ref[base + slot] == base + m, slot, found)
        return found

    slot_list = [slot_of(m) for m in range(slots)]
    x_own = jnp.concatenate([x_ref[slot_list[m]].astype(f32) for m in range(slots)], axis=0)
    g_own = jnp.concatenate([g_ref[slot_list[m]].astype(f32) for m in range(slots)], axis=0)
    both = jnp.concatenate([x_own, g_own], axis=0).astype(bf16)
    cut = jnp.dot(both, take[...], preferred_element_type=f32)

    def strips_of(value, cut_value):
        return [
            value[:, :width],
            value[:, pixels - width :],
            cut_value[:, :width],
            cut_value[:, width:],
        ]

    x_strips = strips_of(x_own, cut[:rows])
    g_strips = strips_of(g_own, cut[rows:])
    for m in range(slots):
        at = slice(m * chans, (m + 1) * chans)
        for e in range(4):
            x_mine[m * 4 + e] = x_strips[e][at].astype(bf16)
            g_mine[m * 4 + e] = g_strips[e][at].astype(bf16)
    sends = 12 * OUTSIDE
    for d, peer in enumerate(tile_peers):
        for i in range(packed):
            index = table_ref[sends + (j * tiles_n + peer) * packed + i]
            x_pack[d, i] = x_mine[index]
            g_pack[d, i] = g_mine[index]
    for m in range(slots):
        at = slice(m * chans, (m + 1) * chans)
        for e in range(4):
            x_ext[m * 4 + e] = x_strips[e][at].astype(bf16)

    def landing(sender):
        return pl.ds(slots * 4 + sender * packed, packed)

    def x_copy(d, sender, peer):
        return remote(
            x_pack.at[d], x_ext.at[landing(sender)], x_send, x_recv, {"tile": peer}
        )

    def strip_copy(d, sender, peer):
        return remote(
            g_pack.at[d],
            g_ext.at[s, landing(sender)],
            s_send,
            s_recv,
            {"tile": peer},
        )

    def forward_copy(q, d, sender, peer):
        held = g_ext.at[sender, landing(q)]
        return remote(held, held, f_send, f_recv, {"sub": peer})

    def block_copy(d, sender, peer):
        return remote(block, block_in.at[sender], w_send, w_recv, {"tile": peer})

    def x_crosses(sender, peer):
        return jnp.logical_not((sender == 0) & (peer == tiles_n - 1))

    def direct_copy(q, d, sender, peer):
        at = 0 if 2 * q >= tiles_n else tiles_n - 2
        return remote(
            g_pack.at[at, pl.ds(0, counts[q])],
            g_ext.at[sender, pl.ds(slots * 4 + q * packed, counts[q])],
            d_send,
            d_recv,
            {"tile": 0, "sub": peer},
        )

    def far_copy(peer):
        return remote(
            g_pack.at[0, pl.ds(0, far_count)],
            g_ext.at[s, pl.ds(slots * 4, far_count)],
            d_send,
            d_recv,
            {"tile": tiles_n - 1, "sub": peer},
        )

    def await_bytes(held, semaphore):
        pltpu.make_async_copy(held, held, semaphore).wait()

    def first_strips(rows_of, count):
        return g_ext.at[pl.ds(0, rows_of), pl.ds(0, count)]

    def for_direct(action):
        for q in range(1, tiles_n):

            @pl.when(j == q)
            def _():
                for d, peer in enumerate([s] + sub_peers):
                    action(direct_copy(q, d, s, peer))

    def send_strips():
        for_direct(lambda copy: copy.start())
        for d, peer in enumerate(tile_peers):
            pl.when((peer != 0) & x_crosses(j, peer))(strip_copy(d, j, peer).start)

    @pl.when(tail)
    def _():
        x_ext[landing(0)] = jnp.zeros((packed, chans, width), bf16)


    lane = lax.broadcasted_iota(jnp.int32, (rows, pixels), 1)
    y_at = lane % side

    def around(value):
        out = jnp.where(lane < side, 0.0, pltpu.roll(value, side, 1))
        out = out + jnp.where(lane >= pixels - side, 0.0, pltpu.roll(value, pixels - side, 1))
        out = out + jnp.where(y_at == 0, 0.0, pltpu.roll(value, 1, 1))
        return out + jnp.where(y_at == side - 1, 0.0, pltpu.roll(value, pixels - 1, 1))

    def of_slot(value, m, count):
        return value[m * count : (m + 1) * count]

    open_up()
    for d, peer in enumerate(tile_peers):
        pl.when(x_crosses(j, peer))(x_copy(d, j, peer).start)
    for d, peer in enumerate(sub_peers):
        g_copy(d, s, peer).start()
    send_strips()

    @pl.when(tail)
    def _():
        for other in [s] + sub_peers:
            pl.semaphore_signal(
                ready,
                inc=1,
                device_id={"tile": 0, "sub": other},
                device_id_type=pl.DeviceIdType.MESH,
            )

    chain = [x_own, -0.25 * around(x_own)]
    for k in range(2, K):
        chain.append(-0.5 * around(chain[k - 1]) - chain[k - 2])

    for copy in loads:
        copy.wait()
    pl.when(jnp.logical_not(one_kind))(second.wait)
    outer = OUTSIDE * width
    mid_first = [kinds[m] == kinds[0] for m in range(slots)]
    scales = (1.0, -0.5, 0.25, -0.125)

    def ghost_lines(value, at, count, single=False):
        first = jnp.dot(value, ghost[0, at], preferred_element_type=f32)
        if single:
            return [of_slot(first, m, count) for m in range(slots)]
        last = jnp.dot(value, ghost[1, at], preferred_element_type=f32)
        return [
            jnp.where(mid_first[m], of_slot(first, m, count), of_slot(last, m, count))
            for m in range(slots)
        ]

    x_inner = ghost_lines(
        jnp.concatenate(x_strips, axis=1).astype(bf16), slice(outer, outer + 4 * width), chans
    )

    x_edge = product(x_own.astype(bf16), inward[...])
    filters = jnp.concatenate([f_ref[k].astype(f32) for k in range(K)], axis=1).astype(bf16)
    pick_row = lax.broadcasted_iota(jnp.int32, (chans, total), 0) + chans * s
    pick_col = lax.broadcasted_iota(jnp.int32, (chans, total), 1)
    mine = jnp.dot(
        jnp.where(pick_row == pick_col, 1.0, 0.0).astype(bf16),
        filters,
        preferred_element_type=f32,
    )
    mixing = jnp.concatenate(
        [mine[:, k * total : (k + 1) * total] for k in range(K)], axis=0
    ).astype(bf16)
    outside = []
    for m in range(DEPTH):
        pieces = [mine[:, (m + 1) * total :]]
        if m > 0:
            pieces.append(jnp.zeros((chans, m * total), f32))
        outside.append(jnp.concatenate(pieces, axis=1))
    outside = jnp.concatenate(outside, axis=0)
    outside = jnp.concatenate([outside, outside], axis=1).astype(bf16)

    def load_g():
        return [
            jnp.concatenate([g_all[e, slot_list[m]].astype(f32) for e in range(subs)], axis=0)
            for m in range(slots)
        ]

    def await_g():
        await_bytes(g_all.at[pl.ds(0, subs - 1)], g_recv)

    def local_part(single):
        g_full = load_g()
        g_bf = [value.astype(bf16) for value in g_full]
        mixed = [jnp.dot(mixing, g_bf[m], preferred_element_type=f32) for m in range(slots)]
        grads = [
            jnp.concatenate([of_slot(mixed[m], k, chans) for m in range(slots)], axis=0)
            for k in range(K)
        ]
        after, upper = grads[K - 1], grads[K - 2] - 0.5 * around(grads[K - 1])
        for k in range(K - 3, 0, -1):
            after, upper = upper, grads[k] - 0.5 * around(upper) - after
        inner = grads[0] - 0.25 * around(upper) - after

        for m in range(slots):
            result[m] = of_slot(inner, m, chans)
        whole = jnp.concatenate(g_full, axis=0)
        whole_strips = strips_of(
            whole, jnp.dot(whole.astype(bf16), take[...], preferred_element_type=f32)
        )
        for m in range(slots):
            for e in range(subs):
                at = slice(m * total + e * chans, m * total + (e + 1) * chans)
                for side_at in range(4):
                    g_ext[e, m * 4 + side_at] = whole_strips[side_at][at].astype(bf16)
        g_inner = ghost_lines(
            jnp.concatenate(whole_strips, axis=1).astype(bf16),
            slice(outer, outer + 4 * width),
            total,
            single,
        )
        for m in range(slots):
            g_lines_own[m] = g_inner[m]

    @pl.when(head)
    def _():
        await_g()
        pl.semaphore_wait(ready, subs)
        for peer in [s] + sub_peers:
            far_copy(peer).start()
        local_part(True)


    @pl.when(tail)
    def _():
        await_bytes(x_ext.at[pl.ds(0, (tiles_n - 2) * packed)], x_recv)

    @pl.when(jnp.logical_not(tail))
    def _():
        await_bytes(x_ext.at[pl.ds(0, (tiles_n - 1) * packed)], x_recv)

    def pass_on():
        @pl.when(tail)
        def _():
            await_bytes(g_ext.at[0, pl.ds(0, (tiles_n - 2) * packed)], s_recv)

        @pl.when(jnp.logical_not(tail))
        def _():
            await_bytes(g_ext.at[0, pl.ds(0, (tiles_n - 1) * packed)], s_recv)

        for q, peer in enumerate(tile_peers):

            @pl.when(x_crosses(peer, j))
            def _():
                for d, other in enumerate(sub_peers):
                    forward_copy(peer, d, s, other).start()

    wanted = [
        [table_ref[(base + m) * OUTSIDE + r] for r in range(OUTSIDE)] for m in range(slots)
    ]

    def outer_strips(read):
        return jnp.concatenate(
            [
                jnp.concatenate([read(wanted[m][r]).astype(f32) for r in range(OUTSIDE)], axis=1)
                for m in range(slots)
            ],
            axis=0,
        )

    def by_power(lines):
        return jnp.concatenate(
            [
                lines[:, n * width : (n + 1) * width] * scales[n] for n in range(DEPTH)
            ],
            axis=0,
        )

    half = DEPTH * chans

    def by_degree(across):
        across = across[:half] + across[half:]
        across = across[:, : DEPTH * total] + across[:, DEPTH * total :]
        place = lax.broadcasted_iota(jnp.int32, (chans, DEPTH * total), 1)
        out = of_slot(across, 0, chans)
        for n in range(1, DEPTH):
            shifted = pltpu.roll(of_slot(across, n, chans), n * total, 1)
            out = out + jnp.where(place < n * total, 0.0, shifted)
        return out

    x_lines = ghost_lines(
        outer_strips(lambda index: x_ext[index]).astype(bf16), slice(0, outer), chans
    )
    x_lines = [by_power(x_lines[m] + x_inner[m]) for m in range(slots)]
    entering = []
    for k in range(1, K):
        for m in range(slots):
            pieces = [of_slot(x_lines[m], k - 1 - n, chans) for n in range(k)]
            if k < DEPTH:
                pieces.append(jnp.zeros((chans, (DEPTH - k) * width), f32))
            entering.append(jnp.concatenate(pieces, axis=1))
    entering = jnp.concatenate(split(jnp.concatenate(entering, axis=0)), axis=0)
    entering = jnp.dot(entering.astype(bf16), inward[...], preferred_element_type=f32)
    entering = entering[: DEPTH * rows] + entering[DEPTH * rows :]
    held = [x_own]
    for k in range(1, K):
        held += list(split(chain[k] + of_slot(entering, k - 1, rows)))
    terms = [
        jnp.concatenate([of_slot(value, m, chans) for value in held], axis=0).astype(bf16)
        for m in range(slots)
    ]
    pl.when(jnp.logical_not(head))(await_g)
    g_bf = [value.astype(bf16) for value in load_g()]
    grad = product(terms[0], g_bf[0])
    for m in range(1, slots):
        grad = grad + product(terms[m], g_bf[m])
    later = [
        of_slot(grad, 2 * k - 1, chans) + of_slot(grad, 2 * k, chans) for k in range(1, K)
    ]
    block[0] = jnp.concatenate(later, axis=1) * scale
    block[1] = jnp.concatenate(
        [grad[:chans] * scale, jnp.zeros((chans, width - total), f32)], axis=1
    )

    def send_blocks():
        for d, peer in enumerate(tile_peers):
            block_copy(d, j, peer).start()

    @pl.when(j != 0)
    def _():
        send_blocks()
        pass_on()
        local_part(False)


    def finish(single):
        if single:

            @pl.when(tail)
            def _():
                await_bytes(first_strips(subs, far_count), d_recv)
                await_bytes(first_strips(subs - 1, (tiles_n - 2) * packed), f_recv)

        @pl.when((j != 0) & jnp.logical_not(tail))
        def _():
            await_bytes(first_strips(subs - 1, (tiles_n - 1) * packed), f_recv)

        @pl.when(head)
        def _():
            await_bytes(first_strips(subs, sum(counts[1:])), d_recv)

        if single and far:
            far_lines, far_edge = [], []
            for m, r, index in far:
                held = jnp.concatenate(
                    [g_ext[e, index].astype(f32) for e in range(subs)], axis=0
                ).astype(bf16)
                rows_at = ghost[m // 4, r * width : (r + 1) * width]
                far_lines.append(by_power(jnp.dot(held, rows_at, preferred_element_type=f32)))
                mine_edge = of_slot(x_edge, m, chans)
                far_edge.append(
                    jnp.concatenate(
                        [mine_edge[:, n * width : (n + 1) * width] for n in range(DEPTH)], axis=0
                    )
                )
            far_lines = jnp.concatenate(split(jnp.concatenate(far_lines, axis=1)), axis=0)
            far_edge = jnp.concatenate(split(jnp.concatenate(far_edge, axis=1)), axis=0)
            crossed = by_degree(product(far_edge.astype(bf16), far_lines.astype(bf16)))
        if single:

            @pl.when(head)
            def _():
                if far:
                    block[0] = block[0] + crossed * scale
                send_blocks()

        gathered = outer_strips(
            lambda index: jnp.concatenate([g_ext[e, index].astype(f32) for e in range(subs)], axis=0)
        )
        g_lines = ghost_lines(gathered.astype(bf16), slice(0, outer), total, single)
        g_lines = jnp.concatenate(
            [by_power(g_lines[m] + g_lines_own[m]) for m in range(slots)], axis=1
        )
        mixed = jnp.dot(
            outside,
            jnp.concatenate(split(g_lines), axis=0).astype(bf16),
            preferred_element_type=f32,
        )
        mixed = jnp.concatenate(
            [
                jnp.concatenate(
                    [
                        of_slot(mixed, n, chans)[:, m * width : (m + 1) * width]
                        for n in range(DEPTH)
                    ],
                    axis=1,
                )
                for m in range(slots)
            ],
            axis=0,
        )
        spread = jnp.dot(
            jnp.concatenate(split(mixed), axis=0).astype(bf16),
            inward[...],
            preferred_element_type=f32,
        )
        inner = spread[:rows] + spread[rows:]
        for m in range(slots):
            result[m] = result[m] + of_slot(inner, m, chans)
        for slot in range(slots):
            in_ref[slot] = result[lax.rem(map_ref[base + slot], slots)].astype(bf16)
    pl.when(one_kind)(functools.partial(finish, True))
    pl.when(jnp.logical_not(one_kind))(functools.partial(finish, False))

    await_bytes(block_in.at[pl.ds(0, tiles_n - 1)], w_recv)
    block_in[j] = block[...]
    summed = block_in[0]
    for q in range(1, tiles_n):
        summed = summed + block_in[q]
    w_ref[0] = summed[1, :, :total]
    for k in range(1, K):
        w_ref[k] = summed[0, :, (k - 1) * total : k * total]

    await_bytes(block_in.at[pl.ds(0, tiles_n - 1)], w_send)
    await_bytes(g_all.at[pl.ds(0, subs - 1)], g_send)
    await_bytes(g_pack.at[pl.ds(0, tiles_n - 2)], s_send)

    @pl.when(head)
    def _():
        await_bytes(x_pack.at[pl.ds(0, tiles_n - 2)], x_send)
        await_bytes(first_strips(subs, far_count), d_send)

    @pl.when(j != 0)
    def _():
        await_bytes(x_pack, x_send)

    for q in range(1, tiles_n):

        @pl.when(j == q)
        def _():
            await_bytes(first_strips(subs, counts[q]), d_send)
            moved = tiles_n - 2 if q == tiles_n - 1 else tiles_n - 1
            await_bytes(first_strips(subs - 1, moved * packed), f_send)


def store_kernel(in_vmem, w_vmem, in_hbm, w_hbm, sem):
    copies = [
        pltpu.make_async_copy(in_vmem, in_hbm, sem.at[0]),
        pltpu.make_async_copy(w_vmem, w_hbm, sem.at[1]),
    ]
    for copy in copies:
        copy.start()
    for copy in copies:
        copy.wait()


def face_path(features, out_grad, filters, tile_map):
    slots, chans, pixels = features.shape
    side = math.isqrt(pixels)
    tiles_n, subs = lax.axis_size("tile"), lax.axis_size("sub")
    matrices, table, links, inward = ghost_tables(side, slots, tiles_n)
    scale = 1.0 / math.sqrt(slots * tiles_n * pixels)
    width = DEPTH * side
    vmem = pl.BlockSpec(memory_space=pltpu.VMEM)
    hbm = pl.BlockSpec(memory_space=pltpu.HBM)
    dma = pltpu.SemaphoreType.DMA
    bf16, f32 = jnp.bfloat16, jnp.float32
    held = slots * 4 + tiles_n * links[0]
    held_outs = pl.pallas_call(
        functools.partial(face_kernel, (slots, tiles_n, subs, side, links, scale)),
        out_shape=(
            pltpu.VMEM(features.shape, bf16),
            pltpu.VMEM((K, chans, filters.shape[2]), f32),
        ),
        in_specs=[hbm] * 7,
        out_specs=(vmem, vmem),
        scratch_shapes=[
            pltpu.VMEM((2,) + features.shape, bf16),
            pltpu.VMEM((subs,) + features.shape, bf16),
            pltpu.VMEM((slots * 4, chans, width), bf16),
            pltpu.VMEM((slots * 4, chans, width), bf16),
            pltpu.VMEM((tiles_n - 1, links[0], chans, width), bf16),
            pltpu.VMEM((tiles_n - 1, links[0], chans, width), bf16),
            pltpu.VMEM((held, chans, width), bf16),
            pltpu.VMEM((subs, held, chans, width), bf16),
            pltpu.VMEM((2, chans, width), f32),
            pltpu.VMEM((tiles_n, 2, chans, width), f32),
            pltpu.VMEM((slots, chans, pixels), f32),
            pltpu.VMEM((slots, chans * subs, DEPTH * width), f32),
            pltpu.VMEM((2,) + matrices.shape[1:], bf16),
            pltpu.VMEM(inward.shape, bf16),
            pltpu.VMEM((pixels, 2 * width), bf16),
            pltpu.VMEM(filters.shape, bf16),
            pltpu.SMEM(tile_map.shape, jnp.int32),
            pltpu.SMEM(table.shape, jnp.int32),
            pltpu.SemaphoreType.REGULAR,
            dma((9,)),
        ]
        + [dma] * 12,
        compiler_params=pltpu.CompilerParams(
            collective_id=0, has_side_effects=True, vmem_limit_bytes=67043328 - 512 * 1024
        ),
    )(
        features,
        out_grad,
        filters,
        tile_map,
        jnp.asarray(table),
        jnp.asarray(matrices, bf16),
        jnp.asarray(inward, bf16),
    )
    held_outs = [pltpu.with_memory_space_constraint(value, pltpu.VMEM) for value in held_outs]
    return pl.pallas_call(
        store_kernel,
        out_shape=(
            jax.ShapeDtypeStruct(features.shape, bf16),
            jax.ShapeDtypeStruct((K, chans, filters.shape[2]), f32),
        ),
        in_specs=[vmem] * 2,
        out_specs=(hbm, hbm),
        scratch_shapes=[dma((2,))],
    )(*held_outs)


def on_device(features, out_grad, filters, tile_map):
    slots, chans, pixels = features.shape
    side = math.isqrt(pixels)
    whole_faces = slots * lax.axis_size("tile") == 12
    channels = chans * lax.axis_size("sub")
    if whole_faces and 1 < slots < 5 and DEPTH * side == 128 and chans % 8 == 0 and channels == 32:
        return face_path(features, out_grad, filters, tile_map)
    return general_path(features, out_grad, filters, tile_map)


def solution(mesh):
    placed = (P(("grp", "tile"), "sub", None), P(("grp", "tile"), "sub", None), P(), P())
    return jax.shard_map(
        on_device,
        mesh=mesh,
        in_specs=placed,
        out_specs=(P(("grp", "tile"), "sub", None), P("grp", "sub", None)),
        check_vma=False,
    )
```
